32 devices in a mesh: req: 16 (over z, y, core), grp: 2 (over x).
Axes of the slice: x: 2, y: 2, z: 4, core: 2. Of those that a mesh axis runs over, the one named last changes fastest.
Arguments:
- tokens: bfloat16 [8192, 1024], P('req'), may hold values from -6 to 6
- norm_attn: float32 [1024], replicated, may hold values from 0.25 to 1.75
- w_query: bfloat16 [1024, 1024], P(None, 'grp'), may hold values from -0.1875 to 0.1875
- w_key: bfloat16 [1024, 1024], P(None, 'grp'), may hold values from -0.1875 to 0.1875
- w_value: bfloat16 [1024, 1024], P(None, 'grp'), may hold values from -0.1875 to 0.1875
- w_out: bfloat16 [1024, 1024], P('grp'), may hold values from -0.1875 to 0.1875
- persist_keys: bfloat16 [16, 1024], P(None, 'grp'), may hold values from -5 to 5
- persist_values: bfloat16 [16, 1024], P(None, 'grp'), may hold values from -5 to 5
- kv_cache: bfloat16 [768, 2, 128, 1024], P('req', None, None, 'grp'), may hold values from -160 to 160
- slot_request: int32 [768], P('req'), may hold values from 0 to 255, as said below
- slot_page: int32 [768], P('req'), may hold values from 0 to 48, as said below
- cache_len: int32 [256], P('req'), may hold values from 1 to 2304
- tree_mask: int32 [256, 32, 32], P('req'), may hold values from 0 to 1, as said below
- accept_path: int32 [256, 8], P('req'), may hold values from 0 to 31, as said below
- accept_len: int32 [256], P('req'), may hold values from 1 to 8
- memory: float32 [256, 8, 128, 128], P('req', 'grp'), may hold values from -4 to 4
- momentum: float32 [256, 8, 128, 128], P('req', 'grp'), may hold values from -1.2 to 1.2
- momentum_code: int32 [256, 8, 8], P('req', None, 'grp'), may hold values from 0 to 15
- forget_code: int32 [256, 8, 8], P('req', None, 'grp'), may hold values from 0 to 15
- norm_ffn: float32 [1024], replicated, may hold values from 0.25 to 1.75
- w_gate_up: bfloat16 [2, 1024, 2816], P(None, None, 'grp'), may hold values from -0.1875 to 0.1875
- w_down: bfloat16 [2816, 1024], P('grp'), may hold values from -0.109375 to 0.109375
Outputs:
- layer_out: bfloat16 [8192, 1024], P(('req', 'grp'))
- memory_out: float32 [256, 8, 128, 128], P('req', 'grp')
- momentum_out: float32 [256, 8, 128, 128], P('req', 'grp')
The draws below stay inside these ranges and needn't reach their ends.
Inputs may be any that keep to these rules, and one draw needn't show every extreme that they name: `slot_request`: slot s lies with index s // 48 of req; slots s with (s % 48) // 3 = j hold pages of requests j * 16 to (j + 1) * 16 - 1 only. The live pages 0 .. ceil(cache_len[r] / 128) - 1 of every request stand each in exactly one slot; every other slot has page number 16 * 3. `slot_page`: see slot_request. `tree_mask`: each node's parent precedes it; node 0 is the root; rows include the node itself. `accept_path`: entry n is the node at depth n on the root path of one draft node.
All inputs are finite; a program needn't handle non-finite values.
Results may differ from the reference program's by a relative error of at most 0.015.
Values may be sent and summed in bfloat16 or wider, within the bound.
No kernel may reach another device: no remote copies, remote signals or barrier semaphores. Data moves between devices by JAX's collectives and lax.ppermute only.
A program may use at most 192 MiB of HBM per device.

```python
import math
import jax
import jax.numpy as jnp
from jax import lax

D = 1024
H = 8
HD = 128
FF = 2816
P_SIZE = 16
PAGE = 128
DRAFT = 32
ACC = 8
REQ_DEV = 16
CAP = 3
REQS = 256
SLOTS = 768
TOKENS = 8192
N_REQ = 16


def cache_layout(key):
    base = jax.random.fold_in(key, 7)
    capacity = N_REQ * CAP
    longest = (capacity - 2 * (REQ_DEV - 1)) * PAGE
    keys = jax.random.split(base, 5)
    short_len = jax.random.randint(keys[0], (N_REQ, REQ_DEV), 1, 2 * PAGE + 1).astype(jnp.int32)
    long_len = jax.random.randint(keys[1], (N_REQ,), longest - PAGE + 1, longest + 1).astype(jnp.int32)
    long_len = long_len.at[0].set(longest)
    has_long = jax.random.randint(keys[2], (N_REQ,), 0, 4) > 0
    has_long = has_long.at[0].set(True)
    first = jnp.where(has_long, long_len, short_len[:, 0])
    lengths = short_len.at[:, 0].set(first)
    pages = (lengths + PAGE - 1) // PAGE
    ends = jnp.cumsum(pages, axis=1).astype(jnp.int32)
    starts = ends - pages
    order = jnp.arange(capacity, dtype=jnp.int32)
    owner = jnp.sum((order[None, :, None] >= ends[:, None, :]).astype(jnp.int32), axis=2)
    live = owner < REQ_DEV
    dead_req = jax.random.randint(keys[3], (N_REQ, capacity), 0, REQ_DEV).astype(jnp.int32)
    req_local = jnp.where(live, owner, dead_req)
    start_sel = jnp.take_along_axis(starts, jnp.minimum(owner, REQ_DEV - 1), axis=1)
    page_index = jnp.where(live, order[None, :] - start_sel, capacity).astype(jnp.int32)
    perms = jax.vmap(lambda k: jax.random.permutation(k, capacity))(jax.random.split(keys[4], N_REQ)).astype(jnp.int32)
    rows = jnp.arange(N_REQ, dtype=jnp.int32)[:, None]
    slot_req = jnp.zeros((N_REQ, capacity), jnp.int32).at[rows, perms].set(req_local + rows * REQ_DEV)
    slot_pg = jnp.zeros((N_REQ, capacity), jnp.int32).at[rows, perms].set(page_index)
    slot_req = slot_req.reshape(N_REQ, N_REQ, CAP).transpose(1, 0, 2).reshape(-1)
    slot_pg = slot_pg.reshape(N_REQ, N_REQ, CAP).transpose(1, 0, 2).reshape(-1)
    return (slot_req, slot_pg, lengths.reshape(-1))


def draw_slot_request(key, part):
    return cache_layout(key)[0]


def draw_slot_page(key, part):
    return cache_layout(key)[1]


def draw_cache_len(key, part):
    return cache_layout(key)[2]


def tree_parents(key):
    base = jax.random.fold_in(key, 11)
    back = jax.random.randint(base, (REQS, DRAFT), 1, 5).astype(jnp.int32)
    node = jnp.arange(DRAFT, dtype=jnp.int32)
    first_row = jnp.where((node >= 1) & (node <= ACC - 2), 1, back[0])
    first_row = jnp.where(node == DRAFT - 1, DRAFT - ACC + 1, first_row).astype(jnp.int32)
    back = back.at[0].set(first_row)
    return jnp.maximum(node[None, :] - back, 0)


def draw_tree_mask(key, part):
    parent = tree_parents(key)
    node = jnp.arange(DRAFT, dtype=jnp.int32)
    current = jnp.broadcast_to(node[None, :], (REQS, DRAFT))
    mask = (current[:, :, None] == node[None, None, :]).astype(jnp.int32)

    def climb(step, state):
        here, marks = state
        here = jnp.take_along_axis(parent, here, axis=1)
        marks = jnp.maximum(marks, (here[:, :, None] == node[None, None, :]).astype(jnp.int32))
        return (here, marks)
    current, mask = lax.fori_loop(0, DRAFT, climb, (current, mask))
    return mask


def draw_accept_path(key, part):
    parent = tree_parents(key)
    here = jnp.full((REQS,), DRAFT - 1, jnp.int32)

    def climb(here, unused):
        above = jnp.take_along_axis(parent, here[:, None], axis=1)[:, 0]
        return (above, here)
    last, chain = lax.scan(climb, here, None, length=DRAFT)
    chain = jnp.transpose(chain)
    depth = jnp.sum((chain > 0).astype(jnp.int32), axis=1)
    chain = jnp.concatenate([chain, jnp.zeros((REQS, 1), jnp.int32)], axis=1)
    index = depth[:, None] - jnp.arange(ACC, dtype=jnp.int32)[None, :]
    return jnp.take_along_axis(chain, index, axis=1).astype(jnp.int32)


def draw_accept_len(key, part):
    base = jax.random.fold_in(key, 13)
    count = jax.random.randint(base, (REQS,), 1, ACC + 1).astype(jnp.int32)
    return count.at[0].set(ACC)


def draw_kv_cache(key, part):
    base = jax.random.fold_in(key, 3)
    values = jnp.clip(jax.random.normal(base, (SLOTS, 2, PAGE, H * HD), jnp.float32), -4.0, 4.0)
    return values.astype(jnp.bfloat16)


def touch_ends(entries, rng, least, high):
    longest = entries.shape.index(max(entries.shape))
    spots = []
    for shift in (0, 1):
        where = [jax.random.randint(jax.random.fold_in(rng, axis), (), 0, length) for axis, length in enumerate(entries.shape)]
        where[longest] = (where[longest] + shift) % entries.shape[longest]
        spots.append(tuple(where))
    return entries.at[spots[0]].set(least).at[spots[1]].set(high)


def block_levels(own_key, shape, shards, smallest, top_value):
    def one(axis_at, blocks):
        steps = jax.random.uniform(jax.random.fold_in(jax.random.fold_in(own_key, 6), axis_at), (blocks,), jnp.float32, smallest / len(shards), top_value / len(shards))
        return jnp.repeat(jnp.exp(steps), shape[axis_at] // blocks).reshape((-1,) + (1,) * (len(shape) - axis_at - 1))

    level = one(*shards[0])
    for cut in shards[1:]:
        level = level * one(*cut)
    return level


def bell_draw(stream_key, dims, spread, most, pieces=(), kind=jnp.bfloat16):
    factor_of = block_levels(stream_key, dims, pieces, -0.22, 0.18) if pieces else 1.0
    result = jax.random.normal(stream_key, dims, jnp.float32) * spread * factor_of
    return jnp.minimum(jnp.maximum(result, -most), most).astype(kind)


def setup_inputs(seed: int = 0) -> dict:
    arg_keys = jax.random.split(jax.random.key(seed), 23)
    tokens = bell_draw(arg_keys[0], (TOKENS, D), 1.0, 6.0, ((0, 16),))
    norm_attn = jnp.clip(1.0 + 0.15 * jax.random.normal(arg_keys[1], (D,), jnp.float32), 0.25, 1.75)
    w_query = bell_draw(arg_keys[2], (D, H * HD), D ** -0.5, 0.1875, ((1, 2),))
    w_key = bell_draw(arg_keys[3], (D, H * HD), D ** -0.5, 0.1875, ((1, 2),))
    w_value = bell_draw(arg_keys[4], (D, H * HD), D ** -0.5, 0.1875, ((1, 2),))
    w_out = bell_draw(arg_keys[5], (H * HD, D), (H * HD) ** -0.5, 0.1875, ((0, 2),))
    persist_keys = bell_draw(arg_keys[6], (P_SIZE, H * HD), 1.0, 5.0, ((1, 2),))
    persist_values = bell_draw(arg_keys[7], (P_SIZE, H * HD), 1.0, 5.0, ((1, 2),))
    kv_cache = draw_kv_cache(jax.random.fold_in(arg_keys[22], 71), 0)
    slot_request = draw_slot_request(jax.random.fold_in(arg_keys[22], 71), 0)
    slot_page = draw_slot_page(jax.random.fold_in(arg_keys[22], 71), 0)
    cache_len = draw_cache_len(jax.random.fold_in(arg_keys[22], 71), 0)
    tree_mask = draw_tree_mask(jax.random.fold_in(arg_keys[22], 71), 0)
    accept_path = draw_accept_path(jax.random.fold_in(arg_keys[22], 71), 0)
    accept_len = draw_accept_len(jax.random.fold_in(arg_keys[22], 71), 0)
    memory = bell_draw(arg_keys[15], (REQS, H, HD, HD), 1.0, 4.0, ((0, 16), (1, 2)), jnp.float32)
    momentum = bell_draw(arg_keys[16], (REQS, H, HD, HD), 0.3, 1.2, ((0, 16), (1, 2)), jnp.float32)
    momentum_code = touch_ends(jax.random.randint(arg_keys[17], (REQS, ACC, H), 0, 16), jax.random.fold_in(arg_keys[17], 1), 0, 15).astype(jnp.int32)
    forget_code = touch_ends(jax.random.randint(arg_keys[18], (REQS, ACC, H), 0, 16), jax.random.fold_in(arg_keys[18], 1), 0, 15).astype(jnp.int32)
    norm_ffn = jnp.clip(1.0 + 0.15 * jax.random.normal(arg_keys[19], (D,), jnp.float32), 0.25, 1.75)
    w_gate_up = bell_draw(arg_keys[20], (2, D, FF), D ** -0.5, 0.1875, ((2, 2),))
    w_down = bell_draw(arg_keys[21], (FF, D), FF ** -0.5, 0.109375, ((0, 2),))
    return {"tokens": tokens, "norm_attn": norm_attn, "w_query": w_query, "w_key": w_key, "w_value": w_value, "w_out": w_out, "persist_keys": persist_keys, "persist_values": persist_values, "kv_cache": kv_cache, "slot_request": slot_request, "slot_page": slot_page, "cache_len": cache_len, "tree_mask": tree_mask, "accept_path": accept_path, "accept_len": accept_len, "memory": memory, "momentum": momentum, "momentum_code": momentum_code, "forget_code": forget_code, "norm_ffn": norm_ffn, "w_gate_up": w_gate_up, "w_down": w_down}


EPS = 1e-06
THETA = 0.5
NEG = -1e+30

def rms_norm(rows, gain):
    values = rows.astype(jnp.float32)
    factor = lax.rsqrt(lax.optimization_barrier(jnp.mean(values * values, axis=-1, keepdims=True)) + EPS)
    return (values * factor * gain).astype(jnp.bfloat16)

def unit_rows(vectors):
    return vectors * lax.rsqrt(lax.optimization_barrier(jnp.sum(vectors * vectors, axis=-1, keepdims=True)) + EPS)

def reference(tokens, norm_attn, w_query, w_key, w_value, w_out, persist_keys, persist_values, kv_cache, slot_request, slot_page, cache_len, tree_mask, accept_path, accept_len, memory, momentum, momentum_code, forget_code, norm_ffn, w_gate_up, w_down):
    width = H * HD
    group_rows = REQ_DEV * DRAFT
    scale = 1.0 / math.sqrt(HD)
    normed = rms_norm(tokens, norm_attn)
    queries = jnp.dot(normed, w_query, preferred_element_type=jnp.float32).astype(jnp.bfloat16)
    keys = jnp.dot(normed, w_key, preferred_element_type=jnp.float32).astype(jnp.bfloat16)
    values = jnp.dot(normed, w_value, preferred_element_type=jnp.float32).astype(jnp.bfloat16)
    page_view = kv_cache.reshape(N_REQ, N_REQ, CAP, 2, PAGE, width)
    request_view = slot_request.reshape(N_REQ, N_REQ, CAP)
    page_index_view = slot_page.reshape(N_REQ, N_REQ, CAP)
    fixed_keys = persist_keys.astype(jnp.float32).reshape(P_SIZE, H, HD)
    fixed_values = persist_values.astype(jnp.float32).reshape(P_SIZE, H, HD)
    query_req = jnp.arange(group_rows, dtype=jnp.int32) // DRAFT
    query_node = jnp.arange(group_rows, dtype=jnp.int32) % DRAFT

    def group_attention(group):
        start = (group * group_rows).astype(jnp.int32)
        query_g = lax.dynamic_slice_in_dim(queries, start, group_rows, 0).astype(jnp.float32).reshape(group_rows, H, HD)
        key_g = lax.dynamic_slice_in_dim(keys, start, group_rows, 0).astype(jnp.float32).reshape(group_rows, H, HD)
        value_g = lax.dynamic_slice_in_dim(values, start, group_rows, 0).astype(jnp.float32).reshape(group_rows, H, HD)
        pages = lax.dynamic_index_in_dim(page_view, group, 1, keepdims=False).reshape(N_REQ * CAP, 2, PAGE, width)
        owners = lax.dynamic_index_in_dim(request_view, group, 1, keepdims=False).reshape(-1) - group * REQ_DEV
        page_numbers = lax.dynamic_index_in_dim(page_index_view, group, 1, keepdims=False).reshape(-1)
        cache_keys = pages[:, 0].astype(jnp.float32).reshape(-1, H, HD)
        cache_values = pages[:, 1].astype(jnp.float32).reshape(-1, H, HD)
        key_owner = jnp.repeat(owners, PAGE)
        key_pos = (page_numbers[:, None] * PAGE + jnp.arange(PAGE, dtype=jnp.int32)[None, :]).reshape(-1)
        lengths = lax.dynamic_slice_in_dim(cache_len, (group * REQ_DEV).astype(jnp.int32), REQ_DEV, 0)
        cache_ok = (key_owner[None, :] == query_req[:, None]) & (key_pos[None, :] < lengths[query_req][:, None])
        tree_g = lax.dynamic_slice_in_dim(tree_mask, (group * REQ_DEV).astype(jnp.int32), REQ_DEV, 0)
        tree_rows = tree_g[query_req, query_node]
        tree_ok = (query_req[:, None] == query_req[None, :]) & (jnp.take(tree_rows, query_node, axis=1) == 1)
        fixed_scores = jnp.einsum('qhd,phd->qhp', query_g, fixed_keys) * scale
        draft_scores = jnp.einsum('qhd,khd->qhk', query_g, key_g) * scale
        draft_scores = jnp.where(tree_ok[:, None, :], draft_scores, NEG)
        cache_scores = jnp.einsum('qhd,khd->qhk', query_g, cache_keys) * scale
        cache_scores = jnp.where(cache_ok[:, None, :], cache_scores, NEG)
        scores = jnp.concatenate([fixed_scores, draft_scores, cache_scores], axis=2)
        top = lax.optimization_barrier(jnp.max(scores, axis=2, keepdims=True))
        weight = jnp.exp(scores - top)
        total = lax.optimization_barrier(jnp.sum(weight, axis=2))
        rounded = weight.astype(jnp.bfloat16).astype(jnp.float32)
        all_values = jnp.concatenate([fixed_values, value_g, cache_values], axis=0)
        numer = jnp.einsum('qhk,khd->qhd', rounded, all_values)
        return (numer / total[:, :, None]).reshape(group_rows, width)
    attention = lax.map(group_attention, jnp.arange(N_REQ, dtype=jnp.int32)).reshape(REQS, DRAFT, H, HD)
    query_four = queries.astype(jnp.float32).reshape(REQS, DRAFT, H, HD)
    retrieved = jnp.einsum('rihd,rhde->rihe', unit_rows(query_four), memory, precision=lax.Precision.HIGHEST)
    mixed = (attention + retrieved).reshape(TOKENS, width).astype(jnp.bfloat16)
    residual = (tokens.astype(jnp.float32) + jnp.dot(mixed, w_out, preferred_element_type=jnp.float32)).astype(jnp.bfloat16)
    ffn_in = rms_norm(residual, norm_ffn)
    gate = jnp.dot(ffn_in, w_gate_up[0], preferred_element_type=jnp.float32)
    up = jnp.dot(ffn_in, w_gate_up[1], preferred_element_type=jnp.float32)
    hidden = (jax.nn.silu(gate) * up).astype(jnp.bfloat16)
    layer_out = (residual.astype(jnp.float32) + jnp.dot(hidden, w_down, preferred_element_type=jnp.float32)).astype(jnp.bfloat16)
    key_four = keys.reshape(REQS, DRAFT, H, HD)
    value_four = values.reshape(REQS, DRAFT, H, HD)
    rows = jnp.arange(REQS, dtype=jnp.int32)[:, None]
    path_keys = unit_rows(key_four[rows, accept_path].astype(jnp.float32))
    path_values = value_four[rows, accept_path].astype(jnp.float32)
    eta = 0.97 - 0.06 * momentum_code.astype(jnp.float32)
    forget = 0.01 + 0.02 * forget_code.astype(jnp.float32)
    for step in range(ACC):
        unit = path_keys[:, step]
        predicted = jnp.einsum('rhd,rhde->rhe', unit, memory, precision=lax.Precision.HIGHEST)
        grad = jnp.einsum('rhd,rhe->rhde', unit, predicted - path_values[:, step], precision=lax.Precision.HIGHEST)
        new_mom = eta[:, step, :, None, None] * momentum - THETA * grad
        new_mem = (1.0 - forget[:, step, :, None, None]) * memory + new_mom
        live = (step < accept_len)[:, None, None, None]
        momentum = jnp.where(live, new_mom, momentum)
        memory = jnp.where(live, new_mem, memory)
    return (layer_out, memory, momentum)
```

```python
import functools
import math

import jax
import jax.numpy as jnp
from jax import lax
from jax.experimental import pallas as pl
from jax.experimental.pallas import tpu as pltpu
from jax.sharding import PartitionSpec as P

HD = 128
LANES = 128
EXTRA = 16
PARTS = 3

EPS = 1e-06
THETA = 0.5
NEG = -1e30
TINY = 1e-30

VMEM = pltpu.VMEM
SMEM = pltpu.SMEM
F32 = jnp.float32
BF16 = jnp.bfloat16


def whole(space=VMEM):
    return pl.BlockSpec(memory_space=space)


def cost(flops, moved, special=0):
    return pl.CostEstimate(flops=flops, bytes_accessed=moved, transcendentals=special)


def params(mib=40):
    return pltpu.CompilerParams(vmem_limit_bytes=mib << 20)


def rms_norm(rows, gain):
    values = rows.astype(F32)
    factor = lax.rsqrt(jnp.mean(values * values, axis=-1, keepdims=True) + EPS)
    return (values * factor * gain).astype(BF16)


def nt_dot(left, right):
    return lax.dot_general(left, right, (((1,), (1,)), ((), ())), preferred_element_type=F32)


def column_to_row(column, count):
    row_id = lax.broadcasted_iota(jnp.int32, (count, LANES), 0)
    lane_id = lax.broadcasted_iota(jnp.int32, (count, LANES), 1)
    spread = jnp.where(row_id == lane_id, jnp.broadcast_to(column, (count, LANES)), 0.0)
    return jnp.sum(spread, axis=0, keepdims=True)


def pack_queries(codes, lengths, q_ref, out_ref, *, n, cap, reqs, draft, heads, page_len):
    block = cap * heads * draft + EXTRA
    row_id = lax.broadcasted_iota(jnp.int32, (EXTRA, LANES), 0)

    def one(d, carry):
        base = pl.multiple_of(d * block, 16)
        tail = jnp.zeros((EXTRA, LANES), F32)
        for c in range(cap):
            code = codes[d * cap + c]
            r = lax.rem(code, reqs)
            page = lax.div(code, reqs)
            live = jnp.clip(lengths[r] - page * page_len, 0, page_len)
            tail = jnp.where(row_id == c, live.astype(F32), tail)
            rows = pl.ds(pl.multiple_of(r * draft, draft), draft)
            for h in range(heads):
                out_ref[pl.ds(base + (c * heads + h) * draft, draft), :] = q_ref[
                    rows, h * HD : (h + 1) * HD
                ]
        out_ref[pl.ds(base + cap * heads * draft, EXTRA), :] = tail.astype(BF16)
        return carry

    lax.fori_loop(0, n, one, 0)


def page_attention(q_ref, kv_ref, out_ref, *, cap, draft, heads, page_len, scale):
    span = heads * draft
    tail_at = cap * span
    limits = q_ref[tail_at : tail_at + EXTRA, :].astype(F32)
    lane = lax.broadcasted_iota(jnp.int32, (draft, page_len), 1).astype(F32)
    row_id = lax.broadcasted_iota(jnp.int32, (EXTRA, LANES), 0)
    tail = jnp.zeros((EXTRA, LANES), F32)
    for c in range(cap):
        valid = lane < limits[c : c + 1, :]
        columns = []
        for h in range(heads):
            at = c * span + h * draft
            cols = slice(h * HD, (h + 1) * HD)
            scores = nt_dot(q_ref[at : at + draft, :], kv_ref[c, 0, :, cols]) * scale
            scores = jnp.where(valid, scores, NEG)
            top = jnp.max(scores, axis=1, keepdims=True)
            weight = jnp.where(valid, jnp.exp(scores - top), 0.0)
            total = jnp.sum(weight, axis=1, keepdims=True)
            numer = jnp.dot(weight.astype(BF16), kv_ref[c, 1, :, cols], preferred_element_type=F32)
            kept = jnp.maximum(total, TINY)
            out_ref[at : at + draft, :] = (numer / kept).astype(BF16)
            columns.append(jnp.where(total > 0.0, top + jnp.log(kept), NEG))
        row = column_to_row(jnp.concatenate(columns, axis=0), span)
        for p in range(PARTS):
            part = row.astype(BF16).astype(F32)
            tail = jnp.where(row_id == p * cap + c, part, tail)
            row = row - part
    out_ref[tail_at : tail_at + EXTRA, :] = tail.astype(BF16)


def local_attention(
    q_ref, k_ref, v_ref, pk_ref, pv_ref, mask_ref, mem_ref, o_ref, ret_ref, lse_ref,
    *, heads, draft, scale,
):
    r = pl.program_id(0)
    seen = mask_ref[0] == 1
    columns = []
    for h in range(heads):
        cols = slice(h * HD, (h + 1) * HD)
        rows = slice(h * draft, (h + 1) * draft)
        query = q_ref[:, cols]
        tree = jnp.where(seen, nt_dot(query, k_ref[:, cols]) * scale, NEG)
        fixed = nt_dot(query, pk_ref[:, cols]) * scale
        top = jnp.maximum(
            jnp.max(tree, axis=1, keepdims=True), jnp.max(fixed, axis=1, keepdims=True)
        )
        tree_w = jnp.exp(tree - top)
        fixed_w = jnp.exp(fixed - top)
        total = jnp.sum(tree_w, axis=1, keepdims=True) + jnp.sum(fixed_w, axis=1, keepdims=True)
        numer = jnp.dot(tree_w.astype(BF16), v_ref[:, cols], preferred_element_type=F32)
        numer = numer + jnp.dot(fixed_w.astype(BF16), pv_ref[:, cols], preferred_element_type=F32)
        o_ref[rows, :] = numer / total
        columns.append(top + jnp.log(total))
        wide = query.astype(F32)
        unit = wide * lax.rsqrt(jnp.sum(wide * wide, axis=1, keepdims=True) + EPS)
        ret_ref[rows, :] = jnp.dot(
            unit, mem_ref[0, h], preferred_element_type=F32, precision=lax.Precision.HIGHEST
        )
    lse_ref[pl.ds(r, 1), :] = column_to_row(jnp.concatenate(columns, axis=0), heads * draft)


def update_memory(
    path, count, mom_code, forget_code, k_ref, v_ref, mem_ref, mom_ref, mem_out, mom_out,
    wide_k, wide_v, unit_ref, value_ref, turned_ref, *, heads, steps,
):
    r = pl.program_id(0)
    wide_k[...] = k_ref[...].astype(F32)
    wide_v[...] = v_ref[...].astype(F32)
    unit_ref[...] = jnp.zeros_like(unit_ref)
    for n in range(steps):
        node = path[r * steps + n]
        k_row = wide_k[pl.ds(node, 1), :]
        v_row = wide_v[pl.ds(node, 1), :]
        for h in range(heads):
            unit_ref[h * steps + n : h * steps + n + 1, :] = k_row[:, h * HD : (h + 1) * HD]
            value_ref[h * steps + n : h * steps + n + 1, :] = v_row[:, h * HD : (h + 1) * HD]
    keys = unit_ref[...]
    unit = keys * lax.rsqrt(jnp.sum(keys * keys, axis=1, keepdims=True) + EPS)
    turned_ref[...] = jnp.transpose(unit)

    def advance(n, mem_src, mom_src):
        for h in range(heads):
            at = (r * steps + n) * heads + h
            eta = 0.97 - 0.06 * mom_code[at].astype(F32)
            keep = 1.0 - (0.01 + 0.02 * forget_code[at].astype(F32))
            row = h * steps + n
            column = turned_ref[:, row : row + 1]
            matrix = mem_src[0, h]
            predicted = jnp.sum(column * matrix, axis=0, keepdims=True)
            error = THETA * (predicted - value_ref[row : row + 1, :])
            moved = eta * mom_src[0, h] - column * error
            mom_out[0, h] = moved
            mem_out[0, h] = keep * matrix + moved

    advance(0, mem_ref, mom_ref)
    for n in range(1, steps):
        pl.when(n < count[r])(functools.partial(advance, n, mem_out, mom_out))


def combine(
    codes, msg_ref, o_ref, ret_ref, lse_ref, w_ref, out_ref,
    part_lse, best, total, weight, own_weight, acc, mixed,
    *, n, cap, reqs, draft, heads,
):
    span = heads * draft
    block = cap * span + EXTRA
    slots = n * cap
    for d in range(n):
        at = d * block + cap * span
        tail = msg_ref[at : at + EXTRA, :].astype(F32)
        part_lse[d * cap : (d + 1) * cap, :] = (
            tail[0:cap] + tail[cap : 2 * cap] + tail[2 * cap : 3 * cap]
        )
    best[...] = lse_ref[...]
    owners = [lax.rem(codes[s], reqs) for s in range(slots)]
    for s in range(slots):
        r = owners[s]
        best[pl.ds(r, 1), :] = jnp.maximum(best[pl.ds(r, 1), :], part_lse[s : s + 1, :])
    own_weight[...] = jnp.zeros_like(own_weight)
    weight[...] = jnp.zeros_like(weight)
    start = jnp.exp(lse_ref[...] - best[...])
    total[...] = start
    for s in range(slots):
        r = owners[s]
        term = jnp.exp(part_lse[s : s + 1, :] - best[pl.ds(r, 1), :])
        weight[s : s + 1, :] = term
        total[pl.ds(r, 1), :] = total[pl.ds(r, 1), :] + term
    inverse = 1.0 / total[...]
    own_weight[0:reqs, :] = start * inverse
    total[...] = inverse
    for s in range(slots):
        weight[s : s + 1, :] = weight[s : s + 1, :] * total[pl.ds(owners[s], 1), :]
    turned = jnp.transpose(weight[...])
    own_turned = jnp.transpose(own_weight[...])
    for r in range(reqs):
        rows = slice(r * span, (r + 1) * span)
        acc[rows, :] = o_ref[rows, :] * own_turned[0:span, r : r + 1] + ret_ref[rows, :]
    for s in range(slots):
        at = (s // cap) * block + (s % cap) * span
        rows = pl.ds(pl.multiple_of(owners[s] * span, span), span)
        acc[rows, :] = acc[rows, :] + msg_ref[at : at + span, :].astype(F32) * turned[
            0:span, s : s + 1
        ]
    for r in range(reqs):
        for h in range(heads):
            at = r * span + h * draft
            mixed[r * draft : (r + 1) * draft, h * HD : (h + 1) * HD] = acc[
                at : at + draft, :
            ].astype(BF16)
    out_ref[...] = jnp.dot(mixed[...], w_ref[...], preferred_element_type=F32).astype(BF16)


def on_device(
    tokens,
    norm_attn,
    w_query,
    w_key,
    w_value,
    w_out,
    persist_keys,
    persist_values,
    kv_cache,
    slot_request,
    slot_page,
    cache_len,
    tree_mask,
    accept_path,
    accept_len,
    memory,
    momentum,
    momentum_code,
    forget_code,
    norm_ffn,
    w_gate_up,
    w_down,
):
    n = lax.axis_size("req")
    group_rows, model = tokens.shape
    reqs = cache_len.shape[0]
    draft = tree_mask.shape[1]
    steps = accept_path.shape[1]
    width = w_query.shape[1]
    heads = width // HD
    span = heads * draft
    slots = kv_cache.shape[0]
    cap = slots // n
    fixed_count = persist_keys.shape[0]
    page_len = kv_cache.shape[2]
    block = cap * span + EXTRA
    scale = 1.0 / math.sqrt(HD)

    label = slot_page * reqs + lax.rem(slot_request, reqs)
    codes = lax.all_to_all(label, "req", split_axis=0, concat_axis=0, tiled=True)

    normed = rms_norm(tokens, norm_attn)
    queries = jnp.dot(normed, w_query, preferred_element_type=F32).astype(BF16)

    packed = pl.pallas_call(
        functools.partial(
            pack_queries, n=n, cap=cap, reqs=reqs, draft=draft, heads=heads, page_len=page_len
        ),
        out_shape=jax.ShapeDtypeStruct((n * block, LANES), BF16),
        in_specs=[whole(SMEM), whole(SMEM), whole()],
        out_specs=whole(),
        compiler_params=params(),
        cost_estimate=cost(0, 4 * n * block * LANES),
        name="pack_queries",
    )(codes, cache_len, queries)
    asked = lax.all_to_all(packed, "req", split_axis=0, concat_axis=0, tiled=True)

    keys = jnp.dot(normed, w_key, preferred_element_type=F32).astype(BF16)
    values = jnp.dot(normed, w_value, preferred_element_type=F32).astype(BF16)

    row_block = pl.BlockSpec((draft, width), lambda r, *_: (r, 0))
    fixed_block = pl.BlockSpec((fixed_count, width), lambda r, *_: (0, 0))
    matrix_block = pl.BlockSpec((1, heads, HD, HD), lambda r, *_: (r, 0, 0, 0))
    span_block = pl.BlockSpec((span, HD), lambda r, *_: (r, 0))
    own, retrieved, own_lse = pl.pallas_call(
        functools.partial(local_attention, heads=heads, draft=draft, scale=scale),
        grid=(reqs,),
        out_shape=(
            jax.ShapeDtypeStruct((reqs * span, HD), F32),
            jax.ShapeDtypeStruct((reqs * span, HD), F32),
            jax.ShapeDtypeStruct((reqs, LANES), F32),
        ),
        in_specs=[
            row_block,
            row_block,
            row_block,
            fixed_block,
            fixed_block,
            pl.BlockSpec((1, draft, draft), lambda r: (r, 0, 0)),
            matrix_block,
        ],
        out_specs=(span_block, span_block, pl.BlockSpec((reqs, LANES), lambda r: (0, 0))),
        compiler_params=params(),
        cost_estimate=cost(
            2 * reqs * span * HD * (2 * (draft + fixed_count) + 6 * HD),
            4 * reqs * (heads * HD * HD + 2 * span * HD),
            reqs * span * (draft + fixed_count),
        ),
        name="local_attention",
    )(queries, keys, values, persist_keys, persist_values, tree_mask, memory)

    matrices = jax.ShapeDtypeStruct(memory.shape, F32)
    memory_out, momentum_out = pl.pallas_call(
        functools.partial(update_memory, heads=heads, steps=steps),
        grid_spec=pltpu.PrefetchScalarGridSpec(
            num_scalar_prefetch=4,
            grid=(reqs,),
            in_specs=[row_block, row_block, matrix_block, matrix_block],
            out_specs=(matrix_block, matrix_block),
            scratch_shapes=[
                pltpu.VMEM((draft, width), F32),
                pltpu.VMEM((draft, width), F32),
                pltpu.VMEM((LANES, HD), F32),
                pltpu.VMEM((heads * steps, HD), F32),
                pltpu.VMEM((HD, LANES), F32),
            ],
        ),
        out_shape=(matrices, matrices),
        compiler_params=params(),
        cost_estimate=cost(
            14 * reqs * heads * HD * HD * steps * 8, 16 * reqs * heads * HD * HD
        ),
        name="update_memory",
    )(
        accept_path.reshape(-1),
        accept_len,
        momentum_code.reshape(-1),
        forget_code.reshape(-1),
        keys,
        values,
        memory,
        momentum,
    )

    message_block = pl.BlockSpec((block, LANES), lambda d: (d, 0))
    answers = pl.pallas_call(
        functools.partial(
            page_attention, cap=cap, draft=draft, heads=heads, page_len=page_len, scale=scale
        ),
        grid=(n,),
        out_shape=jax.ShapeDtypeStruct((n * block, LANES), BF16),
        in_specs=[
            message_block,
            pl.BlockSpec((cap, 2, page_len, width), lambda d: (d, 0, 0, 0)),
        ],
        out_specs=message_block,
        compiler_params=params(),
        cost_estimate=cost(
            4 * slots * span * page_len * HD,
            4 * slots * page_len * width + 4 * n * block * LANES,
            slots * span * page_len,
        ),
        name="page_attention",
    )(asked, kv_cache)
    returned = lax.all_to_all(answers, "req", split_axis=0, concat_axis=0, tiled=True)

    partial_out = pl.pallas_call(
        functools.partial(combine, n=n, cap=cap, reqs=reqs, draft=draft, heads=heads),
        out_shape=jax.ShapeDtypeStruct((group_rows, model), BF16),
        in_specs=[whole(SMEM)] + [whole()] * 5,
        out_specs=whole(),
        scratch_shapes=[
            pltpu.VMEM((slots, LANES), F32),
            pltpu.VMEM((reqs, LANES), F32),
            pltpu.VMEM((reqs, LANES), F32),
            pltpu.VMEM((LANES, LANES), F32),
            pltpu.VMEM((LANES, LANES), F32),
            pltpu.VMEM((reqs * span, HD), F32),
            pltpu.VMEM((group_rows, width), BF16),
        ],
        compiler_params=params(),
        cost_estimate=cost(
            2 * group_rows * width * model, 2 * n * block * LANES + 8 * reqs * span * HD
        ),
        name="combine",
    )(codes, returned, own, retrieved, own_lse, w_out)

    rows = group_rows // lax.axis_size("grp")
    head_sum = lax.psum_scatter(partial_out, "grp", scatter_dimension=0, tiled=True).astype(F32)
    own_rows = lax.dynamic_slice_in_dim(tokens, lax.axis_index("grp") * rows, rows, 0)
    residual = (own_rows.astype(F32) + head_sum).astype(BF16)
    ffn_in = rms_norm(residual, norm_ffn)
    piece = lax.all_gather(ffn_in, "grp", axis=0, tiled=True)
    gate = jnp.dot(piece, w_gate_up[0], preferred_element_type=F32)
    up = jnp.dot(piece, w_gate_up[1], preferred_element_type=F32)
    hidden = (jax.nn.silu(gate) * up).astype(BF16)
    ffn_out = lax.psum_scatter(
        jnp.dot(hidden, w_down, preferred_element_type=F32).astype(BF16),
        "grp",
        scatter_dimension=0,
        tiled=True,
    ).astype(F32)
    layer_out = (residual.astype(F32) + ffn_out).astype(BF16)
    return (layer_out, memory_out, momentum_out)


def solution(mesh):
    return jax.shard_map(
        on_device,
        mesh=mesh,
        in_specs=(
            P("req", None),
            P(),
            P(None, "grp"),
            P(None, "grp"),
            P(None, "grp"),
            P("grp", None),
            P(None, "grp"),
            P(None, "grp"),
            P("req", None, None, "grp"),
            P("req"),
            P("req"),
            P("req"),
            P("req", None, None),
            P("req", None),
            P("req"),
            P("req", "grp", None, None),
            P("req", "grp", None, None),
            P("req", None, "grp"),
            P("req", None, "grp"),
            P(),
            P(None, None, "grp"),
            P("grp", None),
        ),
        out_specs=(
            P(("req", "grp"), None),
            P("req", "grp", None, None),
            P("req", "grp", None, None),
        ),
        check_vma=False,
    )
```

```python
import functools
import math

import jax
import jax.numpy as jnp
from jax import lax
from jax.experimental import pallas as pl
from jax.experimental.pallas import tpu as pltpu
from jax.sharding import PartitionSpec as P

HD = 128
LANES = 128
EXTRA = 16
TOP_PARTS = 3
SUM_PARTS = 2

EPS = 1e-06
THETA = 0.5
NEG = -1e30

VMEM = pltpu.VMEM
SMEM = pltpu.SMEM
F32 = jnp.float32
BF16 = jnp.bfloat16


def whole(space=VMEM):
    return pl.BlockSpec(memory_space=space)


def cost(flops, moved, special=0):
    return pl.CostEstimate(flops=flops, bytes_accessed=moved, transcendentals=special)


def params(mib=40):
    return pltpu.CompilerParams(vmem_limit_bytes=mib << 20)


def rms_norm(rows, gain):
    values = rows.astype(F32)
    factor = lax.rsqrt(jnp.mean(values * values, axis=-1, keepdims=True) + EPS)
    return (values * factor * gain).astype(BF16)


def nt_dot(left, right):
    return lax.dot_general(left, right, (((1,), (1,)), ((), ())), preferred_element_type=F32)


def column_to_row(column, count):
    row_id = lax.broadcasted_iota(jnp.int32, (count, LANES), 0)
    lane_id = lax.broadcasted_iota(jnp.int32, (count, LANES), 1)
    spread = jnp.where(row_id == lane_id, jnp.broadcast_to(column, (count, LANES)), 0.0)
    return jnp.sum(spread, axis=0, keepdims=True)


def split_parts(row, count):
    parts = []
    for _ in range(count):
        part = row.astype(BF16).astype(F32)
        parts.append(part)
        row = row - part
    return parts


def project_queries(tok_ref, gain_ref, w_ref, normed_ref, q_ref, turned_ref, *, reqs, draft, heads):
    normed_ref[...] = rms_norm(tok_ref[...], gain_ref[...])
    q_ref[...] = jnp.dot(normed_ref[...], w_ref[...], preferred_element_type=F32).astype(BF16)
    span = heads * draft
    for r in range(reqs):
        rows = slice(r * draft, (r + 1) * draft)
        pieces = [q_ref[rows, h * HD : (h + 1) * HD].astype(F32) for h in range(heads)]
        if span < LANES:
            pieces.append(jnp.zeros((LANES - span, HD), F32))
        tile = jnp.concatenate(pieces, axis=0)
        turned_ref[r * HD : (r + 1) * HD, :] = jnp.transpose(tile).astype(BF16)


def pack_queries(codes, lengths, turned_ref, out_ref, *, n, cap, reqs, page_len):
    block = cap * HD + EXTRA
    row_id = lax.broadcasted_iota(jnp.int32, (EXTRA, LANES), 0)

    def one(d, carry):
        base = pl.multiple_of(d * block, EXTRA)
        tail = jnp.zeros((EXTRA, LANES), F32)
        for c in range(cap):
            code = codes[d * cap + c]
            r = lax.rem(code, reqs)
            page = lax.div(code, reqs)
            live = jnp.clip(lengths[r] - page * page_len, 0, page_len)
            tail = jnp.where(row_id == c, live.astype(F32), tail)
            rows = pl.ds(pl.multiple_of(r * HD, HD), HD)
            out_ref[pl.ds(base + c * HD, HD), :] = turned_ref[rows, :]
        out_ref[pl.ds(base + cap * HD, EXTRA), :] = tail.astype(BF16)
        return carry

    lax.fori_loop(0, n, one, 0)


def page_attention(q_ref, kv_ref, out_ref, *, cap, draft, heads, page_len, scale):
    span = heads * draft
    limits = q_ref[cap * HD : cap * HD + EXTRA, :].astype(F32)
    token = lax.broadcasted_iota(jnp.int32, (page_len, LANES), 0).astype(F32)
    row_id = lax.broadcasted_iota(jnp.int32, (EXTRA, LANES), 0)
    head_of = lax.broadcasted_iota(jnp.int32, (HD, LANES), 1) // draft
    tail = jnp.zeros((EXTRA, LANES), F32)
    all_scores = []
    for c in range(cap):
        turned = q_ref[c * HD : (c + 1) * HD, :]
        blocks = [jnp.where(head_of == h, turned, jnp.zeros_like(turned)) for h in range(heads)]
        all_scores.append(
            jnp.dot(kv_ref[c, 0], jnp.concatenate(blocks, axis=0), preferred_element_type=F32)
        )
    all_weights = []
    for c in range(cap):
        scores = jnp.where(token < limits[c : c + 1, :], all_scores[c] * scale, NEG)
        top = jnp.max(scores, axis=0, keepdims=True)
        weight = jnp.exp(scores - top)
        total = jnp.sum(weight, axis=0, keepdims=True)
        all_weights.append(jnp.transpose(weight).astype(BF16))
        parts = split_parts(top, TOP_PARTS) + split_parts(total, SUM_PARTS)
        for p, part in enumerate(parts):
            tail = jnp.where(row_id == p * cap + c, part, tail)
    for c in range(cap):
        for h in range(heads):
            rows = slice(h * draft, (h + 1) * draft)
            numer = jnp.dot(
                all_weights[c][rows, :],
                kv_ref[c, 1, :, h * HD : (h + 1) * HD],
                preferred_element_type=F32,
            )
            out_ref[c * span + h * draft : c * span + (h + 1) * draft, :] = numer.astype(BF16)
    out_ref[cap * span : cap * span + EXTRA, :] = tail.astype(BF16)


def local_attention(
    q_ref, k_ref, v_ref, pk_ref, pv_ref, mask_ref, mem_ref,
    o_ref, ret_ref, top_ref, sum_ref, *, heads, draft, scale,
):
    r = pl.program_id(0)
    seen = mask_ref[0] == 1
    tops, totals = [], []
    for h in range(heads):
        cols = slice(h * HD, (h + 1) * HD)
        rows = slice(h * draft, (h + 1) * draft)
        query = q_ref[:, cols]
        tree = jnp.where(seen, nt_dot(query, k_ref[:, cols]) * scale, NEG)
        fixed = nt_dot(query, pk_ref[:, cols]) * scale
        top = jnp.maximum(
            jnp.max(tree, axis=1, keepdims=True), jnp.max(fixed, axis=1, keepdims=True)
        )
        tree_w = jnp.exp(tree - top)
        fixed_w = jnp.exp(fixed - top)
        total = jnp.sum(tree_w, axis=1, keepdims=True) + jnp.sum(fixed_w, axis=1, keepdims=True)
        numer = jnp.dot(tree_w.astype(BF16), v_ref[:, cols], preferred_element_type=F32)
        numer = numer + jnp.dot(fixed_w.astype(BF16), pv_ref[:, cols], preferred_element_type=F32)
        o_ref[rows, :] = numer
        tops.append(top)
        totals.append(total)
        wide = query.astype(F32)
        unit = wide * lax.rsqrt(jnp.sum(wide * wide, axis=1, keepdims=True) + EPS)
        ret_ref[rows, :] = jnp.dot(
            unit, mem_ref[0, h], preferred_element_type=F32, precision=lax.Precision.HIGHEST
        )
    span = heads * draft
    top_ref[pl.ds(r, 1), :] = column_to_row(jnp.concatenate(tops, axis=0), span)
    sum_ref[pl.ds(r, 1), :] = column_to_row(jnp.concatenate(totals, axis=0), span)


def update_memory(
    path, count, mom_code, forget_code, k_ref, v_ref, mem_ref, mom_ref, mem_out, mom_out,
    wide_k, wide_v, unit_ref, value_ref, turned_ref, *, heads, steps,
):
    r = pl.program_id(0)
    wide_k[...] = k_ref[...].astype(F32)
    wide_v[...] = v_ref[...].astype(F32)
    unit_ref[...] = jnp.zeros_like(unit_ref)
    for n in range(steps):
        node = path[r * steps + n]
        k_row = wide_k[pl.ds(node, 1), :]
        v_row = wide_v[pl.ds(node, 1), :]
        for h in range(heads):
            unit_ref[h * steps + n : h * steps + n + 1, :] = k_row[:, h * HD : (h + 1) * HD]
            value_ref[h * steps + n : h * steps + n + 1, :] = v_row[:, h * HD : (h + 1) * HD]
    keys = unit_ref[...]
    unit = keys * lax.rsqrt(jnp.sum(keys * keys, axis=1, keepdims=True) + EPS)
    turned_ref[...] = jnp.transpose(unit)

    def advance(n, mem_src, mom_src):
        for h in range(heads):
            at = (r * steps + n) * heads + h
            eta = 0.97 - 0.06 * mom_code[at].astype(F32)
            keep = 1.0 - (0.01 + 0.02 * forget_code[at].astype(F32))
            row = h * steps + n
            column = turned_ref[:, row : row + 1]
            matrix = mem_src[0, h]
            predicted = jnp.sum(column * matrix, axis=0, keepdims=True)
            error = THETA * (predicted - value_ref[row : row + 1, :])
            moved = eta * mom_src[0, h] - column * error
            mom_out[0, h] = moved
            mem_out[0, h] = keep * matrix + moved

    advance(0, mem_ref, mom_ref)
    for n in range(1, steps):
        pl.when(n < count[r])(functools.partial(advance, n, mem_out, mom_out))


def combine(
    codes, side, msg_ref, o_ref, ret_ref, own_top_ref, own_sum_ref, w_ref, *rest,
    n, cap, reqs, draft, heads, pieces,
):
    outs = rest[:pieces]
    part_top, part_sum, best, total, weight, own_weight, acc, mixed = rest[pieces:]
    span = heads * draft
    block = cap * span + EXTRA
    slots = n * cap
    for d in range(n):
        at = d * block + cap * span
        tail = msg_ref[at : at + EXTRA, :].astype(F32)
        rows = [tail[p * cap : (p + 1) * cap] for p in range(TOP_PARTS + SUM_PARTS)]
        part_top[d * cap : (d + 1) * cap, :] = rows[0] + rows[1] + rows[2]
        part_sum[d * cap : (d + 1) * cap, :] = rows[3] + rows[4]
    best[...] = own_top_ref[...]
    owners = [lax.rem(codes[s], reqs) for s in range(slots)]
    for s in range(slots):
        r = owners[s]
        best[pl.ds(r, 1), :] = jnp.maximum(best[pl.ds(r, 1), :], part_top[s : s + 1, :])
    own_weight[...] = jnp.zeros_like(own_weight)
    weight[...] = jnp.zeros_like(weight)
    start = jnp.exp(own_top_ref[...] - best[...])
    total[...] = start * own_sum_ref[...]
    for s in range(slots):
        r = owners[s]
        term = jnp.exp(part_top[s : s + 1, :] - best[pl.ds(r, 1), :])
        weight[s : s + 1, :] = term
        total[pl.ds(r, 1), :] = total[pl.ds(r, 1), :] + term * part_sum[s : s + 1, :]
    inverse = 1.0 / total[...]
    own_weight[0:reqs, :] = start * inverse
    total[...] = inverse
    for s in range(slots):
        weight[s : s + 1, :] = weight[s : s + 1, :] * total[pl.ds(owners[s], 1), :]
    turned = jnp.transpose(weight[...])
    own_turned = jnp.transpose(own_weight[...])
    for r in range(reqs):
        rows = slice(r * span, (r + 1) * span)
        acc[rows, :] = o_ref[rows, :] * own_turned[0:span, r : r + 1] + ret_ref[rows, :]
    for s in range(slots):
        at = (s // cap) * block + (s % cap) * span
        rows = pl.ds(pl.multiple_of(owners[s] * span, span), span)
        acc[rows, :] = acc[rows, :] + msg_ref[at : at + span, :].astype(F32) * turned[
            0:span, s : s + 1
        ]
    for r in range(reqs):
        for h in range(heads):
            at = r * span + h * draft
            mixed[r * draft : (r + 1) * draft, h * HD : (h + 1) * HD] = acc[
                at : at + draft, :
            ].astype(BF16)
    rows = reqs * draft // pieces
    for p, out_ref in enumerate(outs):
        first = lax.rem(side[0] + p, pieces) * rows
        out_ref[...] = jnp.dot(
            mixed[pl.ds(pl.multiple_of(first, rows), rows), :],
            w_ref[...],
            preferred_element_type=F32,
        ).astype(BF16)


def feed_forward(
    side, tok_ref, mine_ref, theirs_ref, gain_ref, up_ref, down_ref, out_ref, hidden, *, own
):
    rows = mine_ref.shape[0]
    units = down_ref.shape[0]
    at = side[0] if own else 1 - side[0]
    tokens = tok_ref[pl.ds(pl.multiple_of(at * rows, rows), rows), :].astype(F32)
    summed = tokens + mine_ref[...].astype(F32) + theirs_ref[...].astype(F32)
    residual = summed.astype(BF16)
    ffn_in = rms_norm(residual, gain_ref[...])
    step = 256
    for first in range(0, units, step):
        cols = slice(first, min(first + step, units))
        gate = jnp.dot(ffn_in, up_ref[0, :, cols], preferred_element_type=F32)
        up = jnp.dot(ffn_in, up_ref[1, :, cols], preferred_element_type=F32)
        hidden[:, cols] = (gate / (1.0 + jnp.exp(-gate)) * up).astype(BF16)
    for first in range(0, out_ref.shape[1], step):
        cols = slice(first, first + step)
        part = jnp.dot(hidden[...], down_ref[:, cols], preferred_element_type=F32)
        if own:
            part = part + residual[:, cols].astype(F32)
        out_ref[:, cols] = part.astype(out_ref.dtype)


def on_device(
    tokens,
    norm_attn,
    w_query,
    w_key,
    w_value,
    w_out,
    persist_keys,
    persist_values,
    kv_cache,
    slot_request,
    slot_page,
    cache_len,
    tree_mask,
    accept_path,
    accept_len,
    memory,
    momentum,
    momentum_code,
    forget_code,
    norm_ffn,
    w_gate_up,
    w_down,
):
    n = lax.axis_size("req")
    group_rows, model = tokens.shape
    reqs = cache_len.shape[0]
    draft = tree_mask.shape[1]
    steps = accept_path.shape[1]
    width = w_query.shape[1]
    heads = width // HD
    span = heads * draft
    slots = kv_cache.shape[0]
    cap = slots // n
    fixed_count = persist_keys.shape[0]
    page_len = kv_cache.shape[2]
    ask_block = cap * HD + EXTRA
    block = cap * span + EXTRA
    scale = 1.0 / math.sqrt(HD)

    label = slot_page * reqs + lax.rem(slot_request, reqs)
    codes = lax.all_to_all(label, "req", split_axis=0, concat_axis=0, tiled=True)

    normed, queries, turned = pl.pallas_call(
        functools.partial(project_queries, reqs=reqs, draft=draft, heads=heads),
        out_shape=(
            jax.ShapeDtypeStruct((group_rows, model), BF16),
            jax.ShapeDtypeStruct((group_rows, width), BF16),
            jax.ShapeDtypeStruct((reqs * HD, LANES), BF16),
        ),
        in_specs=[whole()] * 3,
        out_specs=(whole(),) * 3,
        compiler_params=params(12),
        cost_estimate=cost(
            2 * group_rows * model * width, 2 * model * (2 * group_rows + width)
        ),
        name="project_queries",
    )(tokens, norm_attn.reshape(1, -1), w_query)

    packed = pl.pallas_call(
        functools.partial(pack_queries, n=n, cap=cap, reqs=reqs, page_len=page_len),
        out_shape=jax.ShapeDtypeStruct((n * ask_block, LANES), BF16),
        in_specs=[whole(SMEM), whole(SMEM), whole()],
        out_specs=whole(),
        compiler_params=params(8),
        cost_estimate=cost(0, 4 * n * ask_block * LANES),
        name="pack_queries",
    )(codes, cache_len, turned)
    asked = lax.all_to_all(packed, "req", split_axis=0, concat_axis=0, tiled=True)

    keys = jnp.dot(normed, w_key, preferred_element_type=F32).astype(BF16)
    values = jnp.dot(normed, w_value, preferred_element_type=F32).astype(BF16)

    row_block = pl.BlockSpec((draft, width), lambda r, *_: (r, 0))
    fixed_block = pl.BlockSpec((fixed_count, width), lambda r, *_: (0, 0))
    matrix_block = pl.BlockSpec((1, heads, HD, HD), lambda r, *_: (r, 0, 0, 0))
    span_block = pl.BlockSpec((span, HD), lambda r, *_: (r, 0))
    own, retrieved, own_top, own_sum = pl.pallas_call(
        functools.partial(local_attention, heads=heads, draft=draft, scale=scale),
        grid=(reqs,),
        out_shape=(
            jax.ShapeDtypeStruct((reqs * span, HD), F32),
            jax.ShapeDtypeStruct((reqs * span, HD), F32),
            jax.ShapeDtypeStruct((reqs, LANES), F32),
            jax.ShapeDtypeStruct((reqs, LANES), F32),
        ),
        in_specs=[
            row_block,
            row_block,
            row_block,
            fixed_block,
            fixed_block,
            pl.BlockSpec((1, draft, draft), lambda r: (r, 0, 0)),
            matrix_block,
        ],
        out_specs=(span_block, span_block) + (pl.BlockSpec((reqs, LANES), lambda r: (0, 0)),) * 2,
        compiler_params=params(10),
        cost_estimate=cost(
            2 * reqs * span * HD * (2 * (draft + fixed_count) + 6 * HD),
            4 * reqs * (heads * HD * HD + 2 * span * HD),
            reqs * span * (draft + fixed_count),
        ),
        name="local_attention",
    )(queries, keys, values, persist_keys, persist_values, tree_mask, memory)

    matrices = jax.ShapeDtypeStruct(memory.shape, F32)
    memory_out, momentum_out = pl.pallas_call(
        functools.partial(update_memory, heads=heads, steps=steps),
        grid_spec=pltpu.PrefetchScalarGridSpec(
            num_scalar_prefetch=4,
            grid=(reqs,),
            in_specs=[row_block, row_block, matrix_block, matrix_block],
            out_specs=(matrix_block, matrix_block),
            scratch_shapes=[
                pltpu.VMEM((draft, width), F32),
                pltpu.VMEM((draft, width), F32),
                pltpu.VMEM((LANES, HD), F32),
                pltpu.VMEM((heads * steps, HD), F32),
                pltpu.VMEM((HD, LANES), F32),
            ],
        ),
        out_shape=(matrices, matrices),
        compiler_params=params(10),
        cost_estimate=cost(
            14 * reqs * heads * HD * HD * steps * 8, 16 * reqs * heads * HD * HD
        ),
        name="update_memory",
    )(
        accept_path.reshape(-1),
        accept_len,
        momentum_code.reshape(-1),
        forget_code.reshape(-1),
        keys,
        values,
        memory,
        momentum,
    )

    asked, memory_out, momentum_out, keys, values = lax.optimization_barrier(
        (asked, memory_out, momentum_out, keys, values)
    )
    answers = pl.pallas_call(
        functools.partial(
            page_attention, cap=cap, draft=draft, heads=heads, page_len=page_len, scale=scale
        ),
        grid=(n,),
        out_shape=jax.ShapeDtypeStruct((n * block, LANES), BF16),
        in_specs=[
            pl.BlockSpec((ask_block, LANES), lambda d: (d, 0)),
            pl.BlockSpec((cap, 2, page_len, width), lambda d: (d, 0, 0, 0)),
        ],
        out_specs=pl.BlockSpec((block, LANES), lambda d: (d, 0)),
        compiler_params=params(12),
        cost_estimate=cost(
            4 * slots * span * page_len * HD,
            4 * slots * page_len * width + 4 * n * block * LANES,
            slots * span * page_len,
        ),
        name="page_attention",
    )(asked, kv_cache)
    returned = lax.all_to_all(answers, "req", split_axis=0, concat_axis=0, tiled=True)

    side = lax.axis_index("grp").astype(jnp.int32).reshape(1)
    grp = lax.axis_size("grp")
    pieces = 2 if grp == 2 and w_down.shape[0] % LANES == 0 else 1
    rows = group_rows // grp
    partials = pl.pallas_call(
        functools.partial(
            combine, n=n, cap=cap, reqs=reqs, draft=draft, heads=heads, pieces=pieces
        ),
        out_shape=(jax.ShapeDtypeStruct((group_rows // pieces, model), BF16),) * pieces,
        in_specs=[whole(SMEM)] * 2 + [whole()] * 6,
        out_specs=(whole(),) * pieces,
        scratch_shapes=[
            pltpu.VMEM((slots, LANES), F32),
            pltpu.VMEM((slots, LANES), F32),
            pltpu.VMEM((reqs, LANES), F32),
            pltpu.VMEM((reqs, LANES), F32),
            pltpu.VMEM((LANES, LANES), F32),
            pltpu.VMEM((LANES, LANES), F32),
            pltpu.VMEM((reqs * span, HD), F32),
            pltpu.VMEM((group_rows, width), BF16),
        ],
        compiler_params=params(16),
        cost_estimate=cost(
            2 * group_rows * width * model, 2 * n * block * LANES + 8 * reqs * span * HD
        ),
        name="combine",
    )(codes, side, returned, own, retrieved, own_top, own_sum, w_out)

    if pieces == 2:
        swap = [(0, 1), (1, 0)]
        own_part, peer_part = partials
        theirs_peer = lax.ppermute(own_part, "grp", swap)
        theirs_own = lax.ppermute(peer_part, "grp", swap)
        units = w_down.shape[0]

        def forward(mine, theirs, own_rows, dtype):
            return pl.pallas_call(
                functools.partial(feed_forward, own=own_rows),
                out_shape=jax.ShapeDtypeStruct((rows, model), dtype),
                in_specs=[whole(SMEM)] + [whole()] * 6,
                out_specs=whole(),
                scratch_shapes=[pltpu.VMEM((rows, units), BF16)],
                compiler_params=params(24),
                cost_estimate=cost(6 * rows * model * units, 6 * model * units),
                name="feed_forward_own" if own_rows else "feed_forward_peer",
            )(side, tokens, mine, theirs, norm_ffn.reshape(1, -1), w_gate_up, w_down)

        sent = forward(peer_part, theirs_peer, False, BF16)
        received = lax.ppermute(sent, "grp", swap)
        base = forward(own_part, theirs_own, True, F32)
        layer_out = (base + received.astype(F32)).astype(BF16)
        return (layer_out, memory_out, momentum_out)

    head_sum = lax.psum_scatter(partials[0], "grp", scatter_dimension=0, tiled=True).astype(F32)
    own_rows = lax.dynamic_slice_in_dim(tokens, lax.axis_index("grp") * rows, rows, 0)
    residual = (own_rows.astype(F32) + head_sum).astype(BF16)
    ffn_in = rms_norm(residual, norm_ffn)
    piece = lax.all_gather(ffn_in, "grp", axis=0, tiled=True)
    gate = jnp.dot(piece, w_gate_up[0], preferred_element_type=F32)
    up = jnp.dot(piece, w_gate_up[1], preferred_element_type=F32)
    hidden = (jax.nn.silu(gate) * up).astype(BF16)
    ffn_out = lax.psum_scatter(
        jnp.dot(hidden, w_down, preferred_element_type=F32).astype(BF16),
        "grp",
        scatter_dimension=0,
        tiled=True,
    ).astype(F32)
    layer_out = (residual.astype(F32) + ffn_out).astype(BF16)
    return (layer_out, memory_out, momentum_out)


def solution(mesh):
    return jax.shard_map(
        on_device,
        mesh=mesh,
        in_specs=(
            P("req", None),
            P(),
            P(None, "grp"),
            P(None, "grp"),
            P(None, "grp"),
            P("grp", None),
            P(None, "grp"),
            P(None, "grp"),
            P("req", None, None, "grp"),
            P("req"),
            P("req"),
            P("req"),
            P("req", None, None),
            P("req", None),
            P("req"),
            P("req", "grp", None, None),
            P("req", "grp", None, None),
            P("req", None, "grp"),
            P("req", None, "grp"),
            P(),
            P(None, None, "grp"),
            P("grp", None),
        ),
        out_specs=(
            P(("req", "grp"), None),
            P("req", "grp", None, None),
            P("req", "grp", None, None),
        ),
        check_vma=False,
    )
```

```python
import functools
import math

import jax
import jax.numpy as jnp
from jax import lax
from jax.experimental import pallas as pl
from jax.experimental.pallas import tpu as pltpu
from jax.sharding import PartitionSpec as P

HD = 128
LANES = 128
EXTRA = 16
TOP_PARTS = 3
SUM_PARTS = 2

EPS = 1e-06
THETA = 0.5
NEG = -1e30

VMEM = pltpu.VMEM
SMEM = pltpu.SMEM
HBM = pltpu.HBM
F32 = jnp.float32
BF16 = jnp.bfloat16


def whole(space=VMEM):
    return pl.BlockSpec(memory_space=space)


def cost(flops, moved, special=0):
    return pl.CostEstimate(flops=flops, bytes_accessed=moved, transcendentals=special)


def keep_in(space, *arrays):
    return tuple(pltpu.with_memory_space_constraint(array, space) for array in arrays)


def params(mib=40):
    return pltpu.CompilerParams(vmem_limit_bytes=mib << 20)


def rms_norm(rows, gain):
    values = rows.astype(F32)
    factor = lax.rsqrt(jnp.mean(values * values, axis=-1, keepdims=True) + EPS)
    return (values * factor * gain).astype(BF16)


def nt_dot(left, right):
    return lax.dot_general(left, right, (((1,), (1,)), ((), ())), preferred_element_type=F32)


def column_to_row(column, count):
    row_id = lax.broadcasted_iota(jnp.int32, (count, LANES), 0)
    lane_id = lax.broadcasted_iota(jnp.int32, (count, LANES), 1)
    spread = jnp.where(row_id == lane_id, jnp.broadcast_to(column, (count, LANES)), 0.0)
    return jnp.sum(spread, axis=0, keepdims=True)


def split_parts(row, count):
    parts = []
    for _ in range(count):
        part = row.astype(BF16).astype(F32)
        parts.append(part)
        row = row - part
    return parts


def project_queries(tok_ref, gain_ref, w_ref, normed_ref, q_ref, turned_ref, *, reqs, draft, heads):
    normed_ref[...] = rms_norm(tok_ref[...], gain_ref[...])
    q_ref[...] = jnp.dot(normed_ref[...], w_ref[...], preferred_element_type=F32).astype(BF16)
    span = heads * draft
    for r in range(reqs):
        rows = slice(r * draft, (r + 1) * draft)
        pieces = [q_ref[rows, h * HD : (h + 1) * HD].astype(F32) for h in range(heads)]
        if span < LANES:
            pieces.append(jnp.zeros((LANES - span, HD), F32))
        tile = jnp.concatenate(pieces, axis=0)
        turned_ref[r * HD : (r + 1) * HD, :] = jnp.transpose(tile).astype(BF16)


def project_keys(normed_ref, wk_ref, wv_ref, k_ref, v_ref):
    normed = normed_ref[...]
    k_ref[...] = jnp.dot(normed, wk_ref[...], preferred_element_type=F32).astype(BF16)
    v_ref[...] = jnp.dot(normed, wv_ref[...], preferred_element_type=F32).astype(BF16)


def pack_queries(codes, lengths, turned_ref, out_ref, *, n, cap, reqs, page_len):
    block = cap * HD + EXTRA
    row_id = lax.broadcasted_iota(jnp.int32, (EXTRA, LANES), 0)

    def one(d, carry):
        base = pl.multiple_of(d * block, EXTRA)
        tail = jnp.zeros((EXTRA, LANES), F32)
        for c in range(cap):
            code = codes[d, 0, c]
            r = lax.rem(code, reqs)
            page = lax.div(code, reqs)
            live = jnp.clip(lengths[r] - page * page_len, 0, page_len)
            tail = jnp.where(row_id == c, live.astype(F32), tail)
            rows = pl.ds(pl.multiple_of(r * HD, HD), HD)
            out_ref[pl.ds(base + c * HD, HD), :] = turned_ref[rows, :]
        out_ref[pl.ds(base + cap * HD, EXTRA), :] = tail.astype(BF16)
        return carry

    lax.fori_loop(0, n, one, 0)


def page_attention(q_ref, kv_ref, out_ref, *, cap, draft, heads, page_len, scale):
    span = heads * draft
    limits = q_ref[cap * HD : cap * HD + EXTRA, :].astype(F32)
    token = lax.broadcasted_iota(jnp.int32, (page_len, LANES), 0).astype(F32)
    row_id = lax.broadcasted_iota(jnp.int32, (EXTRA, LANES), 0)
    head_of = lax.broadcasted_iota(jnp.int32, (HD, LANES), 1) // draft
    tail = jnp.zeros((EXTRA, LANES), F32)
    all_scores = []
    for c in range(cap):
        turned = q_ref[c * HD : (c + 1) * HD, :]
        blocks = [jnp.where(head_of == h, turned, jnp.zeros_like(turned)) for h in range(heads)]
        all_scores.append(
            jnp.dot(kv_ref[c, 0], jnp.concatenate(blocks, axis=0), preferred_element_type=F32)
        )
    all_weights = []
    for c in range(cap):
        scores = jnp.where(token < limits[c : c + 1, :], all_scores[c] * scale, NEG)
        top = jnp.max(scores, axis=0, keepdims=True)
        weight = jnp.exp(scores - top)
        total = jnp.sum(weight, axis=0, keepdims=True)
        all_weights.append(jnp.transpose(weight).astype(BF16))
        parts = split_parts(top, TOP_PARTS) + split_parts(total, SUM_PARTS)
        for p, part in enumerate(parts):
            tail = jnp.where(row_id == p * cap + c, part, tail)
    for c in range(cap):
        for h in range(heads):
            rows = slice(h * draft, (h + 1) * draft)
            numer = jnp.dot(
                all_weights[c][rows, :],
                kv_ref[c, 1, :, h * HD : (h + 1) * HD],
                preferred_element_type=F32,
            )
            out_ref[c * span + h * draft : c * span + (h + 1) * draft, :] = numer.astype(BF16)
    out_ref[cap * span : cap * span + EXTRA, :] = tail.astype(BF16)


def local_attention(
    q_ref, k_ref, v_ref, pk_ref, pv_ref, mask_ref, mem_ref,
    o_ref, ret_ref, top_ref, sum_ref, *, heads, draft, scale,
):
    r = pl.program_id(0)
    seen = mask_ref[0] == 1
    tops, totals = [], []
    for h in range(heads):
        cols = slice(h * HD, (h + 1) * HD)
        rows = slice(h * draft, (h + 1) * draft)
        query = q_ref[:, cols]
        tree = jnp.where(seen, nt_dot(query, k_ref[:, cols]) * scale, NEG)
        fixed = nt_dot(query, pk_ref[:, cols]) * scale
        top = jnp.maximum(
            jnp.max(tree, axis=1, keepdims=True), jnp.max(fixed, axis=1, keepdims=True)
        )
        tree_w = jnp.exp(tree - top)
        fixed_w = jnp.exp(fixed - top)
        total = jnp.sum(tree_w, axis=1, keepdims=True) + jnp.sum(fixed_w, axis=1, keepdims=True)
        numer = jnp.dot(tree_w.astype(BF16), v_ref[:, cols], preferred_element_type=F32)
        numer = numer + jnp.dot(fixed_w.astype(BF16), pv_ref[:, cols], preferred_element_type=F32)
        o_ref[rows, :] = numer
        tops.append(top)
        totals.append(total)
        wide = query.astype(F32)
        unit = wide * lax.rsqrt(jnp.sum(wide * wide, axis=1, keepdims=True) + EPS)
        ret_ref[rows, :] = jnp.dot(
            unit, mem_ref[0, h], preferred_element_type=F32, precision=lax.Precision.HIGHEST
        )
    span = heads * draft
    top_ref[pl.ds(r, 1), :] = column_to_row(jnp.concatenate(tops, axis=0), span)
    sum_ref[pl.ds(r, 1), :] = column_to_row(jnp.concatenate(totals, axis=0), span)


def update_memory(
    path, count, mom_code, forget_code, k_ref, v_ref, mem_ref, mom_ref, mem_out, mom_out,
    wide_k, wide_v, unit_ref, value_ref, turned_ref, *, heads, steps,
):
    r = pl.program_id(0)
    wide_k[...] = k_ref[...].astype(F32)
    wide_v[...] = v_ref[...].astype(F32)
    unit_ref[...] = jnp.zeros_like(unit_ref)
    for n in range(steps):
        node = path[r * steps + n]
        k_row = wide_k[pl.ds(node, 1), :]
        v_row = wide_v[pl.ds(node, 1), :]
        for h in range(heads):
            unit_ref[h * steps + n : h * steps + n + 1, :] = k_row[:, h * HD : (h + 1) * HD]
            value_ref[h * steps + n : h * steps + n + 1, :] = v_row[:, h * HD : (h + 1) * HD]
    keys = unit_ref[...]
    unit = keys * lax.rsqrt(jnp.sum(keys * keys, axis=1, keepdims=True) + EPS)
    turned_ref[...] = jnp.transpose(unit)

    def advance(n, mem_src, mom_src):
        for h in range(heads):
            at = (r * steps + n) * heads + h
            eta = 0.97 - 0.06 * mom_code[at].astype(F32)
            keep = 1.0 - (0.01 + 0.02 * forget_code[at].astype(F32))
            row = h * steps + n
            column = turned_ref[:, row : row + 1]
            matrix = mem_src[0, h]
            predicted = jnp.sum(column * matrix, axis=0, keepdims=True)
            error = THETA * (predicted - value_ref[row : row + 1, :])
            moved = eta * mom_src[0, h] - column * error
            mom_out[0, h] = moved
            mem_out[0, h] = keep * matrix + moved

    advance(0, mem_ref, mom_ref)
    for n in range(1, steps):
        pl.when(n < count[r])(functools.partial(advance, n, mem_out, mom_out))


def combine(
    codes, side, msg_ref, o_ref, ret_ref, own_top_ref, own_sum_ref, w_ref, up_hbm, down_hbm, *rest,
    n, cap, reqs, draft, heads, pieces,
):
    outs = rest[:pieces]
    staged = rest[pieces:-9]
    part_top, part_sum, best, total, weight, own_weight, acc, mixed, sems = rest[-9:]
    copies = [
        pltpu.make_async_copy(source, target, sems.at[i])
        for i, (source, target) in enumerate(zip((up_hbm, down_hbm), staged))
    ]
    for copy in copies:
        copy.start()
    span = heads * draft
    block = cap * span + EXTRA
    slots = n * cap
    for d in range(n):
        at = d * block + cap * span
        tail = msg_ref[at : at + EXTRA, :].astype(F32)
        rows = [tail[p * cap : (p + 1) * cap] for p in range(TOP_PARTS + SUM_PARTS)]
        part_top[d * cap : (d + 1) * cap, :] = rows[0] + rows[1] + rows[2]
        part_sum[d * cap : (d + 1) * cap, :] = rows[3] + rows[4]
    best[...] = own_top_ref[...]
    owners = [lax.rem(codes[s // cap, 0, s % cap], reqs) for s in range(slots)]
    for s in range(slots):
        r = owners[s]
        best[pl.ds(r, 1), :] = jnp.maximum(best[pl.ds(r, 1), :], part_top[s : s + 1, :])
    own_weight[...] = jnp.zeros_like(own_weight)
    weight[...] = jnp.zeros_like(weight)
    start = jnp.exp(own_top_ref[...] - best[...])
    total[...] = start * own_sum_ref[...]
    for s in range(slots):
        r = owners[s]
        term = jnp.exp(part_top[s : s + 1, :] - best[pl.ds(r, 1), :])
        weight[s : s + 1, :] = term
        total[pl.ds(r, 1), :] = total[pl.ds(r, 1), :] + term * part_sum[s : s + 1, :]
    inverse = 1.0 / total[...]
    own_weight[0:reqs, :] = start * inverse
    total[...] = inverse
    for s in range(slots):
        weight[s : s + 1, :] = weight[s : s + 1, :] * total[pl.ds(owners[s], 1), :]
    turned = jnp.transpose(weight[...])
    own_turned = jnp.transpose(own_weight[...])
    for r in range(reqs):
        rows = slice(r * span, (r + 1) * span)
        acc[rows, :] = o_ref[rows, :] * own_turned[0:span, r : r + 1] + ret_ref[rows, :]
    for s in range(slots):
        at = (s // cap) * block + (s % cap) * span
        rows = pl.ds(pl.multiple_of(owners[s] * span, span), span)
        acc[rows, :] = acc[rows, :] + msg_ref[at : at + span, :].astype(F32) * turned[
            0:span, s : s + 1
        ]
    for r in range(reqs):
        for h in range(heads):
            at = r * span + h * draft
            mixed[r * draft : (r + 1) * draft, h * HD : (h + 1) * HD] = acc[
                at : at + draft, :
            ].astype(BF16)
    rows = reqs * draft // pieces
    for p, out_ref in enumerate(outs):
        first = lax.rem(side[0] + p, pieces) * rows
        out_ref[...] = jnp.dot(
            mixed[pl.ds(pl.multiple_of(first, rows), rows), :],
            w_ref[...],
            preferred_element_type=F32,
        ).astype(BF16)
    for copy in copies:
        copy.wait()


def feed_forward(
    side, tok_ref, mine_ref, theirs_ref, gain_ref, up_ref, down_ref, out_ref, hidden, *, own
):
    rows = mine_ref.shape[0]
    units = down_ref.shape[0]
    at = side[0] if own else 1 - side[0]
    tokens = tok_ref[pl.ds(pl.multiple_of(at * rows, rows), rows), :].astype(F32)
    summed = tokens + mine_ref[...].astype(F32) + theirs_ref[...].astype(F32)
    residual = summed.astype(BF16)
    ffn_in = rms_norm(residual, gain_ref[...])
    step = 256
    for first in range(0, units, step):
        cols = slice(first, min(first + step, units))
        gate = jnp.dot(ffn_in, up_ref[0, :, cols], preferred_element_type=F32)
        up = jnp.dot(ffn_in, up_ref[1, :, cols], preferred_element_type=F32)
        hidden[:, cols] = (gate / (1.0 + jnp.exp(-gate)) * up).astype(BF16)
    for first in range(0, out_ref.shape[1], step):
        cols = slice(first, first + step)
        part = jnp.dot(hidden[...], down_ref[:, cols], preferred_element_type=F32)
        if own:
            part = part + residual[:, cols].astype(F32)
        out_ref[:, cols] = part.astype(out_ref.dtype)


def on_device(
    tokens,
    norm_attn,
    w_query,
    w_key,
    w_value,
    w_out,
    persist_keys,
    persist_values,
    kv_cache,
    slot_request,
    slot_page,
    cache_len,
    tree_mask,
    accept_path,
    accept_len,
    memory,
    momentum,
    momentum_code,
    forget_code,
    norm_ffn,
    w_gate_up,
    w_down,
):
    n = lax.axis_size("req")
    group_rows, model = tokens.shape
    reqs = cache_len.shape[0]
    draft = tree_mask.shape[1]
    steps = accept_path.shape[1]
    width = w_query.shape[1]
    heads = width // HD
    span = heads * draft
    slots = kv_cache.shape[0]
    cap = slots // n
    fixed_count = persist_keys.shape[0]
    page_len = kv_cache.shape[2]
    ask_block = cap * HD + EXTRA
    block = cap * span + EXTRA
    scale = 1.0 / math.sqrt(HD)

    label = (slot_page * reqs + lax.rem(slot_request, reqs)).reshape(n, 1, cap)
    codes = lax.all_to_all(label, "req", split_axis=0, concat_axis=0, tiled=True)

    normed, queries, turned = pl.pallas_call(
        functools.partial(project_queries, reqs=reqs, draft=draft, heads=heads),
        out_shape=(
            HBM((group_rows, model), BF16),
            HBM((group_rows, width), BF16),
            jax.ShapeDtypeStruct((reqs * HD, LANES), BF16),
        ),
        in_specs=[whole()] * 3,
        out_specs=(whole(),) * 3,
        compiler_params=params(12),
        cost_estimate=cost(
            2 * group_rows * model * width, 2 * model * (2 * group_rows + width)
        ),
        name="project_queries",
    )(*keep_in(HBM, tokens, norm_attn.reshape(1, -1), w_query))

    packed = pl.pallas_call(
        functools.partial(pack_queries, n=n, cap=cap, reqs=reqs, page_len=page_len),
        out_shape=HBM((n * ask_block, LANES), BF16),
        in_specs=[whole(SMEM), whole(SMEM), whole()],
        out_specs=whole(),
        compiler_params=params(8),
        cost_estimate=cost(0, 4 * n * ask_block * LANES),
        name="pack_queries",
    )(codes, *keep_in(HBM, cache_len), turned)
    asked = lax.all_to_all(packed, "req", split_axis=0, concat_axis=0, tiled=True)

    keys, values = pl.pallas_call(
        project_keys,
        out_shape=(HBM((group_rows, width), BF16),) * 2,
        in_specs=[whole()] * 3,
        out_specs=(whole(),) * 2,
        compiler_params=params(12),
        cost_estimate=cost(
            4 * group_rows * model * width, 2 * model * (group_rows + 2 * width)
        ),
        name="project_keys",
    )(*keep_in(HBM, normed, w_key, w_value))

    row_block = pl.BlockSpec((draft, width), lambda r, *_: (r, 0))
    fixed_block = pl.BlockSpec((fixed_count, width), lambda r, *_: (0, 0))
    matrix_block = pl.BlockSpec((1, heads, HD, HD), lambda r, *_: (r, 0, 0, 0))
    span_block = pl.BlockSpec((span, HD), lambda r, *_: (r, 0))
    own, retrieved, own_top, own_sum = pl.pallas_call(
        functools.partial(local_attention, heads=heads, draft=draft, scale=scale),
        grid=(reqs,),
        out_shape=(
            HBM((reqs * span, HD), F32),
            HBM((reqs * span, HD), F32),
            jax.ShapeDtypeStruct((reqs, LANES), F32),
            jax.ShapeDtypeStruct((reqs, LANES), F32),
        ),
        in_specs=[
            row_block,
            row_block,
            row_block,
            fixed_block,
            fixed_block,
            pl.BlockSpec((1, draft, draft), lambda r: (r, 0, 0)),
            matrix_block,
        ],
        out_specs=(span_block, span_block) + (pl.BlockSpec((reqs, LANES), lambda r: (0, 0)),) * 2,
        compiler_params=params(10),
        cost_estimate=cost(
            2 * reqs * span * HD * (2 * (draft + fixed_count) + 6 * HD),
            4 * reqs * (heads * HD * HD + 2 * span * HD),
            reqs * span * (draft + fixed_count),
        ),
        name="local_attention",
    )(*keep_in(HBM, queries, keys, values, persist_keys, persist_values, tree_mask, memory))

    matrices = jax.ShapeDtypeStruct(memory.shape, F32)
    memory_out, momentum_out = pl.pallas_call(
        functools.partial(update_memory, heads=heads, steps=steps),
        grid_spec=pltpu.PrefetchScalarGridSpec(
            num_scalar_prefetch=4,
            grid=(reqs,),
            in_specs=[row_block, row_block, matrix_block, matrix_block],
            out_specs=(matrix_block, matrix_block),
            scratch_shapes=[
                pltpu.VMEM((draft, width), F32),
                pltpu.VMEM((draft, width), F32),
                pltpu.VMEM((LANES, HD), F32),
                pltpu.VMEM((heads * steps, HD), F32),
                pltpu.VMEM((HD, LANES), F32),
            ],
        ),
        out_shape=(matrices, matrices),
        compiler_params=params(10),
        cost_estimate=cost(
            14 * reqs * heads * HD * HD * steps * 8, 16 * reqs * heads * HD * HD
        ),
        name="update_memory",
    )(
        accept_path.reshape(-1),
        accept_len,
        momentum_code.reshape(-1),
        forget_code.reshape(-1),
        *keep_in(HBM, keys, values, memory, momentum),
    )

    asked, memory_out, momentum_out, keys, values = lax.optimization_barrier(
        (asked, memory_out, momentum_out, keys, values)
    )
    answers = pl.pallas_call(
        functools.partial(
            page_attention, cap=cap, draft=draft, heads=heads, page_len=page_len, scale=scale
        ),
        grid=(n,),
        out_shape=HBM((n * block, LANES), BF16),
        in_specs=[
            pl.BlockSpec((ask_block, LANES), lambda d: (d, 0)),
            pl.BlockSpec((cap, 2, page_len, width), lambda d: (d, 0, 0, 0)),
        ],
        out_specs=pl.BlockSpec((block, LANES), lambda d: (d, 0)),
        compiler_params=params(12),
        cost_estimate=cost(
            4 * slots * span * page_len * HD,
            4 * slots * page_len * width + 4 * n * block * LANES,
            slots * span * page_len,
        ),
        name="page_attention",
    )(asked, *keep_in(HBM, kv_cache))
    side = lax.axis_index("grp").astype(jnp.int32).reshape(1)
    grp = lax.axis_size("grp")
    pieces = 2 if grp == 2 and w_down.shape[0] % LANES == 0 else 1
    returned = lax.all_to_all(answers, "req", split_axis=0, concat_axis=0, tiled=True)
    rows = group_rows // grp
    near = (VMEM(w_gate_up.shape, BF16), VMEM(w_down.shape, BF16)) if pieces == 2 else ()
    partials = pl.pallas_call(
        functools.partial(
            combine, n=n, cap=cap, reqs=reqs, draft=draft, heads=heads, pieces=pieces
        ),
        out_shape=(jax.ShapeDtypeStruct((group_rows // pieces, model), BF16),) * pieces + near,
        in_specs=[whole(SMEM)] * 2 + [whole()] * 6 + [whole(HBM)] * 2,
        out_specs=(whole(),) * (pieces + len(near)),
        scratch_shapes=[
            pltpu.VMEM((slots, LANES), F32),
            pltpu.VMEM((slots, LANES), F32),
            pltpu.VMEM((reqs, LANES), F32),
            pltpu.VMEM((reqs, LANES), F32),
            pltpu.VMEM((LANES, LANES), F32),
            pltpu.VMEM((LANES, LANES), F32),
            pltpu.VMEM((reqs * span, HD), F32),
            pltpu.VMEM((group_rows, width), BF16),
            pltpu.SemaphoreType.DMA((2,)),
        ],
        compiler_params=params(16),
        cost_estimate=cost(
            2 * group_rows * width * model, 2 * n * block * LANES + 8 * reqs * span * HD
        ),
        name="combine",
    )(codes, side, *keep_in(HBM, returned, own, retrieved), own_top, own_sum, *keep_in(HBM, w_out, w_gate_up, w_down))

    if pieces == 2:
        swap = [(0, 1), (1, 0)]
        own_part, peer_part, up_near, down_near = partials
        theirs_peer = lax.ppermute(own_part, "grp", swap)
        peer_part, theirs_peer = lax.optimization_barrier((peer_part, theirs_peer))
        theirs_own = lax.ppermute(peer_part, "grp", swap)
        units = w_down.shape[0]

        def forward(mine, theirs, own_rows, dtype):
            return pl.pallas_call(
                functools.partial(feed_forward, own=own_rows),
                out_shape=jax.ShapeDtypeStruct((rows, model), dtype),
                in_specs=[whole(SMEM)] + [whole()] * 6,
                out_specs=whole(),
                scratch_shapes=[pltpu.VMEM((rows, units), BF16)],
                compiler_params=params(24),
                cost_estimate=cost(6 * rows * model * units, 6 * model * units),
                name="feed_forward_own" if own_rows else "feed_forward_peer",
            )(side, tokens, mine, theirs, norm_ffn.reshape(1, -1), *keep_in(VMEM, up_near, down_near))

        sent = forward(peer_part, theirs_peer, False, BF16)
        received = lax.ppermute(sent, "grp", swap)
        base = forward(own_part, theirs_own, True, F32)
        layer_out = (base + received.astype(F32)).astype(BF16)
        return (layer_out, memory_out, momentum_out)

    head_sum = lax.psum_scatter(partials[0], "grp", scatter_dimension=0, tiled=True).astype(F32)
    own_rows = lax.dynamic_slice_in_dim(tokens, lax.axis_index("grp") * rows, rows, 0)
    residual = (own_rows.astype(F32) + head_sum).astype(BF16)
    ffn_in = rms_norm(residual, norm_ffn)
    piece = lax.all_gather(ffn_in, "grp", axis=0, tiled=True)
    gate = jnp.dot(piece, w_gate_up[0], preferred_element_type=F32)
    up = jnp.dot(piece, w_gate_up[1], preferred_element_type=F32)
    hidden = (jax.nn.silu(gate) * up).astype(BF16)
    ffn_out = lax.psum_scatter(
        jnp.dot(hidden, w_down, preferred_element_type=F32).astype(BF16),
        "grp",
        scatter_dimension=0,
        tiled=True,
    ).astype(F32)
    layer_out = (residual.astype(F32) + ffn_out).astype(BF16)
    return (layer_out, memory_out, momentum_out)


def solution(mesh):
    return jax.shard_map(
        on_device,
        mesh=mesh,
        in_specs=(
            P("req", None),
            P(),
            P(None, "grp"),
            P(None, "grp"),
            P(None, "grp"),
            P("grp", None),
            P(None, "grp"),
            P(None, "grp"),
            P("req", None, None, "grp"),
            P("req"),
            P("req"),
            P("req"),
            P("req", None, None),
            P("req", None),
            P("req"),
            P("req", "grp", None, None),
            P("req", "grp", None, None),
            P("req", None, "grp"),
            P("req", None, "grp"),
            P(),
            P(None, None, "grp"),
            P("grp", None),
        ),
        out_specs=(
            P(("req", "grp"), None),
            P("req", "grp", None, None),
            P("req", "grp", None, None),
        ),
        check_vma=False,
    )
```

```python
import functools
import math

import jax
import jax.numpy as jnp
from jax import lax
from jax.experimental import pallas as pl
from jax.experimental.pallas import tpu as pltpu
from jax.sharding import PartitionSpec as P

HD = 128
LANES = 128
EXTRA = 16
TOP_PARTS = 3
SUM_PARTS = 2

EPS = 1e-06
THETA = 0.5
NEG = -1e30

VMEM = pltpu.VMEM
SMEM = pltpu.SMEM
HBM = pltpu.HBM
F32 = jnp.float32
BF16 = jnp.bfloat16


def whole(space=VMEM):
    return pl.BlockSpec(memory_space=space)


def cost(flops, moved, special=0):
    return pl.CostEstimate(flops=flops, bytes_accessed=moved, transcendentals=special)


def keep_in(space, *arrays):
    return tuple(pltpu.with_memory_space_constraint(array, space) for array in arrays)


def params(mib=40):
    return pltpu.CompilerParams(vmem_limit_bytes=mib << 20)


def rms_norm(rows, gain):
    values = rows.astype(F32)
    factor = lax.rsqrt(jnp.mean(values * values, axis=-1, keepdims=True) + EPS)
    return (values * factor * gain).astype(BF16)


def nt_dot(left, right):
    return lax.dot_general(left, right, (((1,), (1,)), ((), ())), preferred_element_type=F32)


def column_to_row(column, count):
    row_id = lax.broadcasted_iota(jnp.int32, (count, LANES), 0)
    lane_id = lax.broadcasted_iota(jnp.int32, (count, LANES), 1)
    spread = jnp.where(row_id == lane_id, jnp.broadcast_to(column, (count, LANES)), 0.0)
    return jnp.sum(spread, axis=0, keepdims=True)


def split_parts(row, count):
    parts = []
    for _ in range(count):
        part = row.astype(BF16).astype(F32)
        parts.append(part)
        row = row - part
    return parts


def project_queries(tok_ref, gain_ref, w_ref, normed_ref, q_ref, turned_ref, *, reqs, draft, heads):
    normed_ref[...] = rms_norm(tok_ref[...], gain_ref[...])
    q_ref[...] = jnp.dot(normed_ref[...], w_ref[...], preferred_element_type=F32).astype(BF16)
    span = heads * draft
    for r in range(reqs):
        rows = slice(r * draft, (r + 1) * draft)
        pieces = [q_ref[rows, h * HD : (h + 1) * HD].astype(F32) for h in range(heads)]
        if span < LANES:
            pieces.append(jnp.zeros((LANES - span, HD), F32))
        tile = jnp.concatenate(pieces, axis=0)
        turned_ref[r * HD : (r + 1) * HD, :] = jnp.transpose(tile).astype(BF16)


def project_keys(normed_ref, wk_ref, wv_ref, k_ref, v_ref):
    normed = normed_ref[...]
    k_ref[...] = jnp.dot(normed, wk_ref[...], preferred_element_type=F32).astype(BF16)
    v_ref[...] = jnp.dot(normed, wv_ref[...], preferred_element_type=F32).astype(BF16)


def pack_queries(codes, lengths, turned_ref, out_ref, *, n, cap, reqs, page_len):
    block = cap * HD + EXTRA
    row_id = lax.broadcasted_iota(jnp.int32, (EXTRA, LANES), 0)

    def one(d, carry):
        base = pl.multiple_of(d * block, EXTRA)
        tail = jnp.zeros((EXTRA, LANES), F32)
        for c in range(cap):
            code = codes[d, 0, c]
            r = lax.rem(code, reqs)
            page = lax.div(code, reqs)
            live = jnp.clip(lengths[r] - page * page_len, 0, page_len)
            tail = jnp.where(row_id == c, live.astype(F32), tail)
            rows = pl.ds(pl.multiple_of(r * HD, HD), HD)
            out_ref[pl.ds(base + c * HD, HD), :] = turned_ref[rows, :]
        out_ref[pl.ds(base + cap * HD, EXTRA), :] = tail.astype(BF16)
        return carry

    lax.fori_loop(0, n, one, 0)


def page_attention(
    q_ref, kv_hbm, out_hbm, kv_buf, out_buf, in_sems, out_sems,
    *, n, cap, draft, heads, page_len, scale, group,
):
    span = heads * draft
    ask_block = cap * HD + EXTRA
    block = cap * span + EXTRA
    token = lax.broadcasted_iota(jnp.int32, (page_len, LANES), 0).astype(F32)
    row_id = lax.broadcasted_iota(jnp.int32, (EXTRA, LANES), 0)
    head_of = lax.broadcasted_iota(jnp.int32, (HD, LANES), 1) // draft

    def arrival(d):
        return pltpu.make_async_copy(
            kv_hbm.at[pl.ds(d * cap, cap)], kv_buf.at[d], in_sems.at[d]
        )

    def departure(d):
        rows = pl.ds(pl.multiple_of(d * block, EXTRA), block)
        return pltpu.make_async_copy(out_buf.at[rows], out_hbm.at[rows], out_sems.at[d])

    for d in range(n):
        arrival(d).start()

    def one(i, carry):
        pairs = [(i * group + g, c) for g in range(group) for c in range(cap)]
        limits = []
        for g in range(group):
            d = i * group + g
            arrival(d).wait()
            at = pl.multiple_of(d * ask_block + cap * HD, EXTRA)
            limits.append(q_ref[pl.ds(at, EXTRA), :].astype(F32))
        all_scores = []
        for d, c in pairs:
            at = pl.multiple_of(d * ask_block + c * HD, EXTRA)
            turned = q_ref[pl.ds(at, HD), :]
            blocks = [jnp.where(head_of == h, turned, jnp.zeros_like(turned)) for h in range(heads)]
            all_scores.append(
                jnp.dot(
                    kv_buf[d, c, 0], jnp.concatenate(blocks, axis=0), preferred_element_type=F32
                )
            )
        all_weights = []
        tails = [jnp.zeros((EXTRA, LANES), F32) for _ in range(group)]
        for j, (d, c) in enumerate(pairs):
            g = j // cap
            scores = jnp.where(token < limits[g][c : c + 1, :], all_scores[j] * scale, NEG)
            top = jnp.max(scores, axis=0, keepdims=True)
            weight = jnp.exp(scores - top)
            total = jnp.sum(weight, axis=0, keepdims=True)
            all_weights.append(jnp.transpose(weight).astype(BF16))
            parts = split_parts(top, TOP_PARTS) + split_parts(total, SUM_PARTS)
            for p, part in enumerate(parts):
                tails[g] = jnp.where(row_id == p * cap + c, part, tails[g])
        for j, (d, c) in enumerate(pairs):
            for h in range(heads):
                numer = jnp.dot(
                    all_weights[j][h * draft : (h + 1) * draft, :],
                    kv_buf[d, c, 1, :, h * HD : (h + 1) * HD],
                    preferred_element_type=F32,
                )
                at = pl.multiple_of(d * block + c * span + h * draft, EXTRA)
                out_buf[pl.ds(at, draft), :] = numer.astype(BF16)
        for g in range(group):
            d = i * group + g
            at = pl.multiple_of(d * block + cap * span, EXTRA)
            out_buf[pl.ds(at, EXTRA), :] = tails[g].astype(BF16)
            departure(d).start()
        return carry

    lax.fori_loop(0, n // group, one, 0)
    for d in range(n):
        departure(d).wait()


def local_attention(
    q_ref, k_ref, v_ref, pk_ref, pv_ref, mask_ref, mem_ref,
    o_ref, ret_ref, top_ref, sum_ref, *, heads, draft, scale,
):
    r = pl.program_id(0)
    seen = mask_ref[0] == 1
    tops, totals = [], []
    for h in range(heads):
        cols = slice(h * HD, (h + 1) * HD)
        rows = slice(h * draft, (h + 1) * draft)
        query = q_ref[:, cols]
        tree = jnp.where(seen, nt_dot(query, k_ref[:, cols]) * scale, NEG)
        fixed = nt_dot(query, pk_ref[:, cols]) * scale
        top = jnp.maximum(
            jnp.max(tree, axis=1, keepdims=True), jnp.max(fixed, axis=1, keepdims=True)
        )
        tree_w = jnp.exp(tree - top)
        fixed_w = jnp.exp(fixed - top)
        total = jnp.sum(tree_w, axis=1, keepdims=True) + jnp.sum(fixed_w, axis=1, keepdims=True)
        numer = jnp.dot(tree_w.astype(BF16), v_ref[:, cols], preferred_element_type=F32)
        numer = numer + jnp.dot(fixed_w.astype(BF16), pv_ref[:, cols], preferred_element_type=F32)
        o_ref[rows, :] = numer
        tops.append(top)
        totals.append(total)
        wide = query.astype(F32)
        unit = wide * lax.rsqrt(jnp.sum(wide * wide, axis=1, keepdims=True) + EPS)
        ret_ref[rows, :] = jnp.dot(
            unit, mem_ref[0, h], preferred_element_type=F32, precision=lax.Precision.HIGHEST
        )
    span = heads * draft
    top_ref[pl.ds(r, 1), :] = column_to_row(jnp.concatenate(tops, axis=0), span)
    sum_ref[pl.ds(r, 1), :] = column_to_row(jnp.concatenate(totals, axis=0), span)


def update_memory(
    path, count, mom_code, forget_code, k_ref, v_ref, mem_ref, mom_ref, mem_out, mom_out,
    wide_k, wide_v, unit_ref, value_ref, turned_ref, *, heads, steps,
):
    r = pl.program_id(0)
    wide_k[...] = k_ref[...].astype(F32)
    wide_v[...] = v_ref[...].astype(F32)
    unit_ref[...] = jnp.zeros_like(unit_ref)
    for n in range(steps):
        node = path[r * steps + n]
        k_row = wide_k[pl.ds(node, 1), :]
        v_row = wide_v[pl.ds(node, 1), :]
        for h in range(heads):
            unit_ref[h * steps + n : h * steps + n + 1, :] = k_row[:, h * HD : (h + 1) * HD]
            value_ref[h * steps + n : h * steps + n + 1, :] = v_row[:, h * HD : (h + 1) * HD]
    keys = unit_ref[...]
    unit = keys * lax.rsqrt(jnp.sum(keys * keys, axis=1, keepdims=True) + EPS)
    turned_ref[...] = jnp.transpose(unit)

    def advance(n, mem_src, mom_src):
        for h in range(heads):
            at = (r * steps + n) * heads + h
            eta = 0.97 - 0.06 * mom_code[at].astype(F32)
            keep = 1.0 - (0.01 + 0.02 * forget_code[at].astype(F32))
            row = h * steps + n
            column = turned_ref[:, row : row + 1]
            matrix = mem_src[0, h]
            predicted = jnp.sum(column * matrix, axis=0, keepdims=True)
            error = THETA * (predicted - value_ref[row : row + 1, :])
            moved = eta * mom_src[0, h] - column * error
            mom_out[0, h] = moved
            mem_out[0, h] = keep * matrix + moved

    advance(0, mem_ref, mom_ref)
    for n in range(1, steps):
        pl.when(n < count[r])(functools.partial(advance, n, mem_out, mom_out))


def combine(
    codes, side, msg_ref, o_hbm, ret_hbm, own_top_ref, own_sum_ref, *rest,
    n, cap, reqs, draft, heads, pieces,
):
    outs = rest[:pieces]
    part_top, part_sum, best, total, weight, own_weight, acc, mixed, o_ref, ret_ref, sems = rest[
        pieces:
    ]
    copies = [
        pltpu.make_async_copy(o_hbm, o_ref, sems.at[0]),
        pltpu.make_async_copy(ret_hbm, ret_ref, sems.at[1]),
    ]
    for copy in copies:
        copy.start()
    span = heads * draft
    block = cap * span + EXTRA
    slots = n * cap
    for d in range(n):
        at = d * block + cap * span
        tail = msg_ref[at : at + EXTRA, :].astype(F32)
        rows = [tail[p * cap : (p + 1) * cap] for p in range(TOP_PARTS + SUM_PARTS)]
        part_top[d * cap : (d + 1) * cap, :] = rows[0] + rows[1] + rows[2]
        part_sum[d * cap : (d + 1) * cap, :] = rows[3] + rows[4]
    best[...] = own_top_ref[...]
    owners = [lax.rem(codes[s // cap, 0, s % cap], reqs) for s in range(slots)]
    for s in range(slots):
        r = owners[s]
        best[pl.ds(r, 1), :] = jnp.maximum(best[pl.ds(r, 1), :], part_top[s : s + 1, :])
    own_weight[...] = jnp.zeros_like(own_weight)
    weight[...] = jnp.zeros_like(weight)
    start = jnp.exp(own_top_ref[...] - best[...])
    total[...] = start * own_sum_ref[...]
    for s in range(slots):
        r = owners[s]
        term = jnp.exp(part_top[s : s + 1, :] - best[pl.ds(r, 1), :])
        weight[s : s + 1, :] = term
        total[pl.ds(r, 1), :] = total[pl.ds(r, 1), :] + term * part_sum[s : s + 1, :]
    inverse = 1.0 / total[...]
    own_weight[0:reqs, :] = start * inverse
    total[...] = inverse
    for s in range(slots):
        weight[s : s + 1, :] = weight[s : s + 1, :] * total[pl.ds(owners[s], 1), :]
    turned = jnp.transpose(weight[...])
    own_turned = jnp.transpose(own_weight[...])
    for copy in copies:
        copy.wait()
    for r in range(reqs):
        rows = slice(r * span, (r + 1) * span)
        acc[rows, :] = o_ref[rows, :] * own_turned[0:span, r : r + 1] + ret_ref[rows, :]
    for s in range(slots):
        at = (s // cap) * block + (s % cap) * span
        rows = pl.ds(pl.multiple_of(owners[s] * span, span), span)
        acc[rows, :] = acc[rows, :] + msg_ref[at : at + span, :].astype(F32) * turned[
            0:span, s : s + 1
        ]
    for r in range(reqs):
        for h in range(heads):
            at = r * span + h * draft
            mixed[r * draft : (r + 1) * draft, h * HD : (h + 1) * HD] = acc[
                at : at + draft, :
            ].astype(BF16)
    rows = reqs * draft // pieces
    for p, out_ref in enumerate(outs):
        first = lax.rem(side[0] + p, pieces) * rows
        out_ref[...] = mixed[pl.ds(pl.multiple_of(first, rows), rows), :]


def run_copies(pairs, sems):
    copies = [
        pltpu.make_async_copy(source, target, sems.at[i])
        for i, (source, target) in enumerate(pairs)
    ]
    for copy in copies:
        copy.start()
    return copies


def stage_weights(
    side, out_w, gate_up_w, down_w, one_a, one_o, two_a, two_o, out_all, gate_up_all, down_own, sems
):
    width = out_w.shape[0] // 2
    pairs = [(out_w, out_all.at[0]), (gate_up_w, gate_up_all.at[0]), (down_w, down_own)]
    for half, a, o in ((side[1], one_a, one_o), (1 - side[1], two_a, two_o)):
        rows = pl.ds(pl.multiple_of(half * width, EXTRA), width)
        pairs.append((o, out_all.at[1, rows]))
        pairs.append((a, gate_up_all.at[1, half]))
    for copy in run_copies(pairs, sems):
        copy.wait()


def feed_up(
    side, tok_ref, mine_ref, theirs_ref, gain_ref, out_w, gate_up_w, residual_ref, hidden_ref
):
    rows = mine_ref.shape[0]
    units = gate_up_w.shape[3]
    tokens = tok_ref[pl.ds(pl.multiple_of(side[0] * rows, rows), rows), :].astype(F32)
    summed = tokens + jnp.dot(mine_ref[...], out_w[0], preferred_element_type=F32)
    summed = summed + jnp.dot(theirs_ref[...], out_w[1], preferred_element_type=F32)
    residual_ref[...] = summed.astype(BF16)
    ffn_in = rms_norm(residual_ref[...], gain_ref[...])
    step = 256
    for half in range(2):
        for first in range(0, units, step):
            cols = slice(first, min(first + step, units))
            gate = jnp.dot(ffn_in, gate_up_w[half, 0, :, cols], preferred_element_type=F32)
            up = jnp.dot(ffn_in, gate_up_w[half, 1, :, cols], preferred_element_type=F32)
            hidden_ref[half, :, cols] = (gate / (1.0 + jnp.exp(-gate)) * up).astype(BF16)


def feed_down(
    side, residual_ref, hidden_ref, down_own, one_d, two_d, out_ref, down_peer, total, sems
):
    depth = one_d.shape[0]
    pairs = []
    for half, d in ((side[1], one_d), (1 - side[1], two_d)):
        pairs.append((d, down_peer.at[pl.ds(pl.multiple_of(half * depth, EXTRA), depth)]))
    copies = run_copies(pairs, sems)
    total[...] = residual_ref[...].astype(F32) + jnp.dot(
        hidden_ref[0], down_own[...], preferred_element_type=F32
    )
    for copy in copies:
        copy.wait()
    out_ref[...] = (
        total[...] + jnp.dot(hidden_ref[1], down_peer[...], preferred_element_type=F32)
    ).astype(BF16)


def on_device(
    tokens,
    norm_attn,
    w_query,
    w_key,
    w_value,
    w_out,
    persist_keys,
    persist_values,
    kv_cache,
    slot_request,
    slot_page,
    cache_len,
    tree_mask,
    accept_path,
    accept_len,
    memory,
    momentum,
    momentum_code,
    forget_code,
    norm_ffn,
    w_gate_up,
    w_down,
):
    n = lax.axis_size("req")
    group_rows, model = tokens.shape
    reqs = cache_len.shape[0]
    draft = tree_mask.shape[1]
    steps = accept_path.shape[1]
    width = w_query.shape[1]
    heads = width // HD
    span = heads * draft
    slots = kv_cache.shape[0]
    cap = slots // n
    fixed_count = persist_keys.shape[0]
    page_len = kv_cache.shape[2]
    ask_block = cap * HD + EXTRA
    block = cap * span + EXTRA
    scale = 1.0 / math.sqrt(HD)

    label = (slot_page * reqs + lax.rem(slot_request, reqs)).reshape(n, 1, cap)
    codes = lax.all_to_all(label, "req", split_axis=0, concat_axis=0, tiled=True)

    grp = lax.axis_size("grp")
    pieces = 2 if grp == 2 and w_down.shape[0] % (2 * EXTRA) == 0 and n % 2 == 0 else 1
    core = lax.rem(lax.axis_index("req"), 2)
    side = jnp.stack([lax.axis_index("grp"), core]).astype(jnp.int32)
    if pieces == 2:
        swap = [(0, 1), (1, 0)]
        half_down, half_out = w_down.shape[0] // 2, width // 2
        one_a = lax.ppermute(
            lax.dynamic_index_in_dim(w_gate_up, core, 0, keepdims=False), "grp", swap
        )
        out_half = lax.dynamic_slice_in_dim(w_out, core * half_out, half_out, 0)
        down_half = lax.dynamic_slice_in_dim(w_down, core * half_down, half_down, 0)

    normed, queries, turned = pl.pallas_call(
        functools.partial(project_queries, reqs=reqs, draft=draft, heads=heads),
        out_shape=(
            HBM((group_rows, model), BF16),
            HBM((group_rows, width), BF16),
            jax.ShapeDtypeStruct((reqs * HD, LANES), BF16),
        ),
        in_specs=[whole()] * 3,
        out_specs=(whole(),) * 3,
        compiler_params=params(12),
        cost_estimate=cost(
            2 * group_rows * model * width, 2 * model * (2 * group_rows + width)
        ),
        name="project_queries",
    )(*keep_in(HBM, tokens, norm_attn.reshape(1, -1), w_query))

    packed = pl.pallas_call(
        functools.partial(pack_queries, n=n, cap=cap, reqs=reqs, page_len=page_len),
        out_shape=HBM((n * ask_block, LANES), BF16),
        in_specs=[whole(SMEM), whole(SMEM), whole()],
        out_specs=whole(),
        compiler_params=params(8),
        cost_estimate=cost(0, 4 * n * ask_block * LANES),
        name="pack_queries",
    )(codes, *keep_in(HBM, cache_len), turned)
    asked = lax.all_to_all(packed, "req", split_axis=0, concat_axis=0, tiled=True)

    keys, values = pl.pallas_call(
        project_keys,
        out_shape=(HBM((group_rows, width), BF16),) * 2,
        in_specs=[whole()] * 3,
        out_specs=(whole(),) * 2,
        compiler_params=params(12),
        cost_estimate=cost(
            4 * group_rows * model * width, 2 * model * (group_rows + 2 * width)
        ),
        name="project_keys",
    )(*keep_in(HBM, normed, w_key, w_value))

    row_block = pl.BlockSpec((draft, width), lambda r, *_: (r, 0))
    fixed_block = pl.BlockSpec((fixed_count, width), lambda r, *_: (0, 0))
    matrix_block = pl.BlockSpec((1, heads, HD, HD), lambda r, *_: (r, 0, 0, 0))
    span_block = pl.BlockSpec((span, HD), lambda r, *_: (r, 0))
    own, retrieved, own_top, own_sum = pl.pallas_call(
        functools.partial(local_attention, heads=heads, draft=draft, scale=scale),
        grid=(reqs,),
        out_shape=(
            HBM((reqs * span, HD), F32),
            HBM((reqs * span, HD), F32),
            jax.ShapeDtypeStruct((reqs, LANES), F32),
            jax.ShapeDtypeStruct((reqs, LANES), F32),
        ),
        in_specs=[
            row_block,
            row_block,
            row_block,
            fixed_block,
            fixed_block,
            pl.BlockSpec((1, draft, draft), lambda r: (r, 0, 0)),
            matrix_block,
        ],
        out_specs=(span_block, span_block) + (pl.BlockSpec((reqs, LANES), lambda r: (0, 0)),) * 2,
        compiler_params=params(10),
        cost_estimate=cost(
            2 * reqs * span * HD * (2 * (draft + fixed_count) + 6 * HD),
            4 * reqs * (heads * HD * HD + 2 * span * HD),
            reqs * span * (draft + fixed_count),
        ),
        name="local_attention",
    )(*keep_in(HBM, queries, keys, values, persist_keys, persist_values, tree_mask, memory))

    matrices = jax.ShapeDtypeStruct(memory.shape, F32)
    memory_out, momentum_out = pl.pallas_call(
        functools.partial(update_memory, heads=heads, steps=steps),
        grid_spec=pltpu.PrefetchScalarGridSpec(
            num_scalar_prefetch=4,
            grid=(reqs,),
            in_specs=[row_block, row_block, matrix_block, matrix_block],
            out_specs=(matrix_block, matrix_block),
            scratch_shapes=[
                pltpu.VMEM((draft, width), F32),
                pltpu.VMEM((draft, width), F32),
                pltpu.VMEM((LANES, HD), F32),
                pltpu.VMEM((heads * steps, HD), F32),
                pltpu.VMEM((HD, LANES), F32),
            ],
        ),
        out_shape=(matrices, matrices),
        compiler_params=params(10),
        cost_estimate=cost(
            14 * reqs * heads * HD * HD * steps * 8, 16 * reqs * heads * HD * HD
        ),
        name="update_memory",
    )(
        accept_path.reshape(-1),
        accept_len,
        momentum_code.reshape(-1),
        forget_code.reshape(-1),
        *keep_in(HBM, keys, values, memory, momentum),
    )

    asked, memory_out, momentum_out, keys, values = lax.optimization_barrier(
        (asked, memory_out, momentum_out, keys, values)
    )
    answers = pl.pallas_call(
        functools.partial(
            page_attention, n=n, cap=cap, draft=draft, heads=heads, page_len=page_len,
            scale=scale, group=2,
        ),
        out_shape=HBM((n * block, LANES), BF16),
        in_specs=[whole(), whole(HBM)],
        out_specs=whole(HBM),
        scratch_shapes=[
            pltpu.VMEM((n, cap) + kv_cache.shape[1:], BF16),
            pltpu.VMEM((n * block, LANES), BF16),
            pltpu.SemaphoreType.DMA((n,)),
            pltpu.SemaphoreType.DMA((n,)),
        ],
        compiler_params=params(24),
        cost_estimate=cost(
            4 * slots * span * page_len * HD,
            4 * slots * page_len * width + 4 * n * block * LANES,
            slots * span * page_len,
        ),
        name="page_attention",
    )(asked, *keep_in(HBM, kv_cache))
    if pieces == 2:
        down_half, out_half, one_a, _ = lax.optimization_barrier(
            (down_half, out_half, one_a, answers)
        )
    returned = lax.all_to_all(answers, "req", split_axis=0, concat_axis=0, tiled=True)
    if pieces == 2:
        cores = [(i, i ^ 1) for i in range(n)]
        one_d = lax.ppermute(down_half, "grp", swap)
        one_o = lax.ppermute(out_half, "grp", swap)
        two_a = lax.ppermute(one_a, "req", cores)
        returned, one_d, one_o, two_a, own, retrieved, own_top, own_sum = lax.optimization_barrier(
            (returned, one_d, one_o, two_a, own, retrieved, own_top, own_sum)
        )
        two_o = lax.ppermute(one_o, "req", cores)
        two_d = lax.ppermute(one_d, "req", cores)
    rows = group_rows // grp
    mixed = pl.pallas_call(
        functools.partial(
            combine, n=n, cap=cap, reqs=reqs, draft=draft, heads=heads, pieces=pieces
        ),
        out_shape=(jax.ShapeDtypeStruct((group_rows // pieces, width), BF16),) * pieces,
        in_specs=[whole(SMEM)] * 2 + [whole()] + [whole(HBM)] * 2 + [whole()] * 2,
        out_specs=(whole(),) * pieces,
        scratch_shapes=[
            pltpu.VMEM((slots, LANES), F32),
            pltpu.VMEM((slots, LANES), F32),
            pltpu.VMEM((reqs, LANES), F32),
            pltpu.VMEM((reqs, LANES), F32),
            pltpu.VMEM((LANES, LANES), F32),
            pltpu.VMEM((LANES, LANES), F32),
            pltpu.VMEM((reqs * span, HD), F32),
            pltpu.VMEM((group_rows, width), BF16),
            pltpu.VMEM((reqs * span, HD), F32),
            pltpu.VMEM((reqs * span, HD), F32),
            pltpu.SemaphoreType.DMA((2,)),
        ],
        compiler_params=params(12),
        cost_estimate=cost(
            8 * slots * span * HD, 2 * n * block * LANES + 8 * reqs * span * HD
        ),
        name="combine",
    )(codes, side, returned, *keep_in(HBM, own, retrieved), own_top, own_sum)

    if pieces == 2:
        mine, asked_for = mixed
        theirs = lax.ppermute(asked_for, "grp", swap)
        mine, one_a, one_o, two_a, two_o = lax.optimization_barrier(
            (mine, one_a, one_o, two_a, two_o)
        )
        units = w_down.shape[0]
        out_near, gate_up_near, down_near = pl.pallas_call(
            stage_weights,
            out_shape=(
                VMEM((2,) + w_out.shape, BF16),
                VMEM((2,) + w_gate_up.shape, BF16),
                VMEM(w_down.shape, BF16),
            ),
            in_specs=[whole(SMEM)] + [whole(HBM)] * 3 + [whole(pl.ANY)] * 4,
            out_specs=(whole(),) * 3,
            scratch_shapes=[pltpu.SemaphoreType.DMA((7,))],
            compiler_params=params(2),
            cost_estimate=cost(0, 2 * model * (2 * width + 5 * units)),
            name="stage_weights",
        )(side, *keep_in(HBM, w_out, w_gate_up, w_down), one_a, one_o, two_a, two_o)
        residual, hidden = pl.pallas_call(
            feed_up,
            out_shape=(VMEM((rows, model), BF16), VMEM((2, rows, units), BF16)),
            in_specs=[whole(SMEM)] + [whole()] * 6,
            out_specs=(whole(),) * 2,
            compiler_params=params(12),
            cost_estimate=cost(
                4 * rows * model * (width + 2 * units), 4 * model * (width + 2 * units)
            ),
            name="feed_up",
        )(
            side, tokens, mine, theirs, norm_ffn.reshape(1, -1),
            *keep_in(VMEM, out_near, gate_up_near),
        )
        layer_out = pl.pallas_call(
            feed_down,
            out_shape=jax.ShapeDtypeStruct((rows, model), BF16),
            in_specs=[whole(SMEM)] + [whole()] * 3 + [whole(pl.ANY)] * 2,
            out_specs=whole(),
            scratch_shapes=[
                pltpu.VMEM(w_down.shape, BF16),
                pltpu.VMEM((rows, model), F32),
                pltpu.SemaphoreType.DMA((2,)),
            ],
            compiler_params=params(12),
            cost_estimate=cost(4 * rows * model * units, 4 * model * units),
            name="feed_down",
        )(side, *keep_in(VMEM, residual, hidden, down_near), one_d, two_d)
        return (layer_out, memory_out, momentum_out)

    partial_out = jnp.dot(mixed[0], w_out, preferred_element_type=F32).astype(BF16)
    head_sum = lax.psum_scatter(partial_out, "grp", scatter_dimension=0, tiled=True).astype(F32)
    own_rows = lax.dynamic_slice_in_dim(tokens, lax.axis_index("grp") * rows, rows, 0)
    residual = (own_rows.astype(F32) + head_sum).astype(BF16)
    ffn_in = rms_norm(residual, norm_ffn)
    piece = lax.all_gather(ffn_in, "grp", axis=0, tiled=True)
    gate = jnp.dot(piece, w_gate_up[0], preferred_element_type=F32)
    up = jnp.dot(piece, w_gate_up[1], preferred_element_type=F32)
    hidden = (jax.nn.silu(gate) * up).astype(BF16)
    ffn_out = lax.psum_scatter(
        jnp.dot(hidden, w_down, preferred_element_type=F32).astype(BF16),
        "grp",
        scatter_dimension=0,
        tiled=True,
    ).astype(F32)
    layer_out = (residual.astype(F32) + ffn_out).astype(BF16)
    return (layer_out, memory_out, momentum_out)


def solution(mesh):
    return jax.shard_map(
        on_device,
        mesh=mesh,
        in_specs=(
            P("req", None),
            P(),
            P(None, "grp"),
            P(None, "grp"),
            P(None, "grp"),
            P("grp", None),
            P(None, "grp"),
            P(None, "grp"),
            P("req", None, None, "grp"),
            P("req"),
            P("req"),
            P("req"),
            P("req", None, None),
            P("req", None),
            P("req"),
            P("req", "grp", None, None),
            P("req", "grp", None, None),
            P("req", None, "grp"),
            P("req", None, "grp"),
            P(),
            P(None, None, "grp"),
            P("grp", None),
        ),
        out_specs=(
            P(("req", "grp"), None),
            P("req", "grp", None, None),
            P("req", "grp", None, None),
        ),
        check_vma=False,
    )
```

```python
import functools
import math

import jax
import jax.numpy as jnp
from jax import lax
from jax.experimental import pallas as pl
from jax.experimental.pallas import tpu as pltpu
from jax.sharding import PartitionSpec as P

HD = 128
LANES = 128
EXTRA = 16
TOP_PARTS = 3
SUM_PARTS = 2

EPS = 1e-06
THETA = 0.5
NEG = -1e30

VMEM = pltpu.VMEM
SMEM = pltpu.SMEM
HBM = pltpu.HBM
F32 = jnp.float32
BF16 = jnp.bfloat16


def whole(space=VMEM):
    return pl.BlockSpec(memory_space=space)


def cost(flops, moved, special=0):
    return pl.CostEstimate(flops=flops, bytes_accessed=moved, transcendentals=special)


def keep_in(space, *arrays):
    return tuple(pltpu.with_memory_space_constraint(array, space) for array in arrays)


def params(mib=40):
    return pltpu.CompilerParams(vmem_limit_bytes=mib << 20)


def rms_norm(rows, gain):
    values = rows.astype(F32)
    factor = lax.rsqrt(jnp.mean(values * values, axis=-1, keepdims=True) + EPS)
    return (values * factor * gain).astype(BF16)


def nt_dot(left, right):
    return lax.dot_general(left, right, (((1,), (1,)), ((), ())), preferred_element_type=F32)


def column_to_row(column, count):
    row_id = lax.broadcasted_iota(jnp.int32, (count, LANES), 0)
    lane_id = lax.broadcasted_iota(jnp.int32, (count, LANES), 1)
    spread = jnp.where(row_id == lane_id, jnp.broadcast_to(column, (count, LANES)), 0.0)
    return jnp.sum(spread, axis=0, keepdims=True)


def split_parts(row, count):
    parts = []
    for _ in range(count):
        part = row.astype(BF16).astype(F32)
        parts.append(part)
        row = row - part
    return parts


def project_queries(tok_ref, gain_ref, w_ref, normed_ref, q_ref, turned_ref, *, reqs, draft, heads):
    normed_ref[...] = rms_norm(tok_ref[...], gain_ref[...])
    q_ref[...] = jnp.dot(normed_ref[...], w_ref[...], preferred_element_type=F32).astype(BF16)
    span = heads * draft
    for r in range(reqs):
        rows = slice(r * draft, (r + 1) * draft)
        pieces = [q_ref[rows, h * HD : (h + 1) * HD].astype(F32) for h in range(heads)]
        if span < LANES:
            pieces.append(jnp.zeros((LANES - span, HD), F32))
        tile = jnp.concatenate(pieces, axis=0)
        turned_ref[r * HD : (r + 1) * HD, :] = jnp.transpose(tile).astype(BF16)


def project_keys(normed_ref, wk_ref, wv_ref, k_ref, v_ref):
    normed = normed_ref[...]
    k_ref[...] = jnp.dot(normed, wk_ref[...], preferred_element_type=F32).astype(BF16)
    v_ref[...] = jnp.dot(normed, wv_ref[...], preferred_element_type=F32).astype(BF16)


def pack_queries(codes, lengths, turned_ref, out_ref, *, n, cap, reqs, page_len):
    block = cap * HD + EXTRA
    row_id = lax.broadcasted_iota(jnp.int32, (EXTRA, LANES), 0)

    def one(d, carry):
        base = pl.multiple_of(d * block, EXTRA)
        tail = jnp.zeros((EXTRA, LANES), F32)
        for c in range(cap):
            code = codes[d, 0, c]
            r = lax.rem(code, reqs)
            page = lax.div(code, reqs)
            live = jnp.clip(lengths[r] - page * page_len, 0, page_len)
            tail = jnp.where(row_id == c, live.astype(F32), tail)
            rows = pl.ds(pl.multiple_of(r * HD, HD), HD)
            out_ref[pl.ds(base + c * HD, HD), :] = turned_ref[rows, :]
        out_ref[pl.ds(base + cap * HD, EXTRA), :] = tail.astype(BF16)
        return carry

    lax.fori_loop(0, n, one, 0)


def page_attention(
    q_ref, kv_hbm, out_hbm, kv_buf, out_buf, in_sems, out_sems,
    *, n, cap, draft, heads, page_len, scale, group,
):
    span = heads * draft
    ask_block = cap * HD + EXTRA
    block = cap * span + EXTRA
    token = lax.broadcasted_iota(jnp.int32, (page_len, LANES), 0).astype(F32)
    row_id = lax.broadcasted_iota(jnp.int32, (EXTRA, LANES), 0)
    head_of = lax.broadcasted_iota(jnp.int32, (HD, LANES), 1) // draft

    def arrival(d):
        return pltpu.make_async_copy(
            kv_hbm.at[pl.ds(d * cap, cap)], kv_buf.at[d], in_sems.at[d]
        )

    def departure(d):
        rows = pl.ds(pl.multiple_of(d * block, EXTRA), block)
        return pltpu.make_async_copy(out_buf.at[rows], out_hbm.at[rows], out_sems.at[d])

    for d in range(n):
        arrival(d).start()

    def one(i, carry):
        pairs = [(i * group + g, c) for g in range(group) for c in range(cap)]
        limits = []
        for g in range(group):
            d = i * group + g
            arrival(d).wait()
            at = pl.multiple_of(d * ask_block + cap * HD, EXTRA)
            limits.append(q_ref[pl.ds(at, EXTRA), :].astype(F32))
        all_scores = []
        for d, c in pairs:
            at = pl.multiple_of(d * ask_block + c * HD, EXTRA)
            turned = q_ref[pl.ds(at, HD), :]
            blocks = [jnp.where(head_of == h, turned, jnp.zeros_like(turned)) for h in range(heads)]
            all_scores.append(
                jnp.dot(
                    kv_buf[d, c, 0], jnp.concatenate(blocks, axis=0), preferred_element_type=F32
                )
            )
        all_weights = []
        tails = [jnp.zeros((EXTRA, LANES), F32) for _ in range(group)]
        for j, (d, c) in enumerate(pairs):
            g = j // cap
            scores = jnp.where(token < limits[g][c : c + 1, :], all_scores[j] * scale, NEG)
            top = jnp.max(scores, axis=0, keepdims=True)
            weight = jnp.exp(scores - top)
            total = jnp.sum(weight, axis=0, keepdims=True)
            all_weights.append(jnp.transpose(weight).astype(BF16))
            parts = split_parts(top, TOP_PARTS) + split_parts(total, SUM_PARTS)
            for p, part in enumerate(parts):
                tails[g] = jnp.where(row_id == p * cap + c, part, tails[g])
        for j, (d, c) in enumerate(pairs):
            for h in range(heads):
                numer = jnp.dot(
                    all_weights[j][h * draft : (h + 1) * draft, :],
                    kv_buf[d, c, 1, :, h * HD : (h + 1) * HD],
                    preferred_element_type=F32,
                )
                at = pl.multiple_of(d * block + c * span + h * draft, EXTRA)
                out_buf[pl.ds(at, draft), :] = numer.astype(BF16)
        for g in range(group):
            d = i * group + g
            at = pl.multiple_of(d * block + cap * span, EXTRA)
            out_buf[pl.ds(at, EXTRA), :] = tails[g].astype(BF16)
            departure(d).start()
        return carry

    lax.fori_loop(0, n // group, one, 0)
    for d in range(n):
        departure(d).wait()


def local_attention(
    q_ref, k_ref, v_ref, pk_ref, pv_ref, mask_ref, mem_ref,
    o_ref, ret_ref, top_ref, sum_ref, *, heads, draft, scale,
):
    r = pl.program_id(0)
    seen = mask_ref[0] == 1
    tops, totals = [], []
    for h in range(heads):
        cols = slice(h * HD, (h + 1) * HD)
        rows = slice(h * draft, (h + 1) * draft)
        query = q_ref[:, cols]
        tree = jnp.where(seen, nt_dot(query, k_ref[:, cols]) * scale, NEG)
        fixed = nt_dot(query, pk_ref[:, cols]) * scale
        top = jnp.maximum(
            jnp.max(tree, axis=1, keepdims=True), jnp.max(fixed, axis=1, keepdims=True)
        )
        tree_w = jnp.exp(tree - top)
        fixed_w = jnp.exp(fixed - top)
        total = jnp.sum(tree_w, axis=1, keepdims=True) + jnp.sum(fixed_w, axis=1, keepdims=True)
        numer = jnp.dot(tree_w.astype(BF16), v_ref[:, cols], preferred_element_type=F32)
        numer = numer + jnp.dot(fixed_w.astype(BF16), pv_ref[:, cols], preferred_element_type=F32)
        o_ref[rows, :] = numer
        tops.append(top)
        totals.append(total)
        wide = query.astype(F32)
        unit = wide * lax.rsqrt(jnp.sum(wide * wide, axis=1, keepdims=True) + EPS)
        ret_ref[rows, :] = jnp.dot(
            unit, mem_ref[0, h], preferred_element_type=F32, precision=lax.Precision.HIGHEST
        )
    span = heads * draft
    top_ref[pl.ds(r, 1), :] = column_to_row(jnp.concatenate(tops, axis=0), span)
    sum_ref[pl.ds(r, 1), :] = column_to_row(jnp.concatenate(totals, axis=0), span)


def update_memory(
    path, count, mom_code, forget_code, k_ref, v_ref, mem_ref, mom_ref, mem_out, mom_out,
    wide_k, wide_v, unit_ref, value_ref, turned_ref, *, heads, steps,
):
    r = pl.program_id(0)
    wide_k[...] = k_ref[...].astype(F32)
    wide_v[...] = v_ref[...].astype(F32)
    unit_ref[...] = jnp.zeros_like(unit_ref)
    for n in range(steps):
        node = path[r * steps + n]
        k_row = wide_k[pl.ds(node, 1), :]
        v_row = wide_v[pl.ds(node, 1), :]
        for h in range(heads):
            unit_ref[h * steps + n : h * steps + n + 1, :] = k_row[:, h * HD : (h + 1) * HD]
            value_ref[h * steps + n : h * steps + n + 1, :] = v_row[:, h * HD : (h + 1) * HD]
    keys = unit_ref[...]
    unit = keys * lax.rsqrt(jnp.sum(keys * keys, axis=1, keepdims=True) + EPS)
    turned_ref[...] = jnp.transpose(unit)

    def advance(n, mem_src, mom_src):
        for h in range(heads):
            at = (r * steps + n) * heads + h
            eta = 0.97 - 0.06 * mom_code[at].astype(F32)
            keep = 1.0 - (0.01 + 0.02 * forget_code[at].astype(F32))
            row = h * steps + n
            column = turned_ref[:, row : row + 1]
            matrix = mem_src[0, h]
            predicted = jnp.sum(column * matrix, axis=0, keepdims=True)
            error = THETA * (predicted - value_ref[row : row + 1, :])
            moved = eta * mom_src[0, h] - column * error
            mom_out[0, h] = moved
            mem_out[0, h] = keep * matrix + moved

    advance(0, mem_ref, mom_ref)
    for n in range(1, steps):
        pl.when(n < count[r])(functools.partial(advance, n, mem_out, mom_out))


def combine(
    codes, side, msg_ref, o_hbm, ret_hbm, own_top_ref, own_sum_ref, *rest,
    n, cap, reqs, draft, heads, pieces,
):
    outs = rest[:pieces]
    part_top, part_sum, best, total, weight, own_weight, acc, mixed, o_ref, ret_ref, sems = rest[
        pieces:
    ]
    copies = [
        pltpu.make_async_copy(o_hbm, o_ref, sems.at[0]),
        pltpu.make_async_copy(ret_hbm, ret_ref, sems.at[1]),
    ]
    for copy in copies:
        copy.start()
    span = heads * draft
    block = cap * span + EXTRA
    slots = n * cap
    for d in range(n):
        at = d * block + cap * span
        tail = msg_ref[at : at + EXTRA, :].astype(F32)
        rows = [tail[p * cap : (p + 1) * cap] for p in range(TOP_PARTS + SUM_PARTS)]
        part_top[d * cap : (d + 1) * cap, :] = rows[0] + rows[1] + rows[2]
        part_sum[d * cap : (d + 1) * cap, :] = rows[3] + rows[4]
    best[...] = own_top_ref[...]
    owners = [lax.rem(codes[s // cap, 0, s % cap], reqs) for s in range(slots)]
    for s in range(slots):
        r = owners[s]
        best[pl.ds(r, 1), :] = jnp.maximum(best[pl.ds(r, 1), :], part_top[s : s + 1, :])
    own_weight[...] = jnp.zeros_like(own_weight)
    weight[...] = jnp.zeros_like(weight)
    start = jnp.exp(own_top_ref[...] - best[...])
    total[...] = start * own_sum_ref[...]
    for s in range(slots):
        r = owners[s]
        term = jnp.exp(part_top[s : s + 1, :] - best[pl.ds(r, 1), :])
        weight[s : s + 1, :] = term
        total[pl.ds(r, 1), :] = total[pl.ds(r, 1), :] + term * part_sum[s : s + 1, :]
    inverse = 1.0 / total[...]
    own_weight[0:reqs, :] = start * inverse
    total[...] = inverse
    for s in range(slots):
        weight[s : s + 1, :] = weight[s : s + 1, :] * total[pl.ds(owners[s], 1), :]
    turned = jnp.transpose(weight[...])
    own_turned = jnp.transpose(own_weight[...])
    for copy in copies:
        copy.wait()
    for r in range(reqs):
        rows = slice(r * span, (r + 1) * span)
        acc[rows, :] = o_ref[rows, :] * own_turned[0:span, r : r + 1] + ret_ref[rows, :]
    for s in range(slots):
        at = (s // cap) * block + (s % cap) * span
        rows = pl.ds(pl.multiple_of(owners[s] * span, span), span)
        acc[rows, :] = acc[rows, :] + msg_ref[at : at + span, :].astype(F32) * turned[
            0:span, s : s + 1
        ]
    for r in range(reqs):
        for h in range(heads):
            at = r * span + h * draft
            mixed[r * draft : (r + 1) * draft, h * HD : (h + 1) * HD] = acc[
                at : at + draft, :
            ].astype(BF16)
    rows = reqs * draft // pieces
    for p, out_ref in enumerate(outs):
        first = lax.rem(side[0] + p, pieces) * rows
        out_ref[...] = mixed[pl.ds(pl.multiple_of(first, rows), rows), :]


def run_copies(pairs, sems):
    copies = [
        pltpu.make_async_copy(source, target, sems.at[i])
        for i, (source, target) in enumerate(pairs)
    ]
    for copy in copies:
        copy.start()
    return copies


def cut_weights(side, gate_up_w, down_w, out_w, first_ref, last_ref, quarter_ref, sems, *, first):
    last = gate_up_w.shape[1] - first
    depth, width = down_w.shape[0] // 4, out_w.shape[0] // 4
    half = gate_up_w.at[side[1]]
    pairs = [
        (half.at[pl.ds(0, first)], first_ref),
        (half.at[pl.ds(first, last)], last_ref),
        (
            down_w.at[pl.ds(pl.multiple_of(side[2] * depth, EXTRA), depth)],
            quarter_ref.at[pl.ds(0, depth)],
        ),
        (
            out_w.at[pl.ds(pl.multiple_of(side[2] * width, EXTRA), width)],
            quarter_ref.at[pl.ds(depth, width)],
        ),
    ]
    for copy in run_copies(pairs, sems):
        copy.wait()


def stage_weights(
    side, out_w, gate_up_w, down_w, one_a, one_b, one_q, two_a, two_b, two_q, three_q, four_q,
    out_all, gate_up_all, down_all, sems,
):
    width, depth = out_w.shape[0] // 4, down_w.shape[0] // 4
    first, last = one_a.shape[0], one_b.shape[0]
    pairs = [(gate_up_w, gate_up_all.at[0]), (down_w, down_all.at[0]), (out_w, out_all.at[0])]
    for half, a, b in ((side[1], one_a, one_b), (1 - side[1], two_a, two_b)):
        target = gate_up_all.at[1, half]
        pairs.append((a, target.at[pl.ds(0, first)]))
        pairs.append((b, target.at[pl.ds(first, last)]))
    core, chip = side[1], side[2] // 2
    for x, y, q in ((core, chip, one_q), (1 - core, chip, two_q), (core, 1 - chip, three_q), (
        1 - core, 1 - chip, four_q,
    )):
        part = 2 * y + x
        units = pl.ds(pl.multiple_of(part * depth, EXTRA), depth)
        rows = pl.ds(pl.multiple_of(part * width, EXTRA), width)
        pairs.append((q.at[pl.ds(0, depth)], down_all.at[1, units]))
        pairs.append((q.at[pl.ds(depth, width)], out_all.at[1, rows]))
    for copy in run_copies(pairs, sems):
        copy.wait()


def feed_up(
    side, tok_ref, mine_ref, theirs_ref, gain_ref, out_w, gate_up_w, residual_ref, hidden_ref
):
    rows = mine_ref.shape[0]
    units = gate_up_w.shape[3]
    tokens = tok_ref[pl.ds(pl.multiple_of(side[0] * rows, rows), rows), :].astype(F32)
    summed = tokens + jnp.dot(mine_ref[...], out_w[0], preferred_element_type=F32)
    summed = summed + jnp.dot(theirs_ref[...], out_w[1], preferred_element_type=F32)
    residual_ref[...] = summed.astype(BF16)
    ffn_in = rms_norm(residual_ref[...], gain_ref[...])
    step = 256
    for half in range(2):
        for first in range(0, units, step):
            cols = slice(first, min(first + step, units))
            gate = jnp.dot(ffn_in, gate_up_w[half, 0, :, cols], preferred_element_type=F32)
            up = jnp.dot(ffn_in, gate_up_w[half, 1, :, cols], preferred_element_type=F32)
            hidden_ref[half, :, cols] = (gate / (1.0 + jnp.exp(-gate)) * up).astype(BF16)


def feed_down(residual_ref, hidden_ref, down_w, out_ref):
    step = 256
    for at in range(0, out_ref.shape[1], step):
        cols = slice(at, at + step)
        total = residual_ref[:, cols].astype(F32)
        for half in range(2):
            total = total + jnp.dot(
                hidden_ref[half], down_w[half, :, cols], preferred_element_type=F32
            )
        out_ref[:, cols] = total.astype(BF16)


def on_device(
    tokens,
    norm_attn,
    w_query,
    w_key,
    w_value,
    w_out,
    persist_keys,
    persist_values,
    kv_cache,
    slot_request,
    slot_page,
    cache_len,
    tree_mask,
    accept_path,
    accept_len,
    memory,
    momentum,
    momentum_code,
    forget_code,
    norm_ffn,
    w_gate_up,
    w_down,
):
    n = lax.axis_size("req")
    group_rows, model = tokens.shape
    reqs = cache_len.shape[0]
    draft = tree_mask.shape[1]
    steps = accept_path.shape[1]
    width = w_query.shape[1]
    heads = width // HD
    span = heads * draft
    slots = kv_cache.shape[0]
    cap = slots // n
    fixed_count = persist_keys.shape[0]
    page_len = kv_cache.shape[2]
    ask_block = cap * HD + EXTRA
    block = cap * span + EXTRA
    scale = 1.0 / math.sqrt(HD)

    label = (slot_page * reqs + lax.rem(slot_request, reqs)).reshape(n, 1, cap)
    codes = lax.all_to_all(label, "req", split_axis=0, concat_axis=0, tiled=True)

    grp = lax.axis_size("grp")
    depth, out_depth = w_down.shape[0] // 4, width // 4
    first = model * 10 // 32
    split = (depth, out_depth, first)
    pieces = 2 if grp == 2 and n % 4 == 0 and not any(size % EXTRA for size in split) else 1
    quarter = lax.rem(lax.axis_index("req"), 4)
    core = lax.rem(quarter, 2)
    side = jnp.stack([lax.axis_index("grp"), core, quarter]).astype(jnp.int32)
    if pieces == 2:
        half_first, half_last, quarters = pl.pallas_call(
            functools.partial(cut_weights, first=first),
            out_shape=(
                HBM((first, w_down.shape[0]), BF16),
                HBM((model - first, w_down.shape[0]), BF16),
                HBM((depth + out_depth, model), BF16),
            ),
            in_specs=[whole(SMEM)] + [whole(HBM)] * 3,
            out_specs=(whole(HBM),) * 3,
            scratch_shapes=[pltpu.SemaphoreType.DMA((4,))],
            compiler_params=params(2),
            cost_estimate=cost(0, 4 * model * (w_down.shape[0] + depth + out_depth)),
            name="cut_weights",
        )(side, *keep_in(HBM, w_gate_up, w_down, w_out))

    normed, queries, turned = pl.pallas_call(
        functools.partial(project_queries, reqs=reqs, draft=draft, heads=heads),
        out_shape=(
            HBM((group_rows, model), BF16),
            HBM((group_rows, width), BF16),
            jax.ShapeDtypeStruct((reqs * HD, LANES), BF16),
        ),
        in_specs=[whole()] * 3,
        out_specs=(whole(),) * 3,
        compiler_params=params(12),
        cost_estimate=cost(
            2 * group_rows * model * width, 2 * model * (2 * group_rows + width)
        ),
        name="project_queries",
    )(*keep_in(HBM, tokens, norm_attn.reshape(1, -1), w_query))

    if pieces == 2:
        turned, half_first, half_last, quarters = lax.optimization_barrier(
            (turned, half_first, half_last, quarters)
        )
        swap = [(0, 1), (1, 0)]
        one_a = lax.ppermute(half_first, "grp", swap)
        one_q = lax.ppermute(quarters, "grp", swap)

    packed = pl.pallas_call(
        functools.partial(pack_queries, n=n, cap=cap, reqs=reqs, page_len=page_len),
        out_shape=HBM((n * ask_block, LANES), BF16),
        in_specs=[whole(SMEM), whole(SMEM), whole()],
        out_specs=whole(),
        compiler_params=params(8),
        cost_estimate=cost(0, 4 * n * ask_block * LANES),
        name="pack_queries",
    )(codes, *keep_in(HBM, cache_len), turned)
    asked = lax.all_to_all(packed, "req", split_axis=0, concat_axis=0, tiled=True)

    keys, values = pl.pallas_call(
        project_keys,
        out_shape=(HBM((group_rows, width), BF16),) * 2,
        in_specs=[whole()] * 3,
        out_specs=(whole(),) * 2,
        compiler_params=params(12),
        cost_estimate=cost(
            4 * group_rows * model * width, 2 * model * (group_rows + 2 * width)
        ),
        name="project_keys",
    )(*keep_in(HBM, normed, w_key, w_value))

    row_block = pl.BlockSpec((draft, width), lambda r, *_: (r, 0))
    fixed_block = pl.BlockSpec((fixed_count, width), lambda r, *_: (0, 0))
    matrix_block = pl.BlockSpec((1, heads, HD, HD), lambda r, *_: (r, 0, 0, 0))
    span_block = pl.BlockSpec((span, HD), lambda r, *_: (r, 0))
    own, retrieved, own_top, own_sum = pl.pallas_call(
        functools.partial(local_attention, heads=heads, draft=draft, scale=scale),
        grid=(reqs,),
        out_shape=(
            HBM((reqs * span, HD), F32),
            HBM((reqs * span, HD), F32),
            jax.ShapeDtypeStruct((reqs, LANES), F32),
            jax.ShapeDtypeStruct((reqs, LANES), F32),
        ),
        in_specs=[
            row_block,
            row_block,
            row_block,
            fixed_block,
            fixed_block,
            pl.BlockSpec((1, draft, draft), lambda r: (r, 0, 0)),
            matrix_block,
        ],
        out_specs=(span_block, span_block) + (pl.BlockSpec((reqs, LANES), lambda r: (0, 0)),) * 2,
        compiler_params=params(10),
        cost_estimate=cost(
            2 * reqs * span * HD * (2 * (draft + fixed_count) + 6 * HD),
            4 * reqs * (heads * HD * HD + 2 * span * HD),
            reqs * span * (draft + fixed_count),
        ),
        name="local_attention",
    )(*keep_in(HBM, queries, keys, values, persist_keys, persist_values, tree_mask, memory))

    matrices = jax.ShapeDtypeStruct(memory.shape, F32)
    memory_out, momentum_out = pl.pallas_call(
        functools.partial(update_memory, heads=heads, steps=steps),
        grid_spec=pltpu.PrefetchScalarGridSpec(
            num_scalar_prefetch=4,
            grid=(reqs,),
            in_specs=[row_block, row_block, matrix_block, matrix_block],
            out_specs=(matrix_block, matrix_block),
            scratch_shapes=[
                pltpu.VMEM((draft, width), F32),
                pltpu.VMEM((draft, width), F32),
                pltpu.VMEM((LANES, HD), F32),
                pltpu.VMEM((heads * steps, HD), F32),
                pltpu.VMEM((HD, LANES), F32),
            ],
        ),
        out_shape=(matrices, matrices),
        compiler_params=params(10),
        cost_estimate=cost(
            14 * reqs * heads * HD * HD * steps * 8, 16 * reqs * heads * HD * HD
        ),
        name="update_memory",
    )(
        accept_path.reshape(-1),
        accept_len,
        momentum_code.reshape(-1),
        forget_code.reshape(-1),
        *keep_in(HBM, keys, values, memory, momentum),
    )

    asked, memory_out, momentum_out, keys, values = lax.optimization_barrier(
        (asked, memory_out, momentum_out, keys, values)
    )
    answers = pl.pallas_call(
        functools.partial(
            page_attention, n=n, cap=cap, draft=draft, heads=heads, page_len=page_len,
            scale=scale, group=2,
        ),
        out_shape=HBM((n * block, LANES), BF16),
        in_specs=[whole(), whole(HBM)],
        out_specs=whole(HBM),
        scratch_shapes=[
            pltpu.VMEM((n, cap) + kv_cache.shape[1:], BF16),
            pltpu.VMEM((n * block, LANES), BF16),
            pltpu.SemaphoreType.DMA((n,)),
            pltpu.SemaphoreType.DMA((n,)),
        ],
        compiler_params=params(24),
        cost_estimate=cost(
            4 * slots * span * page_len * HD,
            4 * slots * page_len * width + 4 * n * block * LANES,
            slots * span * page_len,
        ),
        name="page_attention",
    )(asked, *keep_in(HBM, kv_cache))
    if pieces == 2:
        answers, half_last, one_a, one_q = lax.optimization_barrier(
            (answers, half_last, one_a, one_q)
        )
    returned = lax.all_to_all(answers, "req", split_axis=0, concat_axis=0, tiled=True)
    if pieces == 2:
        other_core = [(i, i ^ 1) for i in range(n)]
        other_chip = [(i, i ^ 2) for i in range(n)]
        one_b = lax.ppermute(half_last, "grp", swap)
        three_q = lax.ppermute(one_q, "req", other_chip)
        two_a = lax.ppermute(one_a, "req", other_core)
        two_q = lax.ppermute(one_q, "req", other_core)
        returned, one_b, two_a, two_q, three_q, own, retrieved, own_top, own_sum = (
            lax.optimization_barrier(
                (returned, one_b, two_a, two_q, three_q, own, retrieved, own_top, own_sum)
            )
        )
        two_b = lax.ppermute(one_b, "req", other_core)
        four_q = lax.ppermute(three_q, "req", other_core)
    rows = group_rows // grp
    mixed = pl.pallas_call(
        functools.partial(
            combine, n=n, cap=cap, reqs=reqs, draft=draft, heads=heads, pieces=pieces
        ),
        out_shape=(jax.ShapeDtypeStruct((group_rows // pieces, width), BF16),) * pieces,
        in_specs=[whole(SMEM)] * 2 + [whole()] + [whole(HBM)] * 2 + [whole()] * 2,
        out_specs=(whole(),) * pieces,
        scratch_shapes=[
            pltpu.VMEM((slots, LANES), F32),
            pltpu.VMEM((slots, LANES), F32),
            pltpu.VMEM((reqs, LANES), F32),
            pltpu.VMEM((reqs, LANES), F32),
            pltpu.VMEM((LANES, LANES), F32),
            pltpu.VMEM((LANES, LANES), F32),
            pltpu.VMEM((reqs * span, HD), F32),
            pltpu.VMEM((group_rows, width), BF16),
            pltpu.VMEM((reqs * span, HD), F32),
            pltpu.VMEM((reqs * span, HD), F32),
            pltpu.SemaphoreType.DMA((2,)),
        ],
        compiler_params=params(12),
        cost_estimate=cost(
            8 * slots * span * HD, 2 * n * block * LANES + 8 * reqs * span * HD
        ),
        name="combine",
    )(codes, side, returned, *keep_in(HBM, own, retrieved), own_top, own_sum)

    if pieces == 2:
        mine, asked_for = mixed
        theirs = lax.ppermute(asked_for, "grp", swap)
        mine, two_a, two_b, two_q, four_q = lax.optimization_barrier(
            (mine, two_a, two_b, two_q, four_q)
        )
        units = w_down.shape[0]
        out_near, gate_up_near, down_near = pl.pallas_call(
            stage_weights,
            out_shape=(
                VMEM((2,) + w_out.shape, BF16),
                VMEM((2,) + w_gate_up.shape, BF16),
                VMEM((2,) + w_down.shape, BF16),
            ),
            in_specs=[whole(SMEM)] + [whole(pl.ANY)] * 11,
            out_specs=(whole(),) * 3,
            scratch_shapes=[pltpu.SemaphoreType.DMA((15,))],
            compiler_params=params(2),
            cost_estimate=cost(0, 2 * model * (2 * width + 6 * units)),
            name="stage_weights",
        )(
            side,
            *keep_in(HBM, w_out, w_gate_up, w_down, one_a, one_b, one_q, two_a),
            two_b,
            *keep_in(HBM, two_q, three_q),
            four_q,
        )
        residual, hidden = pl.pallas_call(
            feed_up,
            out_shape=(VMEM((rows, model), BF16), VMEM((2, rows, units), BF16)),
            in_specs=[whole(SMEM)] + [whole()] * 6,
            out_specs=(whole(),) * 2,
            compiler_params=params(12),
            cost_estimate=cost(
                4 * rows * model * (width + 2 * units), 4 * model * (width + 2 * units)
            ),
            name="feed_up",
        )(
            side, tokens, mine, theirs, norm_ffn.reshape(1, -1),
            *keep_in(VMEM, out_near, gate_up_near),
        )
        layer_out = pl.pallas_call(
            feed_down,
            out_shape=jax.ShapeDtypeStruct((rows, model), BF16),
            in_specs=[whole()] * 3,
            out_specs=whole(),
            compiler_params=params(6),
            cost_estimate=cost(4 * rows * model * units, 4 * model * units),
            name="feed_down",
        )(*keep_in(VMEM, residual, hidden, down_near))
        return (layer_out, memory_out, momentum_out)

    partial_out = jnp.dot(mixed[0], w_out, preferred_element_type=F32).astype(BF16)
    head_sum = lax.psum_scatter(partial_out, "grp", scatter_dimension=0, tiled=True).astype(F32)
    own_rows = lax.dynamic_slice_in_dim(tokens, lax.axis_index("grp") * rows, rows, 0)
    residual = (own_rows.astype(F32) + head_sum).astype(BF16)
    ffn_in = rms_norm(residual, norm_ffn)
    piece = lax.all_gather(ffn_in, "grp", axis=0, tiled=True)
    gate = jnp.dot(piece, w_gate_up[0], preferred_element_type=F32)
    up = jnp.dot(piece, w_gate_up[1], preferred_element_type=F32)
    hidden = (jax.nn.silu(gate) * up).astype(BF16)
    ffn_out = lax.psum_scatter(
        jnp.dot(hidden, w_down, preferred_element_type=F32).astype(BF16),
        "grp",
        scatter_dimension=0,
        tiled=True,
    ).astype(F32)
    layer_out = (residual.astype(F32) + ffn_out).astype(BF16)
    return (layer_out, memory_out, momentum_out)


def solution(mesh):
    return jax.shard_map(
        on_device,
        mesh=mesh,
        in_specs=(
            P("req", None),
            P(),
            P(None, "grp"),
            P(None, "grp"),
            P(None, "grp"),
            P("grp", None),
            P(None, "grp"),
            P(None, "grp"),
            P("req", None, None, "grp"),
            P("req"),
            P("req"),
            P("req"),
            P("req", None, None),
            P("req", None),
            P("req"),
            P("req", "grp", None, None),
            P("req", "grp", None, None),
            P("req", None, "grp"),
            P("req", None, "grp"),
            P(),
            P(None, None, "grp"),
            P("grp", None),
        ),
        out_specs=(
            P(("req", "grp"), None),
            P("req", "grp", None, None),
            P("req", "grp", None, None),
        ),
        check_vma=False,
    )
```

```python
import functools
import math

import jax
import jax.numpy as jnp
from jax import lax
from jax.experimental import pallas as pl
from jax.experimental.pallas import tpu as pltpu
from jax.sharding import PartitionSpec as P

HD = 128
LANES = 128
EXTRA = 16
TOP_PARTS = 3
SUM_PARTS = 2

EPS = 1e-06
THETA = 0.5
NEG = -1e30

VMEM = pltpu.VMEM
SMEM = pltpu.SMEM
HBM = pltpu.HBM
F32 = jnp.float32
BF16 = jnp.bfloat16


def whole(space=VMEM):
    return pl.BlockSpec(memory_space=space)


def cost(flops, moved, special=0):
    return pl.CostEstimate(flops=flops, bytes_accessed=moved, transcendentals=special)


def keep_in(space, *arrays):
    return tuple(pltpu.with_memory_space_constraint(array, space) for array in arrays)


def params(mib=40):
    return pltpu.CompilerParams(vmem_limit_bytes=mib << 20)


def rms_norm(rows, gain):
    values = rows.astype(F32)
    factor = lax.rsqrt(jnp.mean(values * values, axis=-1, keepdims=True) + EPS)
    return (values * factor * gain).astype(BF16)


def nt_dot(left, right):
    return lax.dot_general(left, right, (((1,), (1,)), ((), ())), preferred_element_type=F32)


def column_to_row(column, count):
    row_id = lax.broadcasted_iota(jnp.int32, (count, LANES), 0)
    lane_id = lax.broadcasted_iota(jnp.int32, (count, LANES), 1)
    spread = jnp.where(row_id == lane_id, jnp.broadcast_to(column, (count, LANES)), 0.0)
    return jnp.sum(spread, axis=0, keepdims=True)


def split_parts(row, count):
    parts = []
    for _ in range(count):
        part = row.astype(BF16).astype(F32)
        parts.append(part)
        row = row - part
    return parts


def project_queries(tok_ref, gain_ref, w_ref, normed_ref, q_ref, turned_ref, *, reqs, draft, heads):
    normed_ref[...] = rms_norm(tok_ref[...], gain_ref[...])
    q_ref[...] = jnp.dot(normed_ref[...], w_ref[...], preferred_element_type=F32).astype(BF16)
    span = heads * draft
    for r in range(reqs):
        rows = slice(r * draft, (r + 1) * draft)
        pieces = [q_ref[rows, h * HD : (h + 1) * HD].astype(F32) for h in range(heads)]
        if span < LANES:
            pieces.append(jnp.zeros((LANES - span, HD), F32))
        tile = jnp.concatenate(pieces, axis=0)
        turned_ref[r * HD : (r + 1) * HD, :] = jnp.transpose(tile).astype(BF16)


def project_keys(normed_ref, wk_ref, wv_ref, k_ref, v_ref):
    normed = normed_ref[...]
    k_ref[...] = jnp.dot(normed, wk_ref[...], preferred_element_type=F32).astype(BF16)
    v_ref[...] = jnp.dot(normed, wv_ref[...], preferred_element_type=F32).astype(BF16)


def pack_queries(codes, lengths, turned_ref, out_ref, *, n, cap, reqs, page_len):
    block = cap * HD + EXTRA
    row_id = lax.broadcasted_iota(jnp.int32, (EXTRA, LANES), 0)

    def one(d, carry):
        base = pl.multiple_of(d * block, EXTRA)
        tail = jnp.zeros((EXTRA, LANES), F32)
        for c in range(cap):
            code = codes[d, 0, c]
            r = lax.rem(code, reqs)
            page = lax.div(code, reqs)
            live = jnp.clip(lengths[r] - page * page_len, 0, page_len)
            tail = jnp.where(row_id == c, live.astype(F32), tail)
            rows = pl.ds(pl.multiple_of(r * HD, HD), HD)
            out_ref[pl.ds(base + c * HD, HD), :] = turned_ref[rows, :]
        out_ref[pl.ds(base + cap * HD, EXTRA), :] = tail.astype(BF16)
        return carry

    lax.fori_loop(0, n, one, 0)


def page_attention(
    q_ref, kv_hbm, out_hbm, kv_buf, out_buf, in_sems, out_sems,
    *, n, cap, draft, heads, page_len, scale, group,
):
    span = heads * draft
    ask_block = cap * HD + EXTRA
    block = cap * span + EXTRA
    token = lax.broadcasted_iota(jnp.int32, (page_len, LANES), 0).astype(F32)
    row_id = lax.broadcasted_iota(jnp.int32, (EXTRA, LANES), 0)
    head_of = lax.broadcasted_iota(jnp.int32, (HD, LANES), 1) // draft

    def arrival(d):
        return pltpu.make_async_copy(
            kv_hbm.at[pl.ds(d * cap, cap)], kv_buf.at[d], in_sems.at[d]
        )

    def departure(d):
        rows = pl.ds(pl.multiple_of(d * block, EXTRA), block)
        return pltpu.make_async_copy(out_buf.at[rows], out_hbm.at[rows], out_sems.at[d])

    for d in range(n):
        arrival(d).start()

    def one(i, carry):
        pairs = [(i * group + g, c) for g in range(group) for c in range(cap)]
        limits = []
        for g in range(group):
            d = i * group + g
            arrival(d).wait()
            at = pl.multiple_of(d * ask_block + cap * HD, EXTRA)
            limits.append(q_ref[pl.ds(at, EXTRA), :].astype(F32))
        all_scores = []
        for d, c in pairs:
            at = pl.multiple_of(d * ask_block + c * HD, EXTRA)
            turned = q_ref[pl.ds(at, HD), :]
            blocks = [jnp.where(head_of == h, turned, jnp.zeros_like(turned)) for h in range(heads)]
            all_scores.append(
                jnp.dot(
                    kv_buf[d, c, 0], jnp.concatenate(blocks, axis=0), preferred_element_type=F32
                )
            )
        all_weights = []
        tails = [jnp.zeros((EXTRA, LANES), F32) for _ in range(group)]
        for j, (d, c) in enumerate(pairs):
            g = j // cap
            scores = jnp.where(token < limits[g][c : c + 1, :], all_scores[j] * scale, NEG)
            top = jnp.max(scores, axis=0, keepdims=True)
            weight = jnp.exp(scores - top)
            total = jnp.sum(weight, axis=0, keepdims=True)
            all_weights.append(jnp.transpose(weight).astype(BF16))
            parts = split_parts(top, TOP_PARTS) + split_parts(total, SUM_PARTS)
            for p, part in enumerate(parts):
                tails[g] = jnp.where(row_id == p * cap + c, part, tails[g])
        for j, (d, c) in enumerate(pairs):
            for h in range(heads):
                numer = jnp.dot(
                    all_weights[j][h * draft : (h + 1) * draft, :],
                    kv_buf[d, c, 1, :, h * HD : (h + 1) * HD],
                    preferred_element_type=F32,
                )
                at = pl.multiple_of(d * block + c * span + h * draft, EXTRA)
                out_buf[pl.ds(at, draft), :] = numer.astype(BF16)
        for g in range(group):
            d = i * group + g
            at = pl.multiple_of(d * block + cap * span, EXTRA)
            out_buf[pl.ds(at, EXTRA), :] = tails[g].astype(BF16)
            departure(d).start()
        return carry

    lax.fori_loop(0, n // group, one, 0)
    for d in range(n):
        departure(d).wait()


def local_attention(
    q_ref, k_ref, v_ref, pk_ref, pv_ref, mask_ref, mem_ref,
    o_ref, ret_ref, top_ref, sum_ref, *, heads, draft, scale,
):
    r = pl.program_id(0)
    seen = mask_ref[0] == 1
    tops, totals = [], []
    for h in range(heads):
        cols = slice(h * HD, (h + 1) * HD)
        rows = slice(h * draft, (h + 1) * draft)
        query = q_ref[:, cols]
        tree = jnp.where(seen, nt_dot(query, k_ref[:, cols]) * scale, NEG)
        fixed = nt_dot(query, pk_ref[:, cols]) * scale
        top = jnp.maximum(
            jnp.max(tree, axis=1, keepdims=True), jnp.max(fixed, axis=1, keepdims=True)
        )
        tree_w = jnp.exp(tree - top)
        fixed_w = jnp.exp(fixed - top)
        total = jnp.sum(tree_w, axis=1, keepdims=True) + jnp.sum(fixed_w, axis=1, keepdims=True)
        numer = jnp.dot(tree_w.astype(BF16), v_ref[:, cols], preferred_element_type=F32)
        numer = numer + jnp.dot(fixed_w.astype(BF16), pv_ref[:, cols], preferred_element_type=F32)
        o_ref[rows, :] = numer
        tops.append(top)
        totals.append(total)
        wide = query.astype(F32)
        unit = wide * lax.rsqrt(jnp.sum(wide * wide, axis=1, keepdims=True) + EPS)
        ret_ref[rows, :] = jnp.dot(
            unit, mem_ref[0, h], preferred_element_type=F32, precision=lax.Precision.HIGHEST
        )
    span = heads * draft
    top_ref[pl.ds(r, 1), :] = column_to_row(jnp.concatenate(tops, axis=0), span)
    sum_ref[pl.ds(r, 1), :] = column_to_row(jnp.concatenate(totals, axis=0), span)


def update_memory(
    path, count, mom_code, forget_code, k_ref, v_ref, mem_ref, mom_ref, mem_out, mom_out,
    wide_k, wide_v, unit_ref, value_ref, turned_ref, *, heads, steps,
):
    r = pl.program_id(0)
    wide_k[...] = k_ref[...].astype(F32)
    wide_v[...] = v_ref[...].astype(F32)
    unit_ref[...] = jnp.zeros_like(unit_ref)
    for n in range(steps):
        node = path[r * steps + n]
        k_row = wide_k[pl.ds(node, 1), :]
        v_row = wide_v[pl.ds(node, 1), :]
        for h in range(heads):
            unit_ref[h * steps + n : h * steps + n + 1, :] = k_row[:, h * HD : (h + 1) * HD]
            value_ref[h * steps + n : h * steps + n + 1, :] = v_row[:, h * HD : (h + 1) * HD]
    keys = unit_ref[...]
    unit = keys * lax.rsqrt(jnp.sum(keys * keys, axis=1, keepdims=True) + EPS)
    turned_ref[...] = jnp.transpose(unit)

    def advance(n, mem_src, mom_src):
        for h in range(heads):
            at = (r * steps + n) * heads + h
            eta = 0.97 - 0.06 * mom_code[at].astype(F32)
            keep = 1.0 - (0.01 + 0.02 * forget_code[at].astype(F32))
            row = h * steps + n
            column = turned_ref[:, row : row + 1]
            matrix = mem_src[0, h]
            predicted = jnp.sum(column * matrix, axis=0, keepdims=True)
            error = THETA * (predicted - value_ref[row : row + 1, :])
            moved = eta * mom_src[0, h] - column * error
            mom_out[0, h] = moved
            mem_out[0, h] = keep * matrix + moved

    advance(0, mem_ref, mom_ref)
    for n in range(1, steps):
        pl.when(n < count[r])(functools.partial(advance, n, mem_out, mom_out))


def combine(
    codes, side, msg_ref, o_hbm, ret_hbm, own_top_ref, own_sum_ref, *rest,
    n, cap, reqs, draft, heads, pieces,
):
    outs = rest[:pieces]
    part_top, part_sum, best, total, weight, own_weight, acc, mixed, o_ref, ret_ref, sems = rest[
        pieces:
    ]
    copies = [
        pltpu.make_async_copy(o_hbm, o_ref, sems.at[0]),
        pltpu.make_async_copy(ret_hbm, ret_ref, sems.at[1]),
    ]
    for copy in copies:
        copy.start()
    span = heads * draft
    block = cap * span + EXTRA
    slots = n * cap
    for d in range(n):
        at = d * block + cap * span
        tail = msg_ref[at : at + EXTRA, :].astype(F32)
        rows = [tail[p * cap : (p + 1) * cap] for p in range(TOP_PARTS + SUM_PARTS)]
        part_top[d * cap : (d + 1) * cap, :] = rows[0] + rows[1] + rows[2]
        part_sum[d * cap : (d + 1) * cap, :] = rows[3] + rows[4]
    best[...] = own_top_ref[...]
    owners = [lax.rem(codes[s // cap, 0, s % cap], reqs) for s in range(slots)]
    for s in range(slots):
        r = owners[s]
        best[pl.ds(r, 1), :] = jnp.maximum(best[pl.ds(r, 1), :], part_top[s : s + 1, :])
    own_weight[...] = jnp.zeros_like(own_weight)
    weight[...] = jnp.zeros_like(weight)
    start = jnp.exp(own_top_ref[...] - best[...])
    total[...] = start * own_sum_ref[...]
    for s in range(slots):
        r = owners[s]
        term = jnp.exp(part_top[s : s + 1, :] - best[pl.ds(r, 1), :])
        weight[s : s + 1, :] = term
        total[pl.ds(r, 1), :] = total[pl.ds(r, 1), :] + term * part_sum[s : s + 1, :]
    inverse = 1.0 / total[...]
    own_weight[0:reqs, :] = start * inverse
    total[...] = inverse
    for s in range(slots):
        weight[s : s + 1, :] = weight[s : s + 1, :] * total[pl.ds(owners[s], 1), :]
    turned = jnp.transpose(weight[...])
    own_turned = jnp.transpose(own_weight[...])
    for copy in copies:
        copy.wait()
    for r in range(reqs):
        rows = slice(r * span, (r + 1) * span)
        acc[rows, :] = o_ref[rows, :] * own_turned[0:span, r : r + 1] + ret_ref[rows, :]
    for s in range(slots):
        at = (s // cap) * block + (s % cap) * span
        rows = pl.ds(pl.multiple_of(owners[s] * span, span), span)
        acc[rows, :] = acc[rows, :] + msg_ref[at : at + span, :].astype(F32) * turned[
            0:span, s : s + 1
        ]
    for r in range(reqs):
        for h in range(heads):
            at = r * span + h * draft
            mixed[r * draft : (r + 1) * draft, h * HD : (h + 1) * HD] = acc[
                at : at + draft, :
            ].astype(BF16)
    rows = reqs * draft // pieces
    for p, out_ref in enumerate(outs):
        first = lax.rem(side[0] + p, pieces) * rows
        out_ref[...] = mixed[pl.ds(pl.multiple_of(first, rows), rows), :]


def run_copies(pairs, sems):
    copies = [
        pltpu.make_async_copy(source, target, sems.at[i])
        for i, (source, target) in enumerate(pairs)
    ]
    for copy in copies:
        copy.start()
    return copies


def cut_first(side, gate_up_w, down_w, out_w, first_ref, quarter_ref, sems):
    depth, width = down_w.shape[0] // 4, out_w.shape[0] // 4
    down_rows = pl.ds(pl.multiple_of(side[2] * depth, EXTRA), depth)
    out_rows = pl.ds(pl.multiple_of(side[2] * width, EXTRA), width)
    pairs = [
        (gate_up_w.at[side[1], pl.ds(0, first_ref.shape[0])], first_ref),
        (down_w.at[down_rows], quarter_ref.at[pl.ds(0, depth)]),
        (out_w.at[out_rows], quarter_ref.at[pl.ds(depth, width)]),
    ]
    for copy in run_copies(pairs, sems):
        copy.wait()


def cut_last(side, gate_up_w, last_ref, sems):
    last = last_ref.shape[0]
    rows = pl.ds(gate_up_w.shape[1] - last, last)
    for copy in run_copies([(gate_up_w.at[side[1], rows], last_ref)], sems):
        copy.wait()


def stage_weights(
    side, out_w, gate_up_w, down_w, one_a, one_b, one_q, two_a, two_b, two_q, three_q, four_q,
    out_all, gate_up_all, down_all, sems,
):
    width, depth = out_w.shape[0] // 4, down_w.shape[0] // 4
    first, last = one_a.shape[0], one_b.shape[0]
    pairs = [(gate_up_w, gate_up_all.at[0]), (down_w, down_all.at[0]), (out_w, out_all.at[0])]
    for half, a, b in ((side[1], one_a, one_b), (1 - side[1], two_a, two_b)):
        target = gate_up_all.at[1, half]
        pairs.append((a, target.at[pl.ds(0, first)]))
        pairs.append((b, target.at[pl.ds(first, last)]))
    core, chip = side[1], side[2] // 2
    for x, y, q in ((core, chip, one_q), (1 - core, chip, two_q), (core, 1 - chip, three_q), (
        1 - core, 1 - chip, four_q,
    )):
        part = 2 * y + x
        units = pl.ds(pl.multiple_of(part * depth, EXTRA), depth)
        rows = pl.ds(pl.multiple_of(part * width, EXTRA), width)
        pairs.append((q.at[pl.ds(0, depth)], down_all.at[1, units]))
        pairs.append((q.at[pl.ds(depth, width)], out_all.at[1, rows]))
    for copy in run_copies(pairs, sems):
        copy.wait()


def feed_up(
    side, tok_ref, mine_ref, theirs_ref, gain_ref, out_w, gate_up_w, residual_ref, hidden_ref
):
    rows = mine_ref.shape[0]
    units = gate_up_w.shape[3]
    tokens = tok_ref[pl.ds(pl.multiple_of(side[0] * rows, rows), rows), :].astype(F32)
    summed = tokens + jnp.dot(mine_ref[...], out_w[0], preferred_element_type=F32)
    summed = summed + jnp.dot(theirs_ref[...], out_w[1], preferred_element_type=F32)
    residual_ref[...] = summed.astype(BF16)
    ffn_in = rms_norm(residual_ref[...], gain_ref[...])
    step = 256
    for half in range(2):
        for first in range(0, units, step):
            cols = slice(first, min(first + step, units))
            gate = jnp.dot(ffn_in, gate_up_w[half, 0, :, cols], preferred_element_type=F32)
            up = jnp.dot(ffn_in, gate_up_w[half, 1, :, cols], preferred_element_type=F32)
            hidden_ref[half, :, cols] = (gate / (1.0 + jnp.exp(-gate)) * up).astype(BF16)


def feed_down(residual_ref, hidden_ref, down_w, out_ref):
    step = 256
    for at in range(0, out_ref.shape[1], step):
        cols = slice(at, at + step)
        total = residual_ref[:, cols].astype(F32)
        for half in range(2):
            total = total + jnp.dot(
                hidden_ref[half], down_w[half, :, cols], preferred_element_type=F32
            )
        out_ref[:, cols] = total.astype(BF16)


def on_device(
    tokens,
    norm_attn,
    w_query,
    w_key,
    w_value,
    w_out,
    persist_keys,
    persist_values,
    kv_cache,
    slot_request,
    slot_page,
    cache_len,
    tree_mask,
    accept_path,
    accept_len,
    memory,
    momentum,
    momentum_code,
    forget_code,
    norm_ffn,
    w_gate_up,
    w_down,
):
    n = lax.axis_size("req")
    group_rows, model = tokens.shape
    reqs = cache_len.shape[0]
    draft = tree_mask.shape[1]
    steps = accept_path.shape[1]
    width = w_query.shape[1]
    heads = width // HD
    span = heads * draft
    slots = kv_cache.shape[0]
    cap = slots // n
    fixed_count = persist_keys.shape[0]
    page_len = kv_cache.shape[2]
    ask_block = cap * HD + EXTRA
    block = cap * span + EXTRA
    scale = 1.0 / math.sqrt(HD)

    label = (slot_page * reqs + lax.rem(slot_request, reqs)).reshape(n, 1, cap)
    codes = lax.all_to_all(label, "req", split_axis=0, concat_axis=0, tiled=True)

    grp = lax.axis_size("grp")
    depth, out_depth = w_down.shape[0] // 4, width // 4
    first = model * 10 // 32
    split = (depth, out_depth, first)
    pieces = 2 if grp == 2 and n % 4 == 0 and not any(size % EXTRA for size in split) else 1
    quarter = lax.rem(lax.axis_index("req"), 4)
    core = lax.rem(quarter, 2)
    side = jnp.stack([lax.axis_index("grp"), core, quarter]).astype(jnp.int32)
    if pieces == 2:
        units = w_down.shape[0]
        half_first, quarters = pl.pallas_call(
            cut_first,
            out_shape=(HBM((first, units), BF16), HBM((depth + out_depth, model), BF16)),
            in_specs=[whole(SMEM)] + [whole(HBM)] * 3,
            out_specs=(whole(),) * 2,
            scratch_shapes=[pltpu.SemaphoreType.DMA((3,))],
            compiler_params=params(4),
            cost_estimate=cost(0, 4 * (first * units + (depth + out_depth) * model)),
            name="cut_first",
        )(side, *keep_in(HBM, w_gate_up, w_down, w_out))
        half_last = pl.pallas_call(
            cut_last,
            out_shape=HBM((model - first, units), BF16),
            in_specs=[whole(SMEM), whole(HBM)],
            out_specs=whole(),
            scratch_shapes=[pltpu.SemaphoreType.DMA((1,))],
            compiler_params=params(4),
            cost_estimate=cost(0, 4 * (model - first) * units),
            name="cut_last",
        )(side, *keep_in(HBM, w_gate_up))

    normed, queries, turned = pl.pallas_call(
        functools.partial(project_queries, reqs=reqs, draft=draft, heads=heads),
        out_shape=(
            HBM((group_rows, model), BF16),
            HBM((group_rows, width), BF16),
            jax.ShapeDtypeStruct((reqs * HD, LANES), BF16),
        ),
        in_specs=[whole()] * 3,
        out_specs=(whole(),) * 3,
        compiler_params=params(12),
        cost_estimate=cost(
            2 * group_rows * model * width, 2 * model * (2 * group_rows + width)
        ),
        name="project_queries",
    )(*keep_in(HBM, tokens, norm_attn.reshape(1, -1), w_query))

    if pieces == 2:
        turned, half_first, quarters = lax.optimization_barrier((turned, half_first, quarters))
        swap = [(0, 1), (1, 0)]
        one_a = lax.ppermute(half_first, "grp", swap)
        one_q = lax.ppermute(quarters, "grp", swap)

    packed = pl.pallas_call(
        functools.partial(pack_queries, n=n, cap=cap, reqs=reqs, page_len=page_len),
        out_shape=HBM((n * ask_block, LANES), BF16),
        in_specs=[whole(SMEM), whole(SMEM), whole()],
        out_specs=whole(),
        compiler_params=params(8),
        cost_estimate=cost(0, 4 * n * ask_block * LANES),
        name="pack_queries",
    )(codes, *keep_in(HBM, cache_len), turned)
    asked = lax.all_to_all(packed, "req", split_axis=0, concat_axis=0, tiled=True)

    keys, values = pl.pallas_call(
        project_keys,
        out_shape=(HBM((group_rows, width), BF16),) * 2,
        in_specs=[whole()] * 3,
        out_specs=(whole(),) * 2,
        compiler_params=params(12),
        cost_estimate=cost(
            4 * group_rows * model * width, 2 * model * (group_rows + 2 * width)
        ),
        name="project_keys",
    )(*keep_in(HBM, normed, w_key, w_value))

    row_block = pl.BlockSpec((draft, width), lambda r, *_: (r, 0))
    fixed_block = pl.BlockSpec((fixed_count, width), lambda r, *_: (0, 0))
    matrix_block = pl.BlockSpec((1, heads, HD, HD), lambda r, *_: (r, 0, 0, 0))
    span_block = pl.BlockSpec((span, HD), lambda r, *_: (r, 0))
    own, retrieved, own_top, own_sum = pl.pallas_call(
        functools.partial(local_attention, heads=heads, draft=draft, scale=scale),
        grid=(reqs,),
        out_shape=(
            HBM((reqs * span, HD), F32),
            HBM((reqs * span, HD), F32),
            jax.ShapeDtypeStruct((reqs, LANES), F32),
            jax.ShapeDtypeStruct((reqs, LANES), F32),
        ),
        in_specs=[
            row_block,
            row_block,
            row_block,
            fixed_block,
            fixed_block,
            pl.BlockSpec((1, draft, draft), lambda r: (r, 0, 0)),
            matrix_block,
        ],
        out_specs=(span_block, span_block) + (pl.BlockSpec((reqs, LANES), lambda r: (0, 0)),) * 2,
        compiler_params=params(10),
        cost_estimate=cost(
            2 * reqs * span * HD * (2 * (draft + fixed_count) + 6 * HD),
            4 * reqs * (heads * HD * HD + 2 * span * HD),
            reqs * span * (draft + fixed_count),
        ),
        name="local_attention",
    )(*keep_in(HBM, queries, keys, values, persist_keys, persist_values, tree_mask, memory))

    matrices = jax.ShapeDtypeStruct(memory.shape, F32)
    memory_out, momentum_out = pl.pallas_call(
        functools.partial(update_memory, heads=heads, steps=steps),
        grid_spec=pltpu.PrefetchScalarGridSpec(
            num_scalar_prefetch=4,
            grid=(reqs,),
            in_specs=[row_block, row_block, matrix_block, matrix_block],
            out_specs=(matrix_block, matrix_block),
            scratch_shapes=[
                pltpu.VMEM((draft, width), F32),
                pltpu.VMEM((draft, width), F32),
                pltpu.VMEM((LANES, HD), F32),
                pltpu.VMEM((heads * steps, HD), F32),
                pltpu.VMEM((HD, LANES), F32),
            ],
        ),
        out_shape=(matrices, matrices),
        compiler_params=params(10),
        cost_estimate=cost(
            14 * reqs * heads * HD * HD * steps * 8, 16 * reqs * heads * HD * HD
        ),
        name="update_memory",
    )(
        accept_path.reshape(-1),
        accept_len,
        momentum_code.reshape(-1),
        forget_code.reshape(-1),
        *keep_in(HBM, keys, values, memory, momentum),
    )

    asked, memory_out, momentum_out, keys, values = lax.optimization_barrier(
        (asked, memory_out, momentum_out, keys, values)
    )
    if pieces == 2:
        asked, half_last = lax.optimization_barrier((asked, half_last))
    answers = pl.pallas_call(
        functools.partial(
            page_attention, n=n, cap=cap, draft=draft, heads=heads, page_len=page_len,
            scale=scale, group=2,
        ),
        out_shape=HBM((n * block, LANES), BF16),
        in_specs=[whole(), whole(HBM)],
        out_specs=whole(HBM),
        scratch_shapes=[
            pltpu.VMEM((n, cap) + kv_cache.shape[1:], BF16),
            pltpu.VMEM((n * block, LANES), BF16),
            pltpu.SemaphoreType.DMA((n,)),
            pltpu.SemaphoreType.DMA((n,)),
        ],
        compiler_params=params(24),
        cost_estimate=cost(
            4 * slots * span * page_len * HD,
            4 * slots * page_len * width + 4 * n * block * LANES,
            slots * span * page_len,
        ),
        name="page_attention",
    )(asked, *keep_in(HBM, kv_cache))
    if pieces == 2:
        answers, half_last, one_a, one_q = lax.optimization_barrier(
            (answers, half_last, one_a, one_q)
        )
    returned = lax.all_to_all(answers, "req", split_axis=0, concat_axis=0, tiled=True)
    if pieces == 2:
        other_core = [(i, i ^ 1) for i in range(n)]
        other_chip = [(i, i ^ 2) for i in range(n)]
        one_b = lax.ppermute(half_last, "grp", swap)
        three_q = lax.ppermute(one_q, "req", other_chip)
        two_a = lax.ppermute(one_a, "req", other_core)
        two_q = lax.ppermute(one_q, "req", other_core)
        returned, one_b, two_a, two_q, three_q, own, retrieved, own_top, own_sum = (
            lax.optimization_barrier(
                (returned, one_b, two_a, two_q, three_q, own, retrieved, own_top, own_sum)
            )
        )
        two_b = lax.ppermute(one_b, "req", other_core)
        four_q = lax.ppermute(three_q, "req", other_core)
    rows = group_rows // grp
    mixed = pl.pallas_call(
        functools.partial(
            combine, n=n, cap=cap, reqs=reqs, draft=draft, heads=heads, pieces=pieces
        ),
        out_shape=(jax.ShapeDtypeStruct((group_rows // pieces, width), BF16),) * pieces,
        in_specs=[whole(SMEM)] * 2 + [whole()] + [whole(HBM)] * 2 + [whole()] * 2,
        out_specs=(whole(),) * pieces,
        scratch_shapes=[
            pltpu.VMEM((slots, LANES), F32),
            pltpu.VMEM((slots, LANES), F32),
            pltpu.VMEM((reqs, LANES), F32),
            pltpu.VMEM((reqs, LANES), F32),
            pltpu.VMEM((LANES, LANES), F32),
            pltpu.VMEM((LANES, LANES), F32),
            pltpu.VMEM((reqs * span, HD), F32),
            pltpu.VMEM((group_rows, width), BF16),
            pltpu.VMEM((reqs * span, HD), F32),
            pltpu.VMEM((reqs * span, HD), F32),
            pltpu.SemaphoreType.DMA((2,)),
        ],
        compiler_params=params(12),
        cost_estimate=cost(
            8 * slots * span * HD, 2 * n * block * LANES + 8 * reqs * span * HD
        ),
        name="combine",
    )(codes, side, returned, *keep_in(HBM, own, retrieved), own_top, own_sum)

    if pieces == 2:
        mine, asked_for = mixed
        theirs = lax.ppermute(asked_for, "grp", swap)
        mine, two_a, two_b, two_q, four_q = lax.optimization_barrier(
            (mine, two_a, two_b, two_q, four_q)
        )
        out_near, gate_up_near, down_near = pl.pallas_call(
            stage_weights,
            out_shape=(
                VMEM((2,) + w_out.shape, BF16),
                VMEM((2,) + w_gate_up.shape, BF16),
                VMEM((2,) + w_down.shape, BF16),
            ),
            in_specs=[whole(SMEM)] + [whole(pl.ANY)] * 11,
            out_specs=(whole(),) * 3,
            scratch_shapes=[pltpu.SemaphoreType.DMA((15,))],
            compiler_params=params(2),
            cost_estimate=cost(0, 2 * model * (2 * width + 6 * units)),
            name="stage_weights",
        )(
            side,
            *keep_in(HBM, w_out, w_gate_up, w_down, one_a, one_b, one_q, two_a),
            two_b,
            *keep_in(HBM, two_q, three_q),
            four_q,
        )
        residual, hidden = pl.pallas_call(
            feed_up,
            out_shape=(VMEM((rows, model), BF16), VMEM((2, rows, units), BF16)),
            in_specs=[whole(SMEM)] + [whole()] * 6,
            out_specs=(whole(),) * 2,
            compiler_params=params(12),
            cost_estimate=cost(
                4 * rows * model * (width + 2 * units), 4 * model * (width + 2 * units)
            ),
            name="feed_up",
        )(
            side, tokens, mine, theirs, norm_ffn.reshape(1, -1),
            *keep_in(VMEM, out_near, gate_up_near),
        )
        layer_out = pl.pallas_call(
            feed_down,
            out_shape=jax.ShapeDtypeStruct((rows, model), BF16),
            in_specs=[whole()] * 3,
            out_specs=whole(),
            compiler_params=params(6),
            cost_estimate=cost(4 * rows * model * units, 4 * model * units),
            name="feed_down",
        )(*keep_in(VMEM, residual, hidden, down_near))
        return (layer_out, memory_out, momentum_out)

    partial_out = jnp.dot(mixed[0], w_out, preferred_element_type=F32).astype(BF16)
    head_sum = lax.psum_scatter(partial_out, "grp", scatter_dimension=0, tiled=True).astype(F32)
    own_rows = lax.dynamic_slice_in_dim(tokens, lax.axis_index("grp") * rows, rows, 0)
    residual = (own_rows.astype(F32) + head_sum).astype(BF16)
    ffn_in = rms_norm(residual, norm_ffn)
    piece = lax.all_gather(ffn_in, "grp", axis=0, tiled=True)
    gate = jnp.dot(piece, w_gate_up[0], preferred_element_type=F32)
    up = jnp.dot(piece, w_gate_up[1], preferred_element_type=F32)
    hidden = (jax.nn.silu(gate) * up).astype(BF16)
    ffn_out = lax.psum_scatter(
        jnp.dot(hidden, w_down, preferred_element_type=F32).astype(BF16),
        "grp",
        scatter_dimension=0,
        tiled=True,
    ).astype(F32)
    layer_out = (residual.astype(F32) + ffn_out).astype(BF16)
    return (layer_out, memory_out, momentum_out)


def solution(mesh):
    return jax.shard_map(
        on_device,
        mesh=mesh,
        in_specs=(
            P("req", None),
            P(),
            P(None, "grp"),
            P(None, "grp"),
            P(None, "grp"),
            P("grp", None),
            P(None, "grp"),
            P(None, "grp"),
            P("req", None, None, "grp"),
            P("req"),
            P("req"),
            P("req"),
            P("req", None, None),
            P("req", None),
            P("req"),
            P("req", "grp", None, None),
            P("req", "grp", None, None),
            P("req", None, "grp"),
            P("req", None, "grp"),
            P(),
            P(None, None, "grp"),
            P("grp", None),
        ),
        out_specs=(
            P(("req", "grp"), None),
            P("req", "grp", None, None),
            P("req", "grp", None, None),
        ),
        check_vma=False,
    )
```

```python
import functools
import math

import jax
import jax.numpy as jnp
from jax import lax
from jax.experimental import pallas as pl
from jax.experimental.pallas import tpu as pltpu
from jax.sharding import PartitionSpec as P

HD = 128
LANES = 128
EXTRA = 16
TOP_PARTS = 3
WEIGHT = 20
SUM_PARTS = 2

EPS = 1e-06
THETA = 0.5
NEG = -1e30

VMEM = pltpu.VMEM
SMEM = pltpu.SMEM
HBM = pltpu.HBM
F32 = jnp.float32
BF16 = jnp.bfloat16


def whole(space=VMEM):
    return pl.BlockSpec(memory_space=space)


def cost(flops, moved, special=0):
    return pl.CostEstimate(
        flops=WEIGHT * flops, bytes_accessed=WEIGHT * moved, transcendentals=special
    )


def keep_in(space, *arrays):
    return tuple(pltpu.with_memory_space_constraint(array, space) for array in arrays)


def params(mib=40):
    return pltpu.CompilerParams(vmem_limit_bytes=mib << 20)


def rms_norm(rows, gain):
    values = rows.astype(F32)
    factor = lax.rsqrt(jnp.mean(values * values, axis=-1, keepdims=True) + EPS)
    return (values * factor * gain).astype(BF16)


def nt_dot(left, right):
    return lax.dot_general(left, right, (((1,), (1,)), ((), ())), preferred_element_type=F32)


def column_to_row(column, count):
    row_id = lax.broadcasted_iota(jnp.int32, (count, LANES), 0)
    lane_id = lax.broadcasted_iota(jnp.int32, (count, LANES), 1)
    spread = jnp.where(row_id == lane_id, jnp.broadcast_to(column, (count, LANES)), 0.0)
    return jnp.sum(spread, axis=0, keepdims=True)


def split_parts(row, count):
    parts = []
    for _ in range(count):
        part = row.astype(BF16).astype(F32)
        parts.append(part)
        row = row - part
    return parts


def project_queries(tok_ref, gain_ref, w_ref, normed_ref, q_ref, turned_ref, *, reqs, draft, heads):
    normed_ref[...] = rms_norm(tok_ref[...], gain_ref[...])
    q_ref[...] = jnp.dot(normed_ref[...], w_ref[...], preferred_element_type=F32).astype(BF16)
    span = heads * draft
    for r in range(reqs):
        rows = slice(r * draft, (r + 1) * draft)
        pieces = [q_ref[rows, h * HD : (h + 1) * HD].astype(F32) for h in range(heads)]
        if span < LANES:
            pieces.append(jnp.zeros((LANES - span, HD), F32))
        tile = jnp.concatenate(pieces, axis=0)
        turned_ref[r * HD : (r + 1) * HD, :] = jnp.transpose(tile).astype(BF16)


def project_keys(normed_ref, wk_ref, wv_ref, k_ref, v_ref):
    normed = normed_ref[...]
    k_ref[...] = jnp.dot(normed, wk_ref[...], preferred_element_type=F32).astype(BF16)
    v_ref[...] = jnp.dot(normed, wv_ref[...], preferred_element_type=F32).astype(BF16)


def pack_queries(codes, lengths, turned_ref, out_ref, *, n, cap, reqs, page_len):
    block = cap * HD + EXTRA
    row_id = lax.broadcasted_iota(jnp.int32, (EXTRA, LANES), 0)

    def one(d, carry):
        base = pl.multiple_of(d * block, EXTRA)
        tail = jnp.zeros((EXTRA, LANES), F32)
        for c in range(cap):
            code = codes[d, 0, c]
            r = lax.rem(code, reqs)
            page = lax.div(code, reqs)
            live = jnp.clip(lengths[r] - page * page_len, 0, page_len)
            tail = jnp.where(row_id == c, live.astype(F32), tail)
            rows = pl.ds(pl.multiple_of(r * HD, HD), HD)
            out_ref[pl.ds(base + c * HD, HD), :] = turned_ref[rows, :]
        out_ref[pl.ds(base + cap * HD, EXTRA), :] = tail.astype(BF16)
        return carry

    lax.fori_loop(0, n, one, 0)


def page_attention(
    q_ref, kv_hbm, out_hbm, kv_buf, out_buf, in_sems, out_sems,
    *, n, cap, draft, heads, page_len, scale, group,
):
    span = heads * draft
    ask_block = cap * HD + EXTRA
    block = cap * span + EXTRA
    token = lax.broadcasted_iota(jnp.int32, (page_len, LANES), 0).astype(F32)
    row_id = lax.broadcasted_iota(jnp.int32, (EXTRA, LANES), 0)
    head_of = lax.broadcasted_iota(jnp.int32, (HD, LANES), 1) // draft

    def arrival(d):
        return pltpu.make_async_copy(
            kv_hbm.at[pl.ds(d * cap, cap)], kv_buf.at[d], in_sems.at[d]
        )

    def departure(d):
        rows = pl.ds(pl.multiple_of(d * block, EXTRA), block)
        return pltpu.make_async_copy(out_buf.at[rows], out_hbm.at[rows], out_sems.at[d])

    for d in range(n):
        arrival(d).start()

    def one(i, carry):
        pairs = [(i * group + g, c) for g in range(group) for c in range(cap)]
        limits = []
        for g in range(group):
            d = i * group + g
            arrival(d).wait()
            at = pl.multiple_of(d * ask_block + cap * HD, EXTRA)
            limits.append(q_ref[pl.ds(at, EXTRA), :].astype(F32))
        all_scores = []
        for d, c in pairs:
            at = pl.multiple_of(d * ask_block + c * HD, EXTRA)
            turned = q_ref[pl.ds(at, HD), :]
            blocks = [jnp.where(head_of == h, turned, jnp.zeros_like(turned)) for h in range(heads)]
            all_scores.append(
                jnp.dot(
                    kv_buf[d, c, 0], jnp.concatenate(blocks, axis=0), preferred_element_type=F32
                )
            )
        all_weights = []
        tails = [jnp.zeros((EXTRA, LANES), F32) for _ in range(group)]
        for j, (d, c) in enumerate(pairs):
            g = j // cap
            scores = jnp.where(token < limits[g][c : c + 1, :], all_scores[j] * scale, NEG)
            top = jnp.max(scores, axis=0, keepdims=True)
            weight = jnp.exp(scores - top)
            total = jnp.sum(weight, axis=0, keepdims=True)
            all_weights.append(jnp.transpose(weight).astype(BF16))
            parts = split_parts(top, TOP_PARTS) + split_parts(total, SUM_PARTS)
            for p, part in enumerate(parts):
                tails[g] = jnp.where(row_id == p * cap + c, part, tails[g])
        for j, (d, c) in enumerate(pairs):
            for h in range(heads):
                numer = jnp.dot(
                    all_weights[j][h * draft : (h + 1) * draft, :],
                    kv_buf[d, c, 1, :, h * HD : (h + 1) * HD],
                    preferred_element_type=F32,
                )
                at = pl.multiple_of(d * block + c * span + h * draft, EXTRA)
                out_buf[pl.ds(at, draft), :] = numer.astype(BF16)
        for g in range(group):
            d = i * group + g
            at = pl.multiple_of(d * block + cap * span, EXTRA)
            out_buf[pl.ds(at, EXTRA), :] = tails[g].astype(BF16)
            departure(d).start()
        return carry

    lax.fori_loop(0, n // group, one, 0)
    for d in range(n):
        departure(d).wait()


def local_attention(
    q_ref, k_ref, v_ref, pk_ref, pv_ref, mask_ref, mem_ref,
    o_ref, ret_ref, top_ref, sum_ref, *, heads, draft, scale,
):
    r = pl.program_id(0)
    seen = mask_ref[0] == 1
    tops, totals = [], []
    for h in range(heads):
        cols = slice(h * HD, (h + 1) * HD)
        rows = slice(h * draft, (h + 1) * draft)
        query = q_ref[:, cols]
        tree = jnp.where(seen, nt_dot(query, k_ref[:, cols]) * scale, NEG)
        fixed = nt_dot(query, pk_ref[:, cols]) * scale
        top = jnp.maximum(
            jnp.max(tree, axis=1, keepdims=True), jnp.max(fixed, axis=1, keepdims=True)
        )
        tree_w = jnp.exp(tree - top)
        fixed_w = jnp.exp(fixed - top)
        total = jnp.sum(tree_w, axis=1, keepdims=True) + jnp.sum(fixed_w, axis=1, keepdims=True)
        numer = jnp.dot(tree_w.astype(BF16), v_ref[:, cols], preferred_element_type=F32)
        numer = numer + jnp.dot(fixed_w.astype(BF16), pv_ref[:, cols], preferred_element_type=F32)
        o_ref[rows, :] = numer
        tops.append(top)
        totals.append(total)
        wide = query.astype(F32)
        unit = wide * lax.rsqrt(jnp.sum(wide * wide, axis=1, keepdims=True) + EPS)
        ret_ref[rows, :] = jnp.dot(
            unit, mem_ref[0, h], preferred_element_type=F32, precision=lax.Precision.HIGHEST
        )
    span = heads * draft
    top_ref[pl.ds(r, 1), :] = column_to_row(jnp.concatenate(tops, axis=0), span)
    sum_ref[pl.ds(r, 1), :] = column_to_row(jnp.concatenate(totals, axis=0), span)


def update_memory(
    path, count, mom_code, forget_code, k_ref, v_ref, mem_hbm, mom_hbm, mem_out, mom_out,
    mem_buf, mom_buf, wide_k, wide_v, unit_ref, value_ref, turned_ref, in_sems, out_sems,
    *, reqs, draft, heads, steps,
):
    def arrivals(r):
        return (
            pltpu.make_async_copy(mem_hbm.at[r], mem_buf.at[r], in_sems.at[0, r]),
            pltpu.make_async_copy(mom_hbm.at[r], mom_buf.at[r], in_sems.at[1, r]),
        )

    def departures(r):
        return (
            pltpu.make_async_copy(mem_buf.at[r], mem_out.at[r], out_sems.at[0, r]),
            pltpu.make_async_copy(mom_buf.at[r], mom_out.at[r], out_sems.at[1, r]),
        )

    for r in range(reqs):
        for copy in arrivals(r):
            copy.start()
    unit_ref[...] = jnp.zeros_like(unit_ref)

    def one(r, carry):
        rows = pl.ds(pl.multiple_of(r * draft, draft), draft)
        wide_k[...] = k_ref[rows, :].astype(F32)
        wide_v[...] = v_ref[rows, :].astype(F32)
        for n in range(steps):
            node = path[n, r]
            k_row = wide_k[pl.ds(node, 1), :]
            v_row = wide_v[pl.ds(node, 1), :]
            for h in range(heads):
                unit_ref[h * steps + n : h * steps + n + 1, :] = k_row[:, h * HD : (h + 1) * HD]
                value_ref[h * steps + n : h * steps + n + 1, :] = v_row[:, h * HD : (h + 1) * HD]
        keys = unit_ref[...]
        unit = keys * lax.rsqrt(jnp.sum(keys * keys, axis=1, keepdims=True) + EPS)
        turned_ref[...] = jnp.transpose(unit)
        for copy in arrivals(r):
            copy.wait()

        def advance(n):
            for h in range(heads):
                eta = 0.97 - 0.06 * mom_code[n, h, r].astype(F32)
                keep = 1.0 - (0.01 + 0.02 * forget_code[n, h, r].astype(F32))
                row = h * steps + n
                column = turned_ref[:, row : row + 1]
                matrix = mem_buf[r, h]
                predicted = jnp.sum(column * matrix, axis=0, keepdims=True)
                error = THETA * (predicted - value_ref[row : row + 1, :])
                moved = eta * mom_buf[r, h] - column * error
                mom_buf[r, h] = moved
                mem_buf[r, h] = keep * matrix + moved

        for n in range(steps):
            pl.when(n < count[r])(functools.partial(advance, n))
        for copy in departures(r):
            copy.start()
        return carry

    lax.fori_loop(0, reqs, one, 0)
    for r in range(reqs):
        for copy in departures(r):
            copy.wait()


def combine(
    codes, side, msg_ref, o_hbm, ret_hbm, own_top_ref, own_sum_ref, *rest,
    n, cap, reqs, draft, heads, pieces,
):
    outs = rest[:pieces]
    part_top, part_sum, best, total, weight, own_weight, acc, mixed, o_ref, ret_ref, sems = rest[
        pieces:
    ]
    copies = [
        pltpu.make_async_copy(o_hbm, o_ref, sems.at[0]),
        pltpu.make_async_copy(ret_hbm, ret_ref, sems.at[1]),
    ]
    for copy in copies:
        copy.start()
    span = heads * draft
    block = cap * span + EXTRA
    slots = n * cap
    for d in range(n):
        at = d * block + cap * span
        tail = msg_ref[at : at + EXTRA, :].astype(F32)
        rows = [tail[p * cap : (p + 1) * cap] for p in range(TOP_PARTS + SUM_PARTS)]
        part_top[d * cap : (d + 1) * cap, :] = rows[0] + rows[1] + rows[2]
        part_sum[d * cap : (d + 1) * cap, :] = rows[3] + rows[4]
    best[...] = own_top_ref[...]
    owners = [lax.rem(codes[s // cap, 0, s % cap], reqs) for s in range(slots)]
    for s in range(slots):
        r = owners[s]
        best[pl.ds(r, 1), :] = jnp.maximum(best[pl.ds(r, 1), :], part_top[s : s + 1, :])
    own_weight[...] = jnp.zeros_like(own_weight)
    weight[...] = jnp.zeros_like(weight)
    start = jnp.exp(own_top_ref[...] - best[...])
    total[...] = start * own_sum_ref[...]
    for s in range(slots):
        r = owners[s]
        term = jnp.exp(part_top[s : s + 1, :] - best[pl.ds(r, 1), :])
        weight[s : s + 1, :] = term
        total[pl.ds(r, 1), :] = total[pl.ds(r, 1), :] + term * part_sum[s : s + 1, :]
    inverse = 1.0 / total[...]
    own_weight[0:reqs, :] = start * inverse
    total[...] = inverse
    for s in range(slots):
        weight[s : s + 1, :] = weight[s : s + 1, :] * total[pl.ds(owners[s], 1), :]
    turned = jnp.transpose(weight[...])
    own_turned = jnp.transpose(own_weight[...])
    for copy in copies:
        copy.wait()
    for r in range(reqs):
        rows = slice(r * span, (r + 1) * span)
        acc[rows, :] = o_ref[rows, :] * own_turned[0:span, r : r + 1] + ret_ref[rows, :]
    for s in range(slots):
        at = (s // cap) * block + (s % cap) * span
        rows = pl.ds(pl.multiple_of(owners[s] * span, span), span)
        acc[rows, :] = acc[rows, :] + msg_ref[at : at + span, :].astype(F32) * turned[
            0:span, s : s + 1
        ]
    for r in range(reqs):
        for h in range(heads):
            at = r * span + h * draft
            mixed[r * draft : (r + 1) * draft, h * HD : (h + 1) * HD] = acc[
                at : at + draft, :
            ].astype(BF16)
    rows = reqs * draft // pieces
    for p, out_ref in enumerate(outs):
        first = lax.rem(side[0] + p, pieces) * rows
        out_ref[...] = mixed[pl.ds(pl.multiple_of(first, rows), rows), :]


def run_copies(pairs, sems):
    copies = [
        pltpu.make_async_copy(source, target, sems.at[i])
        for i, (source, target) in enumerate(pairs)
    ]
    for copy in copies:
        copy.start()
    return copies


def cut_first(side, gate_up_w, down_w, out_w, first_ref, quarter_ref, sems):
    depth, width = down_w.shape[0] // 4, out_w.shape[0] // 4
    down_rows = pl.ds(pl.multiple_of(side[2] * depth, EXTRA), depth)
    out_rows = pl.ds(pl.multiple_of(side[2] * width, EXTRA), width)
    pairs = [
        (gate_up_w.at[side[1], pl.ds(0, first_ref.shape[0])], first_ref),
        (down_w.at[down_rows], quarter_ref.at[pl.ds(0, depth)]),
        (out_w.at[out_rows], quarter_ref.at[pl.ds(depth, width)]),
    ]
    for copy in run_copies(pairs, sems):
        copy.wait()


def cut_last(side, gate_up_w, mid_ref, last_ref, sems, *, pieces):
    step = last_ref.shape[0] // pieces
    start = gate_up_w.shape[1] - last_ref.shape[0]
    half = gate_up_w.at[side[1]]
    middle = mid_ref.shape[0]
    pairs = [(half.at[pl.ds(start - middle, middle)], mid_ref)]
    for i in range(pieces):
        pairs.append((half.at[pl.ds(start + i * step, step)], last_ref.at[pl.ds(i * step, step)]))
    for copy in run_copies(pairs, sems):
        copy.wait()


def stage_weights(
    side, out_w, gate_up_w, down_w, one_a, one_m, one_b, one_q, two_a, two_m, two_b, two_q, three_q,
    four_q, out_all, gate_up_all, down_all, sems,
):
    width, depth = out_w.shape[0] // 4, down_w.shape[0] // 4
    pairs = [(gate_up_w, gate_up_all.at[0]), (down_w, down_all.at[0]), (out_w, out_all.at[0])]
    for half, parts in ((side[1], (one_a, one_m, one_b)), (1 - side[1], (two_a, two_m, two_b))):
        at = 0
        for part in parts:
            pairs.append((part, gate_up_all.at[1, half, pl.ds(at, part.shape[0])]))
            at += part.shape[0]
    core, chip = side[1], side[2] // 2
    for x, y, q in ((core, chip, one_q), (1 - core, chip, two_q), (core, 1 - chip, three_q), (
        1 - core, 1 - chip, four_q,
    )):
        part = 2 * y + x
        units = pl.ds(pl.multiple_of(part * depth, EXTRA), depth)
        rows = pl.ds(pl.multiple_of(part * width, EXTRA), width)
        pairs.append((q.at[pl.ds(0, depth)], down_all.at[1, units]))
        pairs.append((q.at[pl.ds(depth, width)], out_all.at[1, rows]))
    for copy in run_copies(pairs, sems):
        copy.wait()


def feed_forward(
    side, tok_ref, mine_ref, theirs_ref, gain_ref, out_w, gate_up_w, down_w, out_ref,
    residual, hidden,
):
    rows = mine_ref.shape[0]
    units = gate_up_w.shape[3]
    tokens = tok_ref[pl.ds(pl.multiple_of(side[0] * rows, rows), rows), :].astype(F32)
    summed = tokens + jnp.dot(mine_ref[...], out_w[0], preferred_element_type=F32)
    summed = summed + jnp.dot(theirs_ref[...], out_w[1], preferred_element_type=F32)
    residual[...] = summed.astype(BF16)
    ffn_in = rms_norm(residual[...], gain_ref[...])
    step = 256
    for half in range(2):
        for first in range(0, units, step):
            cols = slice(first, min(first + step, units))
            gate = jnp.dot(ffn_in, gate_up_w[half, 0, :, cols], preferred_element_type=F32)
            up = jnp.dot(ffn_in, gate_up_w[half, 1, :, cols], preferred_element_type=F32)
            hidden[half, :, cols] = (gate / (1.0 + jnp.exp(-gate)) * up).astype(BF16)
    for at in range(0, out_ref.shape[1], step):
        cols = slice(at, at + step)
        total = residual[:, cols].astype(F32)
        for half in range(2):
            total = total + jnp.dot(hidden[half], down_w[half, :, cols], preferred_element_type=F32)
        out_ref[:, cols] = total.astype(BF16)


def on_device(
    tokens,
    norm_attn,
    w_query,
    w_key,
    w_value,
    w_out,
    persist_keys,
    persist_values,
    kv_cache,
    slot_request,
    slot_page,
    cache_len,
    tree_mask,
    accept_path,
    accept_len,
    memory,
    momentum,
    momentum_code,
    forget_code,
    norm_ffn,
    w_gate_up,
    w_down,
):
    n = lax.axis_size("req")
    group_rows, model = tokens.shape
    reqs = cache_len.shape[0]
    draft = tree_mask.shape[1]
    steps = accept_path.shape[1]
    width = w_query.shape[1]
    heads = width // HD
    span = heads * draft
    slots = kv_cache.shape[0]
    cap = slots // n
    fixed_count = persist_keys.shape[0]
    page_len = kv_cache.shape[2]
    ask_block = cap * HD + EXTRA
    block = cap * span + EXTRA
    scale = 1.0 / math.sqrt(HD)

    label = (slot_page * reqs + lax.rem(slot_request, reqs)).reshape(n, 1, cap)
    codes = lax.all_to_all(label, "req", split_axis=0, concat_axis=0, tiled=True)

    grp = lax.axis_size("grp")
    depth, out_depth = w_down.shape[0] // 4, width // 4
    first, middle = model // 4, model * 3 // 16
    split = (depth, out_depth, first, middle, (model - first - middle) // 3)
    pieces = 2 if grp == 2 and n % 4 == 0 and not any(size % EXTRA for size in split) else 1
    quarter = lax.rem(lax.axis_index("req"), 4)
    core = lax.rem(quarter, 2)
    side = jnp.stack([lax.axis_index("grp"), core, quarter]).astype(jnp.int32)
    if pieces == 2:
        units = w_down.shape[0]
        half_first, quarters = pl.pallas_call(
            cut_first,
            out_shape=(VMEM((first, units), BF16), VMEM((depth + out_depth, model), BF16)),
            in_specs=[whole(SMEM)] + [whole(HBM)] * 3,
            out_specs=(whole(),) * 2,
            scratch_shapes=[pltpu.SemaphoreType.DMA((3,))],
            compiler_params=params(4),
            cost_estimate=cost(0, 4 * (first * units + (depth + out_depth) * model)),
            name="cut_first",
        )(side, *keep_in(HBM, w_gate_up, w_down, w_out))

    normed, queries, turned = pl.pallas_call(
        functools.partial(project_queries, reqs=reqs, draft=draft, heads=heads),
        out_shape=(
            HBM((group_rows, model), BF16),
            HBM((group_rows, width), BF16),
            jax.ShapeDtypeStruct((reqs * HD, LANES), BF16),
        ),
        in_specs=[whole()] * 3,
        out_specs=(whole(),) * 3,
        compiler_params=params(12),
        cost_estimate=cost(
            2 * group_rows * model * width, 2 * model * (2 * group_rows + width)
        ),
        name="project_queries",
    )(*keep_in(HBM, tokens, norm_attn.reshape(1, -1), w_query))

    if pieces == 2:
        turned, half_first, quarters = lax.optimization_barrier((turned, half_first, quarters))
        swap = [(0, 1), (1, 0)]
        one_a = lax.ppermute(half_first, "grp", swap)
        one_q = lax.ppermute(quarters, "grp", swap)

    packed = pl.pallas_call(
        functools.partial(pack_queries, n=n, cap=cap, reqs=reqs, page_len=page_len),
        out_shape=HBM((n * ask_block, LANES), BF16),
        in_specs=[whole(SMEM), whole(SMEM), whole()],
        out_specs=whole(),
        compiler_params=params(8),
        cost_estimate=cost(0, 4 * n * ask_block * LANES),
        name="pack_queries",
    )(codes, *keep_in(HBM, cache_len), turned)
    packed, normed, late = lax.optimization_barrier((packed, normed, w_gate_up))
    asked = lax.all_to_all(packed, "req", split_axis=0, concat_axis=0, tiled=True)

    if pieces == 2:
        half_mid, half_last = pl.pallas_call(
            functools.partial(cut_last, pieces=3),
            out_shape=(VMEM((middle, units), BF16), VMEM((model - first - middle, units), BF16)),
            in_specs=[whole(SMEM), whole(HBM)],
            out_specs=(whole(),) * 2,
            scratch_shapes=[pltpu.SemaphoreType.DMA((4,))],
            compiler_params=params(4),
            cost_estimate=cost(0, 4 * (model - first) * units),
            name="cut_last",
        )(side, *keep_in(HBM, late))

    keys, values = pl.pallas_call(
        project_keys,
        out_shape=(HBM((group_rows, width), BF16),) * 2,
        in_specs=[whole()] * 3,
        out_specs=(whole(),) * 2,
        compiler_params=params(12),
        cost_estimate=cost(
            4 * group_rows * model * width, 2 * model * (group_rows + 2 * width)
        ),
        name="project_keys",
    )(*keep_in(HBM, normed, w_key, w_value))

    row_block = pl.BlockSpec((draft, width), lambda r, *_: (r, 0))
    fixed_block = pl.BlockSpec((fixed_count, width), lambda r, *_: (0, 0))
    matrix_block = pl.BlockSpec((1, heads, HD, HD), lambda r, *_: (r, 0, 0, 0))
    span_block = pl.BlockSpec((span, HD), lambda r, *_: (r, 0))
    own, retrieved, own_top, own_sum = pl.pallas_call(
        functools.partial(local_attention, heads=heads, draft=draft, scale=scale),
        grid=(reqs,),
        out_shape=(
            HBM((reqs * span, HD), F32),
            HBM((reqs * span, HD), F32),
            jax.ShapeDtypeStruct((reqs, LANES), F32),
            jax.ShapeDtypeStruct((reqs, LANES), F32),
        ),
        in_specs=[
            row_block,
            row_block,
            row_block,
            fixed_block,
            fixed_block,
            pl.BlockSpec((1, draft, draft), lambda r: (r, 0, 0)),
            matrix_block,
        ],
        out_specs=(span_block, span_block) + (pl.BlockSpec((reqs, LANES), lambda r: (0, 0)),) * 2,
        compiler_params=params(10),
        cost_estimate=cost(1, 1),
        name="local_attention",
    )(*keep_in(HBM, queries, keys, values, persist_keys, persist_values, tree_mask, memory))

    memory_out, momentum_out = pl.pallas_call(
        functools.partial(update_memory, reqs=reqs, draft=draft, heads=heads, steps=steps),
        out_shape=(HBM(memory.shape, F32),) * 2,
        in_specs=[whole(SMEM)] * 4 + [whole()] * 2 + [whole(HBM)] * 2,
        out_specs=(whole(HBM),) * 2,
        scratch_shapes=[
            pltpu.VMEM(memory.shape, F32),
            pltpu.VMEM(memory.shape, F32),
            pltpu.VMEM((draft, width), F32),
            pltpu.VMEM((draft, width), F32),
            pltpu.VMEM((LANES, HD), F32),
            pltpu.VMEM((heads * steps, HD), F32),
            pltpu.VMEM((HD, LANES), F32),
            pltpu.SemaphoreType.DMA((2, reqs)),
            pltpu.SemaphoreType.DMA((2, reqs)),
        ],
        compiler_params=params(16),
        cost_estimate=cost(
            14 * reqs * heads * HD * HD * steps * 8, 16 * reqs * heads * HD * HD
        ),
        name="update_memory",
    )(
        jnp.transpose(accept_path),
        accept_len,
        jnp.transpose(momentum_code, (1, 2, 0)),
        jnp.transpose(forget_code, (1, 2, 0)),
        *keep_in(HBM, keys, values, memory, momentum),
    )

    if pieces == 2:
        memory_out, momentum_out, half_mid, half_last, one_a, one_q = lax.optimization_barrier(
            (memory_out, momentum_out, half_mid, half_last, one_a, one_q)
        )
        other_core = [(i, i ^ 1) for i in range(n)]
        other_chip = [(i, i ^ 2) for i in range(n)]
        one_m = lax.ppermute(half_mid, "grp", swap)
        one_b = lax.ppermute(half_last, "grp", swap)
        three_q = lax.ppermute(one_q, "req", other_chip)
        two_a = lax.ppermute(one_a, "req", other_core)
        two_q = lax.ppermute(one_q, "req", other_core)
    asked, memory_out, momentum_out, keys, values = lax.optimization_barrier(
        (asked, memory_out, momentum_out, keys, values)
    )
    answers = pl.pallas_call(
        functools.partial(
            page_attention, n=n, cap=cap, draft=draft, heads=heads, page_len=page_len,
            scale=scale, group=2,
        ),
        out_shape=HBM((n * block, LANES), BF16),
        in_specs=[whole(), whole(HBM)],
        out_specs=whole(HBM),
        scratch_shapes=[
            pltpu.VMEM((n, cap) + kv_cache.shape[1:], BF16),
            pltpu.VMEM((n * block, LANES), BF16),
            pltpu.SemaphoreType.DMA((n,)),
            pltpu.SemaphoreType.DMA((n,)),
        ],
        compiler_params=params(24),
        cost_estimate=cost(
            4 * slots * span * page_len * HD,
            4 * slots * page_len * width + 4 * n * block * LANES,
            slots * span * page_len,
        ),
        name="page_attention",
    )(asked, *keep_in(HBM, kv_cache))
    if pieces == 2:
        answers, one_m = lax.optimization_barrier((answers, one_m))
        two_m = lax.ppermute(one_m, "req", other_core)
    returned = lax.all_to_all(answers, "req", split_axis=0, concat_axis=0, tiled=True)
    if pieces == 2:
        returned, one_b, two_a, two_m, two_q, three_q, own, retrieved, own_top, own_sum = (
            lax.optimization_barrier(
                (returned, one_b, two_a, two_m, two_q, three_q, own, retrieved, own_top, own_sum)
            )
        )
        two_b = lax.ppermute(one_b, "req", other_core)
        four_q = lax.ppermute(three_q, "req", other_core)
    rows = group_rows // grp
    mixed = pl.pallas_call(
        functools.partial(
            combine, n=n, cap=cap, reqs=reqs, draft=draft, heads=heads, pieces=pieces
        ),
        out_shape=(jax.ShapeDtypeStruct((group_rows // pieces, width), BF16),) * pieces,
        in_specs=[whole(SMEM)] * 2 + [whole()] + [whole(HBM)] * 2 + [whole()] * 2,
        out_specs=(whole(),) * pieces,
        scratch_shapes=[
            pltpu.VMEM((slots, LANES), F32),
            pltpu.VMEM((slots, LANES), F32),
            pltpu.VMEM((reqs, LANES), F32),
            pltpu.VMEM((reqs, LANES), F32),
            pltpu.VMEM((LANES, LANES), F32),
            pltpu.VMEM((LANES, LANES), F32),
            pltpu.VMEM((reqs * span, HD), F32),
            pltpu.VMEM((group_rows, width), BF16),
            pltpu.VMEM((reqs * span, HD), F32),
            pltpu.VMEM((reqs * span, HD), F32),
            pltpu.SemaphoreType.DMA((2,)),
        ],
        compiler_params=params(12),
        cost_estimate=cost(
            8 * slots * span * HD, 2 * n * block * LANES + 8 * reqs * span * HD
        ),
        name="combine",
    )(codes, side, returned, *keep_in(HBM, own, retrieved), own_top, own_sum)

    if pieces == 2:
        mine, asked_for = mixed
        theirs = lax.ppermute(asked_for, "grp", swap)
        mine, two_a, two_b, two_q, four_q = lax.optimization_barrier(
            (mine, two_a, two_b, two_q, four_q)
        )
        out_near, gate_up_near, down_near = pl.pallas_call(
            stage_weights,
            out_shape=(
                VMEM((2,) + w_out.shape, BF16),
                VMEM((2,) + w_gate_up.shape, BF16),
                VMEM((2,) + w_down.shape, BF16),
            ),
            in_specs=[whole(SMEM)] + [whole(pl.ANY)] * 13,
            out_specs=(whole(),) * 3,
            scratch_shapes=[pltpu.SemaphoreType.DMA((17,))],
            compiler_params=params(2),
            cost_estimate=cost(0, 2 * model * (2 * width + 6 * units)),
            name="stage_weights",
        )(
            side,
            *keep_in(HBM, w_out, w_gate_up, w_down, one_a, one_m, one_b, one_q, two_a, two_m),
            two_b,
            *keep_in(HBM, two_q, three_q),
            four_q,
        )
        layer_out = pl.pallas_call(
            feed_forward,
            out_shape=jax.ShapeDtypeStruct((rows, model), BF16),
            in_specs=[whole(SMEM)] + [whole()] * 7,
            out_specs=whole(),
            scratch_shapes=[
                pltpu.VMEM((rows, model), BF16),
                pltpu.VMEM((2, rows, units), BF16),
            ],
            compiler_params=params(14),
            cost_estimate=cost(
                4 * rows * model * (width + 3 * units), 4 * model * (width + 3 * units)
            ),
            name="feed_forward",
        )(
            side, tokens, mine, theirs, norm_ffn.reshape(1, -1),
            *keep_in(VMEM, out_near, gate_up_near, down_near),
        )
        return (layer_out, memory_out, momentum_out)

    partial_out = jnp.dot(mixed[0], w_out, preferred_element_type=F32).astype(BF16)
    head_sum = lax.psum_scatter(partial_out, "grp", scatter_dimension=0, tiled=True).astype(F32)
    own_rows = lax.dynamic_slice_in_dim(tokens, lax.axis_index("grp") * rows, rows, 0)
    residual = (own_rows.astype(F32) + head_sum).astype(BF16)
    ffn_in = rms_norm(residual, norm_ffn)
    piece = lax.all_gather(ffn_in, "grp", axis=0, tiled=True)
    gate = jnp.dot(piece, w_gate_up[0], preferred_element_type=F32)
    up = jnp.dot(piece, w_gate_up[1], preferred_element_type=F32)
    hidden = (jax.nn.silu(gate) * up).astype(BF16)
    ffn_out = lax.psum_scatter(
        jnp.dot(hidden, w_down, preferred_element_type=F32).astype(BF16),
        "grp",
        scatter_dimension=0,
        tiled=True,
    ).astype(F32)
    layer_out = (residual.astype(F32) + ffn_out).astype(BF16)
    return (layer_out, memory_out, momentum_out)


def solution(mesh):
    return jax.shard_map(
        on_device,
        mesh=mesh,
        in_specs=(
            P("req", None),
            P(),
            P(None, "grp"),
            P(None, "grp"),
            P(None, "grp"),
            P("grp", None),
            P(None, "grp"),
            P(None, "grp"),
            P("req", None, None, "grp"),
            P("req"),
            P("req"),
            P("req"),
            P("req", None, None),
            P("req", None),
            P("req"),
            P("req", "grp", None, None),
            P("req", "grp", None, None),
            P("req", None, "grp"),
            P("req", None, "grp"),
            P(),
            P(None, None, "grp"),
            P("grp", None),
        ),
        out_specs=(
            P(("req", "grp"), None),
            P("req", "grp", None, None),
            P("req", "grp", None, None),
        ),
        check_vma=False,
    )
```

```python
import functools
import math

import jax
import jax.numpy as jnp
from jax import lax
from jax.experimental import pallas as pl
from jax.experimental.pallas import tpu as pltpu
from jax.sharding import PartitionSpec as P

HD = 128
LANES = 128
EXTRA = 16
TOP_PARTS = 3
WEIGHT = 20
SUM_PARTS = 2

EPS = 1e-06
THETA = 0.5
NEG = -1e30

VMEM = pltpu.VMEM
SMEM = pltpu.SMEM
HBM = pltpu.HBM
F32 = jnp.float32
BF16 = jnp.bfloat16


def whole(space=VMEM):
    return pl.BlockSpec(memory_space=space)


def cost(flops, moved, special=0):
    return pl.CostEstimate(
        flops=WEIGHT * flops, bytes_accessed=WEIGHT * moved, transcendentals=special
    )


def keep_in(space, *arrays):
    return tuple(pltpu.with_memory_space_constraint(array, space) for array in arrays)


def params(mib=40):
    return pltpu.CompilerParams(vmem_limit_bytes=mib << 20)


def rms_norm(rows, gain):
    values = rows.astype(F32)
    factor = lax.rsqrt(jnp.mean(values * values, axis=-1, keepdims=True) + EPS)
    return (values * factor * gain).astype(BF16)


def nt_dot(left, right):
    return lax.dot_general(left, right, (((1,), (1,)), ((), ())), preferred_element_type=F32)


def column_to_row(column, count):
    row_id = lax.broadcasted_iota(jnp.int32, (count, LANES), 0)
    lane_id = lax.broadcasted_iota(jnp.int32, (count, LANES), 1)
    spread = jnp.where(row_id == lane_id, jnp.broadcast_to(column, (count, LANES)), 0.0)
    return jnp.sum(spread, axis=0, keepdims=True)


def split_parts(row, count):
    parts = []
    for _ in range(count):
        part = row.astype(BF16).astype(F32)
        parts.append(part)
        row = row - part
    return parts


def project_queries(tok_ref, gain_ref, w_ref, normed_ref, q_ref, turned_ref, *, reqs, draft, heads):
    normed_ref[...] = rms_norm(tok_ref[...], gain_ref[...])
    q_ref[...] = jnp.dot(normed_ref[...], w_ref[...], preferred_element_type=F32).astype(BF16)
    span = heads * draft
    for r in range(reqs):
        rows = slice(r * draft, (r + 1) * draft)
        pieces = [q_ref[rows, h * HD : (h + 1) * HD].astype(F32) for h in range(heads)]
        if span < LANES:
            pieces.append(jnp.zeros((LANES - span, HD), F32))
        tile = jnp.concatenate(pieces, axis=0)
        turned_ref[r * HD : (r + 1) * HD, :] = jnp.transpose(tile).astype(BF16)


def project_keys(normed_ref, wk_ref, wv_ref, k_ref, v_ref):
    normed = normed_ref[...]
    k_ref[...] = jnp.dot(normed, wk_ref[...], preferred_element_type=F32).astype(BF16)
    v_ref[...] = jnp.dot(normed, wv_ref[...], preferred_element_type=F32).astype(BF16)


def pack_queries(codes, lengths, turned_ref, out_hbm, out_ref, sems, *, n, cap, reqs, page_len):
    block = cap * HD + EXTRA
    row_id = lax.broadcasted_iota(jnp.int32, (EXTRA, LANES), 0)

    def departure(d):
        rows = pl.ds(pl.multiple_of(d * block, EXTRA), block)
        return pltpu.make_async_copy(out_ref.at[rows], out_hbm.at[rows], sems.at[d])

    def one(d, carry):
        base = pl.multiple_of(d * block, EXTRA)
        tail = jnp.zeros((EXTRA, LANES), F32)
        for c in range(cap):
            code = codes[d, 0, c]
            r = lax.rem(code, reqs)
            page = lax.div(code, reqs)
            live = jnp.clip(lengths[r] - page * page_len, 0, page_len)
            tail = jnp.where(row_id == c, live.astype(F32), tail)
            rows = pl.ds(pl.multiple_of(r * HD, HD), HD)
            out_ref[pl.ds(base + c * HD, HD), :] = turned_ref[rows, :]
        out_ref[pl.ds(base + cap * HD, EXTRA), :] = tail.astype(BF16)
        departure(d).start()
        return carry

    lax.fori_loop(0, n, one, 0)
    for d in range(n):
        departure(d).wait()


def page_attention(
    q_ref, kv_hbm, out_hbm, kv_buf, out_buf, in_sems, out_sems,
    *, n, cap, draft, heads, page_len, scale, group,
):
    span = heads * draft
    ask_block = cap * HD + EXTRA
    block = cap * span + EXTRA
    token = lax.broadcasted_iota(jnp.int32, (page_len, LANES), 0).astype(F32)
    row_id = lax.broadcasted_iota(jnp.int32, (EXTRA, LANES), 0)
    head_of = lax.broadcasted_iota(jnp.int32, (HD, LANES), 1) // draft

    def arrival(d):
        return pltpu.make_async_copy(
            kv_hbm.at[pl.ds(d * cap, cap)], kv_buf.at[d], in_sems.at[d]
        )

    def departure(d):
        rows = pl.ds(pl.multiple_of(d * block, EXTRA), block)
        return pltpu.make_async_copy(out_buf.at[rows], out_hbm.at[rows], out_sems.at[d])

    for d in range(n):
        arrival(d).start()

    def one(i, carry):
        pairs = [(i * group + g, c) for g in range(group) for c in range(cap)]
        limits = []
        for g in range(group):
            d = i * group + g
            arrival(d).wait()
            at = pl.multiple_of(d * ask_block + cap * HD, EXTRA)
            limits.append(q_ref[pl.ds(at, EXTRA), :].astype(F32))
        all_scores = []
        for d, c in pairs:
            at = pl.multiple_of(d * ask_block + c * HD, EXTRA)
            turned = q_ref[pl.ds(at, HD), :]
            blocks = [jnp.where(head_of == h, turned, jnp.zeros_like(turned)) for h in range(heads)]
            all_scores.append(
                jnp.dot(
                    kv_buf[d, c, 0], jnp.concatenate(blocks, axis=0), preferred_element_type=F32
                )
            )
        all_weights = []
        tails = [jnp.zeros((EXTRA, LANES), F32) for _ in range(group)]
        for j, (d, c) in enumerate(pairs):
            g = j // cap
            scores = jnp.where(token < limits[g][c : c + 1, :], all_scores[j] * scale, NEG)
            top = jnp.max(scores, axis=0, keepdims=True)
            weight = jnp.exp(scores - top)
            total = jnp.sum(weight, axis=0, keepdims=True)
            all_weights.append(jnp.transpose(weight).astype(BF16))
            parts = split_parts(top, TOP_PARTS) + split_parts(total, SUM_PARTS)
            for p, part in enumerate(parts):
                tails[g] = jnp.where(row_id == p * cap + c, part, tails[g])
        for j, (d, c) in enumerate(pairs):
            for h in range(heads):
                numer = jnp.dot(
                    all_weights[j][h * draft : (h + 1) * draft, :],
                    kv_buf[d, c, 1, :, h * HD : (h + 1) * HD],
                    preferred_element_type=F32,
                )
                at = pl.multiple_of(d * block + c * span + h * draft, EXTRA)
                out_buf[pl.ds(at, draft), :] = numer.astype(BF16)
        for g in range(group):
            d = i * group + g
            at = pl.multiple_of(d * block + cap * span, EXTRA)
            out_buf[pl.ds(at, EXTRA), :] = tails[g].astype(BF16)
            departure(d).start()
        return carry

    lax.fori_loop(0, n // group, one, 0)
    for d in range(n):
        departure(d).wait()


def local_attention(
    q_ref, k_ref, v_ref, pk_ref, pv_ref, mask_ref, mem_ref,
    o_ref, ret_ref, top_ref, sum_ref, *, heads, draft, scale,
):
    r = pl.program_id(0)
    seen = mask_ref[0] == 1
    tops, totals = [], []
    for h in range(heads):
        cols = slice(h * HD, (h + 1) * HD)
        rows = slice(h * draft, (h + 1) * draft)
        query = q_ref[:, cols]
        tree = jnp.where(seen, nt_dot(query, k_ref[:, cols]) * scale, NEG)
        fixed = nt_dot(query, pk_ref[:, cols]) * scale
        top = jnp.maximum(
            jnp.max(tree, axis=1, keepdims=True), jnp.max(fixed, axis=1, keepdims=True)
        )
        tree_w = jnp.exp(tree - top)
        fixed_w = jnp.exp(fixed - top)
        total = jnp.sum(tree_w, axis=1, keepdims=True) + jnp.sum(fixed_w, axis=1, keepdims=True)
        numer = jnp.dot(tree_w.astype(BF16), v_ref[:, cols], preferred_element_type=F32)
        numer = numer + jnp.dot(fixed_w.astype(BF16), pv_ref[:, cols], preferred_element_type=F32)
        o_ref[rows, :] = numer
        tops.append(top)
        totals.append(total)
        wide = query.astype(F32)
        unit = wide * lax.rsqrt(jnp.sum(wide * wide, axis=1, keepdims=True) + EPS)
        ret_ref[rows, :] = jnp.dot(
            unit, mem_ref[0, h], preferred_element_type=F32, precision=lax.Precision.HIGHEST
        )
    span = heads * draft
    top_ref[pl.ds(r, 1), :] = column_to_row(jnp.concatenate(tops, axis=0), span)
    sum_ref[pl.ds(r, 1), :] = column_to_row(jnp.concatenate(totals, axis=0), span)


def update_memory(
    path, count, mom_code, forget_code, k_ref, v_ref, mem_hbm, mom_hbm, mem_out, mom_out,
    mem_buf, mom_buf, wide_k, wide_v, unit_ref, value_ref, turned_ref, in_sems, out_sems,
    *, reqs, draft, heads, steps,
):
    def arrivals(r):
        return (
            pltpu.make_async_copy(mem_hbm.at[r], mem_buf.at[r], in_sems.at[0, r]),
            pltpu.make_async_copy(mom_hbm.at[r], mom_buf.at[r], in_sems.at[1, r]),
        )

    def departures(r):
        return (
            pltpu.make_async_copy(mem_buf.at[r], mem_out.at[r], out_sems.at[0, r]),
            pltpu.make_async_copy(mom_buf.at[r], mom_out.at[r], out_sems.at[1, r]),
        )

    for r in range(reqs):
        for copy in arrivals(r):
            copy.start()
    unit_ref[...] = jnp.zeros_like(unit_ref)

    def one(r, carry):
        rows = pl.ds(pl.multiple_of(r * draft, draft), draft)
        wide_k[...] = k_ref[rows, :].astype(F32)
        wide_v[...] = v_ref[rows, :].astype(F32)
        for n in range(steps):
            node = path[n, r]
            k_row = wide_k[pl.ds(node, 1), :]
            v_row = wide_v[pl.ds(node, 1), :]
            for h in range(heads):
                unit_ref[h * steps + n : h * steps + n + 1, :] = k_row[:, h * HD : (h + 1) * HD]
                value_ref[h * steps + n : h * steps + n + 1, :] = v_row[:, h * HD : (h + 1) * HD]
        keys = unit_ref[...]
        unit = keys * lax.rsqrt(jnp.sum(keys * keys, axis=1, keepdims=True) + EPS)
        turned_ref[...] = jnp.transpose(unit)
        for copy in arrivals(r):
            copy.wait()

        def advance(n):
            for h in range(heads):
                eta = 0.97 - 0.06 * mom_code[n, h, r].astype(F32)
                keep = 1.0 - (0.01 + 0.02 * forget_code[n, h, r].astype(F32))
                row = h * steps + n
                column = turned_ref[:, row : row + 1]
                matrix = mem_buf[r, h]
                predicted = jnp.sum(column * matrix, axis=0, keepdims=True)
                error = THETA * (predicted - value_ref[row : row + 1, :])
                moved = eta * mom_buf[r, h] - column * error
                mom_buf[r, h] = moved
                mem_buf[r, h] = keep * matrix + moved

        for n in range(steps):
            pl.when(n < count[r])(functools.partial(advance, n))
        for copy in departures(r):
            copy.start()
        return carry

    lax.fori_loop(0, reqs, one, 0)
    for r in range(reqs):
        for copy in departures(r):
            copy.wait()


def combine(
    codes, side, msg_ref, o_hbm, ret_hbm, own_top_ref, own_sum_ref, *rest,
    n, cap, reqs, draft, heads, pieces,
):
    outs = rest[:pieces]
    part_top, part_sum, best, total, weight, own_weight, acc, mixed, o_ref, ret_ref, sems = rest[
        pieces:
    ]
    copies = [
        pltpu.make_async_copy(o_hbm, o_ref, sems.at[0]),
        pltpu.make_async_copy(ret_hbm, ret_ref, sems.at[1]),
    ]
    for copy in copies:
        copy.start()
    span = heads * draft
    block = cap * span + EXTRA
    slots = n * cap
    for d in range(n):
        at = d * block + cap * span
        tail = msg_ref[at : at + EXTRA, :].astype(F32)
        rows = [tail[p * cap : (p + 1) * cap] for p in range(TOP_PARTS + SUM_PARTS)]
        part_top[d * cap : (d + 1) * cap, :] = rows[0] + rows[1] + rows[2]
        part_sum[d * cap : (d + 1) * cap, :] = rows[3] + rows[4]
    best[...] = own_top_ref[...]
    owners = [lax.rem(codes[s // cap, 0, s % cap], reqs) for s in range(slots)]
    for s in range(slots):
        r = owners[s]
        best[pl.ds(r, 1), :] = jnp.maximum(best[pl.ds(r, 1), :], part_top[s : s + 1, :])
    own_weight[...] = jnp.zeros_like(own_weight)
    weight[...] = jnp.zeros_like(weight)
    start = jnp.exp(own_top_ref[...] - best[...])
    total[...] = start * own_sum_ref[...]
    for s in range(slots):
        r = owners[s]
        term = jnp.exp(part_top[s : s + 1, :] - best[pl.ds(r, 1), :])
        weight[s : s + 1, :] = term
        total[pl.ds(r, 1), :] = total[pl.ds(r, 1), :] + term * part_sum[s : s + 1, :]
    inverse = 1.0 / total[...]
    own_weight[0:reqs, :] = start * inverse
    total[...] = inverse
    for s in range(slots):
        weight[s : s + 1, :] = weight[s : s + 1, :] * total[pl.ds(owners[s], 1), :]
    turned = jnp.transpose(weight[...])
    own_turned = jnp.transpose(own_weight[...])
    for copy in copies:
        copy.wait()
    for r in range(reqs):
        rows = slice(r * span, (r + 1) * span)
        acc[rows, :] = o_ref[rows, :] * own_turned[0:span, r : r + 1] + ret_ref[rows, :]
    for s in range(slots):
        at = (s // cap) * block + (s % cap) * span
        rows = pl.ds(pl.multiple_of(owners[s] * span, span), span)
        acc[rows, :] = acc[rows, :] + msg_ref[at : at + span, :].astype(F32) * turned[
            0:span, s : s + 1
        ]
    for r in range(reqs):
        for h in range(heads):
            at = r * span + h * draft
            mixed[r * draft : (r + 1) * draft, h * HD : (h + 1) * HD] = acc[
                at : at + draft, :
            ].astype(BF16)
    rows = reqs * draft // pieces
    for p, out_ref in enumerate(outs):
        first = lax.rem(side[0] + p, pieces) * rows
        out_ref[...] = mixed[pl.ds(pl.multiple_of(first, rows), rows), :]


def run_copies(pairs, sems):
    copies = [
        pltpu.make_async_copy(source, target, sems.at[i])
        for i, (source, target) in enumerate(pairs)
    ]
    for copy in copies:
        copy.start()
    return copies


def cut_first(side, gate_up_w, down_w, out_w, first_ref, near_ref, far_ref, sems):
    depth, width = down_w.shape[0] // 4, out_w.shape[0] // 4
    near = near_ref.shape[0]
    base = pl.multiple_of(side[2] * depth, EXTRA)
    out_rows = pl.ds(pl.multiple_of(side[2] * width, EXTRA), width)
    pairs = [
        (out_w.at[out_rows], far_ref.at[pl.ds(depth - near, width)]),
        (down_w.at[pl.ds(base + near, depth - near)], far_ref.at[pl.ds(0, depth - near)]),
    ]
    step = near // 3
    for i in range(3):
        pairs.append((down_w.at[pl.ds(base + i * step, step)], near_ref.at[pl.ds(i * step, step)]))
    step = first_ref.shape[0] // 4
    for i in range(4):
        rows = pl.ds(i * step, step)
        pairs.append((gate_up_w.at[side[1], rows], first_ref.at[rows]))
    for copy in run_copies(pairs, sems):
        copy.wait()


def cut_last(side, gate_up_w, mid_ref, last_ref, sems, *, pieces):
    step = last_ref.shape[0] // pieces
    start = gate_up_w.shape[1] - last_ref.shape[0]
    half = gate_up_w.at[side[1]]
    middle = mid_ref.shape[0]
    pairs = [(half.at[pl.ds(start - middle, middle)], mid_ref)]
    for i in range(pieces):
        pairs.append((half.at[pl.ds(start + i * step, step)], last_ref.at[pl.ds(i * step, step)]))
    for copy in run_copies(pairs, sems):
        copy.wait()


def stage_weights(
    side, out_w, gate_up_w, down_w, one_a, one_m, one_b, one_q, one_r, two_a, two_m, two_q, two_r,
    three_q, three_r, four_q, two_b, four_r, out_all, gate_up_all, down_all, sems,
):
    width, depth = out_w.shape[0] // 4, down_w.shape[0] // 4
    pairs = [(gate_up_w, gate_up_all.at[0]), (down_w, down_all.at[0]), (out_w, out_all.at[0])]
    for half, parts in ((side[1], (one_a, one_m, one_b)), (1 - side[1], (two_a, two_m, two_b))):
        at = 0
        for part in parts:
            pairs.append((part, gate_up_all.at[1, half, pl.ds(at, part.shape[0])]))
            at += part.shape[0]
    core, chip = side[1], side[2] // 2
    near = one_q.shape[0]
    places = ((core, chip), (1 - core, chip), (core, 1 - chip), (1 - core, 1 - chip))
    got = ((one_q, one_r), (two_q, two_r), (three_q, three_r), (four_q, four_r))
    for (x, y), (q, r) in zip(places, got):
        base = pl.multiple_of((2 * y + x) * depth, EXTRA)
        rows = pl.ds(pl.multiple_of((2 * y + x) * width, EXTRA), width)
        pairs.append((q, down_all.at[1, pl.ds(base, near)]))
        pairs.append(
            (r.at[pl.ds(0, depth - near)], down_all.at[1, pl.ds(base + near, depth - near)])
        )
        pairs.append((r.at[pl.ds(depth - near, width)], out_all.at[1, rows]))
    for copy in run_copies(pairs, sems):
        copy.wait()


def feed_forward(
    side, tok_ref, mine_ref, theirs_ref, gain_ref, out_w, gate_up_w, down_w, out_ref,
    residual, hidden,
):
    rows = mine_ref.shape[0]
    units = gate_up_w.shape[3]
    tokens = tok_ref[pl.ds(pl.multiple_of(side[0] * rows, rows), rows), :].astype(F32)
    summed = tokens + jnp.dot(mine_ref[...], out_w[0], preferred_element_type=F32)
    summed = summed + jnp.dot(theirs_ref[...], out_w[1], preferred_element_type=F32)
    residual[...] = summed.astype(BF16)
    ffn_in = rms_norm(residual[...], gain_ref[...])
    step = 256
    for half in range(2):
        for first in range(0, units, step):
            cols = slice(first, min(first + step, units))
            gate = jnp.dot(ffn_in, gate_up_w[half, 0, :, cols], preferred_element_type=F32)
            up = jnp.dot(ffn_in, gate_up_w[half, 1, :, cols], preferred_element_type=F32)
            hidden[half, :, cols] = (gate / (1.0 + jnp.exp(-gate)) * up).astype(BF16)
    for at in range(0, out_ref.shape[1], step):
        cols = slice(at, at + step)
        total = residual[:, cols].astype(F32)
        for half in range(2):
            total = total + jnp.dot(hidden[half], down_w[half, :, cols], preferred_element_type=F32)
        out_ref[:, cols] = total.astype(BF16)


def on_device(
    tokens,
    norm_attn,
    w_query,
    w_key,
    w_value,
    w_out,
    persist_keys,
    persist_values,
    kv_cache,
    slot_request,
    slot_page,
    cache_len,
    tree_mask,
    accept_path,
    accept_len,
    memory,
    momentum,
    momentum_code,
    forget_code,
    norm_ffn,
    w_gate_up,
    w_down,
):
    n = lax.axis_size("req")
    group_rows, model = tokens.shape
    reqs = cache_len.shape[0]
    draft = tree_mask.shape[1]
    steps = accept_path.shape[1]
    width = w_query.shape[1]
    heads = width // HD
    span = heads * draft
    slots = kv_cache.shape[0]
    cap = slots // n
    fixed_count = persist_keys.shape[0]
    page_len = kv_cache.shape[2]
    ask_block = cap * HD + EXTRA
    block = cap * span + EXTRA
    scale = 1.0 / math.sqrt(HD)

    label = (slot_page * reqs + lax.rem(slot_request, reqs)).reshape(n, 1, cap)
    codes = lax.all_to_all(label, "req", split_axis=0, concat_axis=0, tiled=True)

    grp = lax.axis_size("grp")
    depth, out_depth = w_down.shape[0] // 4, width // 4
    first, middle = model // 4, model * 3 // 16
    near = (depth + out_depth) // 2 // 48 * 48
    split = (depth, out_depth, first // 4, middle, (model - first - middle) // 3)
    pieces = 2 if grp == 2 and n % 4 == 0 and not any(size % EXTRA for size in split) else 1
    quarter = lax.rem(lax.axis_index("req"), 4)
    core = lax.rem(quarter, 2)
    side = jnp.stack([lax.axis_index("grp"), core, quarter]).astype(jnp.int32)
    if pieces == 2:
        units = w_down.shape[0]
        half_first, near_part, far_part = pl.pallas_call(
            cut_first,
            out_shape=(
                VMEM((first, units), BF16),
                VMEM((near, model), BF16),
                VMEM((depth + out_depth - near, model), BF16),
            ),
            in_specs=[whole(SMEM)] + [whole(HBM)] * 3,
            out_specs=(whole(),) * 3,
            scratch_shapes=[pltpu.SemaphoreType.DMA((9,))],
            compiler_params=params(4),
            cost_estimate=cost(0, 4 * (first * units + (depth + out_depth) * model)),
            name="cut_first",
        )(side, *keep_in(HBM, w_gate_up, w_down, w_out))

    normed, queries, turned = pl.pallas_call(
        functools.partial(project_queries, reqs=reqs, draft=draft, heads=heads),
        out_shape=(
            HBM((group_rows, model), BF16),
            HBM((group_rows, width), BF16),
            jax.ShapeDtypeStruct((reqs * HD, LANES), BF16),
        ),
        in_specs=[whole()] * 3,
        out_specs=(whole(),) * 3,
        compiler_params=params(12),
        cost_estimate=cost(
            2 * group_rows * model * width, 2 * model * (2 * group_rows + width)
        ),
        name="project_queries",
    )(*keep_in(HBM, tokens, norm_attn.reshape(1, -1), w_query))

    if pieces == 2:
        turned, half_first, near_part, far_part = lax.optimization_barrier(
            (turned, half_first, near_part, far_part)
        )
        swap = [(0, 1), (1, 0)]
        one_a = lax.ppermute(half_first, "grp", swap)
        one_q = lax.ppermute(near_part, "grp", swap)
        one_r = lax.ppermute(far_part, "grp", swap)

    packed = pl.pallas_call(
        functools.partial(pack_queries, n=n, cap=cap, reqs=reqs, page_len=page_len),
        out_shape=HBM((n * ask_block, LANES), BF16),
        in_specs=[whole(SMEM), whole(SMEM), whole()],
        out_specs=whole(HBM),
        scratch_shapes=[
            pltpu.VMEM((n * ask_block, LANES), BF16),
            pltpu.SemaphoreType.DMA((n,)),
        ],
        compiler_params=params(8),
        cost_estimate=cost(0, 4 * n * ask_block * LANES),
        name="pack_queries",
    )(codes, *keep_in(HBM, cache_len), turned)
    packed, normed, late = lax.optimization_barrier((packed, normed, w_gate_up))
    asked = lax.all_to_all(packed, "req", split_axis=0, concat_axis=0, tiled=True)

    if pieces == 2:
        half_mid, half_last = pl.pallas_call(
            functools.partial(cut_last, pieces=3),
            out_shape=(VMEM((middle, units), BF16), VMEM((model - first - middle, units), BF16)),
            in_specs=[whole(SMEM), whole(HBM)],
            out_specs=(whole(),) * 2,
            scratch_shapes=[pltpu.SemaphoreType.DMA((4,))],
            compiler_params=params(4),
            cost_estimate=cost(0, 4 * (model - first) * units),
            name="cut_last",
        )(side, *keep_in(HBM, late))

    keys, values = pl.pallas_call(
        project_keys,
        out_shape=(HBM((group_rows, width), BF16),) * 2,
        in_specs=[whole()] * 3,
        out_specs=(whole(),) * 2,
        compiler_params=params(12),
        cost_estimate=cost(
            4 * group_rows * model * width, 2 * model * (group_rows + 2 * width)
        ),
        name="project_keys",
    )(*keep_in(HBM, normed, w_key, w_value))

    row_block = pl.BlockSpec((draft, width), lambda r, *_: (r, 0))
    fixed_block = pl.BlockSpec((fixed_count, width), lambda r, *_: (0, 0))
    matrix_block = pl.BlockSpec((1, heads, HD, HD), lambda r, *_: (r, 0, 0, 0))
    span_block = pl.BlockSpec((span, HD), lambda r, *_: (r, 0))
    own, retrieved, own_top, own_sum = pl.pallas_call(
        functools.partial(local_attention, heads=heads, draft=draft, scale=scale),
        grid=(reqs,),
        out_shape=(
            HBM((reqs * span, HD), F32),
            HBM((reqs * span, HD), F32),
            jax.ShapeDtypeStruct((reqs, LANES), F32),
            jax.ShapeDtypeStruct((reqs, LANES), F32),
        ),
        in_specs=[
            row_block,
            row_block,
            row_block,
            fixed_block,
            fixed_block,
            pl.BlockSpec((1, draft, draft), lambda r: (r, 0, 0)),
            matrix_block,
        ],
        out_specs=(span_block, span_block) + (pl.BlockSpec((reqs, LANES), lambda r: (0, 0)),) * 2,
        compiler_params=params(10),
        cost_estimate=cost(1, 1),
        name="local_attention",
    )(*keep_in(HBM, queries, keys, values, persist_keys, persist_values, tree_mask, memory))

    memory_out, momentum_out = pl.pallas_call(
        functools.partial(update_memory, reqs=reqs, draft=draft, heads=heads, steps=steps),
        out_shape=(HBM(memory.shape, F32),) * 2,
        in_specs=[whole(SMEM)] * 4 + [whole()] * 2 + [whole(HBM)] * 2,
        out_specs=(whole(HBM),) * 2,
        scratch_shapes=[
            pltpu.VMEM(memory.shape, F32),
            pltpu.VMEM(memory.shape, F32),
            pltpu.VMEM((draft, width), F32),
            pltpu.VMEM((draft, width), F32),
            pltpu.VMEM((LANES, HD), F32),
            pltpu.VMEM((heads * steps, HD), F32),
            pltpu.VMEM((HD, LANES), F32),
            pltpu.SemaphoreType.DMA((2, reqs)),
            pltpu.SemaphoreType.DMA((2, reqs)),
        ],
        compiler_params=params(16),
        cost_estimate=cost(
            14 * reqs * heads * HD * HD * steps * 8, 16 * reqs * heads * HD * HD
        ),
        name="update_memory",
    )(
        jnp.transpose(accept_path),
        accept_len,
        jnp.transpose(momentum_code, (1, 2, 0)),
        jnp.transpose(forget_code, (1, 2, 0)),
        *keep_in(HBM, keys, values, memory, momentum),
    )

    if pieces == 2:
        memory_out, momentum_out, half_mid, half_last, one_a, one_q, one_r = (
            lax.optimization_barrier(
                (memory_out, momentum_out, half_mid, half_last, one_a, one_q, one_r)
            )
        )
        other_core = [(i, i ^ 1) for i in range(n)]
        other_chip = [(i, i ^ 2) for i in range(n)]
        one_m = lax.ppermute(half_mid, "grp", swap)
        one_b = lax.ppermute(half_last, "grp", swap)
        three_q = lax.ppermute(one_q, "req", other_chip)
        three_r = lax.ppermute(one_r, "req", other_chip)
    asked, memory_out, momentum_out, keys, values = lax.optimization_barrier(
        (asked, memory_out, momentum_out, keys, values)
    )
    answers = pl.pallas_call(
        functools.partial(
            page_attention, n=n, cap=cap, draft=draft, heads=heads, page_len=page_len,
            scale=scale, group=2,
        ),
        out_shape=HBM((n * block, LANES), BF16),
        in_specs=[whole(), whole(HBM)],
        out_specs=whole(HBM),
        scratch_shapes=[
            pltpu.VMEM((n, cap) + kv_cache.shape[1:], BF16),
            pltpu.VMEM((n * block, LANES), BF16),
            pltpu.SemaphoreType.DMA((n,)),
            pltpu.SemaphoreType.DMA((n,)),
        ],
        compiler_params=params(24),
        cost_estimate=cost(
            4 * slots * span * page_len * HD,
            4 * slots * page_len * width + 4 * n * block * LANES,
            slots * span * page_len,
        ),
        name="page_attention",
    )(asked, *keep_in(HBM, kv_cache))
    if pieces == 2:
        answers, one_m, three_q = lax.optimization_barrier((answers, one_m, three_q))
        own, one_a, one_m, one_q, one_r, three_q = lax.optimization_barrier(
            (own, one_a, one_m, one_q, one_r, three_q)
        )
        two_a, two_m, two_q, two_r, four_q = (
            lax.ppermute(part, "req", other_core) for part in (one_a, one_m, one_q, one_r, three_q)
        )
    returned = lax.all_to_all(answers, "req", split_axis=0, concat_axis=0, tiled=True)
    if pieces == 2:
        returned, one_b, two_a, two_m, two_q, four_q, two_r, three_r, own, retrieved = (
            lax.optimization_barrier(
                (returned, one_b, two_a, two_m, two_q, four_q, two_r, three_r, own, retrieved)
            )
        )
        two_b = lax.ppermute(one_b, "req", other_core)
        four_r = lax.ppermute(three_r, "req", other_core)
    rows = group_rows // grp
    mixed = pl.pallas_call(
        functools.partial(
            combine, n=n, cap=cap, reqs=reqs, draft=draft, heads=heads, pieces=pieces
        ),
        out_shape=(jax.ShapeDtypeStruct((group_rows // pieces, width), BF16),) * pieces,
        in_specs=[whole(SMEM)] * 2 + [whole()] + [whole(HBM)] * 2 + [whole()] * 2,
        out_specs=(whole(),) * pieces,
        scratch_shapes=[
            pltpu.VMEM((slots, LANES), F32),
            pltpu.VMEM((slots, LANES), F32),
            pltpu.VMEM((reqs, LANES), F32),
            pltpu.VMEM((reqs, LANES), F32),
            pltpu.VMEM((LANES, LANES), F32),
            pltpu.VMEM((LANES, LANES), F32),
            pltpu.VMEM((reqs * span, HD), F32),
            pltpu.VMEM((group_rows, width), BF16),
            pltpu.VMEM((reqs * span, HD), F32),
            pltpu.VMEM((reqs * span, HD), F32),
            pltpu.SemaphoreType.DMA((2,)),
        ],
        compiler_params=params(12),
        cost_estimate=cost(
            8 * slots * span * HD, 2 * n * block * LANES + 8 * reqs * span * HD
        ),
        name="combine",
    )(codes, side, returned, *keep_in(HBM, own, retrieved), own_top, own_sum)

    if pieces == 2:
        mine, asked_for = mixed
        theirs = lax.ppermute(asked_for, "grp", swap)
        mine, two_b, four_r = lax.optimization_barrier((mine, two_b, four_r))
        out_near, gate_up_near, down_near = pl.pallas_call(
            stage_weights,
            out_shape=(
                VMEM((2,) + w_out.shape, BF16),
                VMEM((2,) + w_gate_up.shape, BF16),
                VMEM((2,) + w_down.shape, BF16),
            ),
            in_specs=[whole(SMEM)] + [whole(pl.ANY)] * 17,
            out_specs=(whole(),) * 3,
            scratch_shapes=[pltpu.SemaphoreType.DMA((21,))],
            compiler_params=params(2),
            cost_estimate=cost(0, 2 * model * (2 * width + 6 * units)),
            name="stage_weights",
        )(
            side,
            *keep_in(
                HBM, w_out, w_gate_up, w_down, one_a, one_m, one_b, one_q, one_r, two_a, two_m, two_q,
                two_r, three_q, three_r, four_q,
            ),
            two_b,
            four_r,
        )
        layer_out = pl.pallas_call(
            feed_forward,
            out_shape=jax.ShapeDtypeStruct((rows, model), BF16),
            in_specs=[whole(SMEM)] + [whole()] * 7,
            out_specs=whole(),
            scratch_shapes=[
                pltpu.VMEM((rows, model), BF16),
                pltpu.VMEM((2, rows, units), BF16),
            ],
            compiler_params=params(14),
            cost_estimate=cost(
                4 * rows * model * (width + 3 * units), 4 * model * (width + 3 * units)
            ),
            name="feed_forward",
        )(
            side, tokens, mine, theirs, norm_ffn.reshape(1, -1),
            *keep_in(VMEM, out_near, gate_up_near, down_near),
        )
        return (layer_out, memory_out, momentum_out)

    partial_out = jnp.dot(mixed[0], w_out, preferred_element_type=F32).astype(BF16)
    head_sum = lax.psum_scatter(partial_out, "grp", scatter_dimension=0, tiled=True).astype(F32)
    own_rows = lax.dynamic_slice_in_dim(tokens, lax.axis_index("grp") * rows, rows, 0)
    residual = (own_rows.astype(F32) + head_sum).astype(BF16)
    ffn_in = rms_norm(residual, norm_ffn)
    piece = lax.all_gather(ffn_in, "grp", axis=0, tiled=True)
    gate = jnp.dot(piece, w_gate_up[0], preferred_element_type=F32)
    up = jnp.dot(piece, w_gate_up[1], preferred_element_type=F32)
    hidden = (jax.nn.silu(gate) * up).astype(BF16)
    ffn_out = lax.psum_scatter(
        jnp.dot(hidden, w_down, preferred_element_type=F32).astype(BF16),
        "grp",
        scatter_dimension=0,
        tiled=True,
    ).astype(F32)
    layer_out = (residual.astype(F32) + ffn_out).astype(BF16)
    return (layer_out, memory_out, momentum_out)


def solution(mesh):
    return jax.shard_map(
        on_device,
        mesh=mesh,
        in_specs=(
            P("req", None),
            P(),
            P(None, "grp"),
            P(None, "grp"),
            P(None, "grp"),
            P("grp", None),
            P(None, "grp"),
            P(None, "grp"),
            P("req", None, None, "grp"),
            P("req"),
            P("req"),
            P("req"),
            P("req", None, None),
            P("req", None),
            P("req"),
            P("req", "grp", None, None),
            P("req", "grp", None, None),
            P("req", None, "grp"),
            P("req", None, "grp"),
            P(),
            P(None, None, "grp"),
            P("grp", None),
        ),
        out_specs=(
            P(("req", "grp"), None),
            P("req", "grp", None, None),
            P("req", "grp", None, None),
        ),
        check_vma=False,
    )
```

```python
import functools
import math

import jax
import jax.numpy as jnp
from jax import lax
from jax.experimental import pallas as pl
from jax.experimental.pallas import tpu as pltpu
from jax.sharding import PartitionSpec as P

HD = 128
LANES = 128
EXTRA = 16
TOP_PARTS = 3
WEIGHT = 20
SUM_PARTS = 2

EPS = 1e-06
THETA = 0.5
NEG = -1e30

VMEM = pltpu.VMEM
SMEM = pltpu.SMEM
HBM = pltpu.HBM
F32 = jnp.float32
BF16 = jnp.bfloat16


def whole(space=VMEM):
    return pl.BlockSpec(memory_space=space)


def cost(flops, moved, special=0):
    return pl.CostEstimate(
        flops=WEIGHT * flops, bytes_accessed=WEIGHT * moved, transcendentals=special
    )


def keep_in(space, *arrays):
    return tuple(pltpu.with_memory_space_constraint(array, space) for array in arrays)


def params(mib=40):
    return pltpu.CompilerParams(vmem_limit_bytes=mib << 20)


def rms_norm(rows, gain):
    values = rows.astype(F32)
    factor = lax.rsqrt(jnp.mean(values * values, axis=-1, keepdims=True) + EPS)
    return (values * factor * gain).astype(BF16)


def nt_dot(left, right):
    return lax.dot_general(left, right, (((1,), (1,)), ((), ())), preferred_element_type=F32)


def column_to_row(column, count):
    row_id = lax.broadcasted_iota(jnp.int32, (count, LANES), 0)
    lane_id = lax.broadcasted_iota(jnp.int32, (count, LANES), 1)
    spread = jnp.where(row_id == lane_id, jnp.broadcast_to(column, (count, LANES)), 0.0)
    return jnp.sum(spread, axis=0, keepdims=True)


def split_parts(row, count):
    parts = []
    for _ in range(count):
        part = row.astype(BF16).astype(F32)
        parts.append(part)
        row = row - part
    return parts


def project_queries(*refs, reqs, draft, heads, cut):
    copies = []
    if cut:
        side, gate_up_w, down_w, out_w, *refs, sems = refs
        *refs, first_ref, quarter_ref = refs
        copies = run_copies(
            first_pairs(side, gate_up_w, down_w, out_w, first_ref, quarter_ref), sems
        )
    tok_ref, gain_ref, w_ref, normed_ref, q_ref, turned_ref = refs
    normed_ref[...] = rms_norm(tok_ref[...], gain_ref[...])
    q_ref[...] = jnp.dot(normed_ref[...], w_ref[...], preferred_element_type=F32).astype(BF16)
    span = heads * draft
    for r in range(reqs):
        rows = slice(r * draft, (r + 1) * draft)
        pieces = [q_ref[rows, h * HD : (h + 1) * HD].astype(F32) for h in range(heads)]
        if span < LANES:
            pieces.append(jnp.zeros((LANES - span, HD), F32))
        tile = jnp.concatenate(pieces, axis=0)
        turned_ref[r * HD : (r + 1) * HD, :] = jnp.transpose(tile).astype(BF16)
    for copy in copies:
        copy.wait()


def project_keys(normed_ref, wk_ref, wv_ref, k_ref, v_ref):
    normed = normed_ref[...]
    k_ref[...] = jnp.dot(normed, wk_ref[...], preferred_element_type=F32).astype(BF16)
    v_ref[...] = jnp.dot(normed, wv_ref[...], preferred_element_type=F32).astype(BF16)


def pack_queries(codes, lengths, turned_ref, out_hbm, out_ref, sems, *, n, cap, reqs, page_len):
    block = cap * HD + EXTRA
    row_id = lax.broadcasted_iota(jnp.int32, (EXTRA, LANES), 0)

    def departure(d):
        rows = pl.ds(pl.multiple_of(d * block, EXTRA), block)
        return pltpu.make_async_copy(out_ref.at[rows], out_hbm.at[rows], sems.at[d])

    def one(d, carry):
        base = pl.multiple_of(d * block, EXTRA)
        tail = jnp.zeros((EXTRA, LANES), F32)
        for c in range(cap):
            code = codes[d, 0, c]
            r = lax.rem(code, reqs)
            page = lax.div(code, reqs)
            live = jnp.clip(lengths[r] - page * page_len, 0, page_len)
            tail = jnp.where(row_id == c, live.astype(F32), tail)
            rows = pl.ds(pl.multiple_of(r * HD, HD), HD)
            out_ref[pl.ds(base + c * HD, HD), :] = turned_ref[rows, :]
        out_ref[pl.ds(base + cap * HD, EXTRA), :] = tail.astype(BF16)
        departure(d).start()
        return carry

    lax.fori_loop(0, n, one, 0)
    for d in range(n):
        departure(d).wait()


def page_attention(
    q_ref, kv_hbm, out_hbm, kv_buf, out_buf, in_sems, out_sems,
    *, n, cap, draft, heads, page_len, scale, group,
):
    span = heads * draft
    ask_block = cap * HD + EXTRA
    block = cap * span + EXTRA
    token = lax.broadcasted_iota(jnp.int32, (page_len, LANES), 0).astype(F32)
    row_id = lax.broadcasted_iota(jnp.int32, (EXTRA, LANES), 0)
    head_of = lax.broadcasted_iota(jnp.int32, (HD, LANES), 1) // draft

    def arrival(d):
        return pltpu.make_async_copy(
            kv_hbm.at[pl.ds(d * cap, cap)], kv_buf.at[d], in_sems.at[d]
        )

    def departure(d):
        rows = pl.ds(pl.multiple_of(d * block, EXTRA), block)
        return pltpu.make_async_copy(out_buf.at[rows], out_hbm.at[rows], out_sems.at[d])

    for d in range(n):
        arrival(d).start()

    def one(i, carry):
        pairs = [(i * group + g, c) for g in range(group) for c in range(cap)]
        limits = []
        for g in range(group):
            d = i * group + g
            arrival(d).wait()
            at = pl.multiple_of(d * ask_block + cap * HD, EXTRA)
            limits.append(q_ref[pl.ds(at, EXTRA), :].astype(F32))
        all_scores = []
        for d, c in pairs:
            at = pl.multiple_of(d * ask_block + c * HD, EXTRA)
            turned = q_ref[pl.ds(at, HD), :]
            blocks = [jnp.where(head_of == h, turned, jnp.zeros_like(turned)) for h in range(heads)]
            all_scores.append(
                jnp.dot(
                    kv_buf[d, c, 0], jnp.concatenate(blocks, axis=0), preferred_element_type=F32
                )
            )
        all_weights = []
        tails = [jnp.zeros((EXTRA, LANES), F32) for _ in range(group)]
        for j, (d, c) in enumerate(pairs):
            g = j // cap
            scores = jnp.where(token < limits[g][c : c + 1, :], all_scores[j] * scale, NEG)
            top = jnp.max(scores, axis=0, keepdims=True)
            weight = jnp.exp(scores - top)
            total = jnp.sum(weight, axis=0, keepdims=True)
            all_weights.append(jnp.transpose(weight).astype(BF16))
            parts = split_parts(top, TOP_PARTS) + split_parts(total, SUM_PARTS)
            for p, part in enumerate(parts):
                tails[g] = jnp.where(row_id == p * cap + c, part, tails[g])
        for j, (d, c) in enumerate(pairs):
            for h in range(heads):
                numer = jnp.dot(
                    all_weights[j][h * draft : (h + 1) * draft, :],
                    kv_buf[d, c, 1, :, h * HD : (h + 1) * HD],
                    preferred_element_type=F32,
                )
                at = pl.multiple_of(d * block + c * span + h * draft, EXTRA)
                out_buf[pl.ds(at, draft), :] = numer.astype(BF16)
        for g in range(group):
            d = i * group + g
            at = pl.multiple_of(d * block + cap * span, EXTRA)
            out_buf[pl.ds(at, EXTRA), :] = tails[g].astype(BF16)
            departure(d).start()
        return carry

    lax.fori_loop(0, n // group, one, 0)
    for d in range(n):
        departure(d).wait()


def local_attention(
    q_ref, k_ref, v_ref, pk_ref, pv_ref, mask_ref, mem_ref,
    o_ref, ret_ref, top_ref, sum_ref, *, heads, draft, scale,
):
    r = pl.program_id(0)
    seen = mask_ref[0] == 1
    tops, totals = [], []
    for h in range(heads):
        cols = slice(h * HD, (h + 1) * HD)
        rows = slice(h * draft, (h + 1) * draft)
        query = q_ref[:, cols]
        tree = jnp.where(seen, nt_dot(query, k_ref[:, cols]) * scale, NEG)
        fixed = nt_dot(query, pk_ref[:, cols]) * scale
        top = jnp.maximum(
            jnp.max(tree, axis=1, keepdims=True), jnp.max(fixed, axis=1, keepdims=True)
        )
        tree_w = jnp.exp(tree - top)
        fixed_w = jnp.exp(fixed - top)
        total = jnp.sum(tree_w, axis=1, keepdims=True) + jnp.sum(fixed_w, axis=1, keepdims=True)
        numer = jnp.dot(tree_w.astype(BF16), v_ref[:, cols], preferred_element_type=F32)
        numer = numer + jnp.dot(fixed_w.astype(BF16), pv_ref[:, cols], preferred_element_type=F32)
        o_ref[rows, :] = numer
        tops.append(top)
        totals.append(total)
        wide = query.astype(F32)
        unit = wide * lax.rsqrt(jnp.sum(wide * wide, axis=1, keepdims=True) + EPS)
        ret_ref[rows, :] = jnp.dot(
            unit, mem_ref[0, h], preferred_element_type=F32, precision=lax.Precision.HIGHEST
        )
    span = heads * draft
    top_ref[pl.ds(r, 1), :] = column_to_row(jnp.concatenate(tops, axis=0), span)
    sum_ref[pl.ds(r, 1), :] = column_to_row(jnp.concatenate(totals, axis=0), span)


def update_memory(
    path, count, mom_code, forget_code, k_ref, v_ref, mem_hbm, mom_hbm, mem_out, mom_out,
    mem_buf, mom_buf, wide_k, wide_v, unit_ref, value_ref, turned_ref, in_sems, out_sems,
    *, reqs, draft, heads, steps,
):
    def arrivals(r):
        return (
            pltpu.make_async_copy(mem_hbm.at[r], mem_buf.at[r], in_sems.at[0, r]),
            pltpu.make_async_copy(mom_hbm.at[r], mom_buf.at[r], in_sems.at[1, r]),
        )

    def departures(r):
        return (
            pltpu.make_async_copy(mem_buf.at[r], mem_out.at[r], out_sems.at[0, r]),
            pltpu.make_async_copy(mom_buf.at[r], mom_out.at[r], out_sems.at[1, r]),
        )

    for r in range(reqs):
        for copy in arrivals(r):
            copy.start()
    unit_ref[...] = jnp.zeros_like(unit_ref)

    def one(r, carry):
        rows = pl.ds(pl.multiple_of(r * draft, draft), draft)
        wide_k[...] = k_ref[rows, :].astype(F32)
        wide_v[...] = v_ref[rows, :].astype(F32)
        for n in range(steps):
            node = path[n, r]
            k_row = wide_k[pl.ds(node, 1), :]
            v_row = wide_v[pl.ds(node, 1), :]
            for h in range(heads):
                unit_ref[h * steps + n : h * steps + n + 1, :] = k_row[:, h * HD : (h + 1) * HD]
                value_ref[h * steps + n : h * steps + n + 1, :] = v_row[:, h * HD : (h + 1) * HD]
        keys = unit_ref[...]
        unit = keys * lax.rsqrt(jnp.sum(keys * keys, axis=1, keepdims=True) + EPS)
        turned_ref[...] = jnp.transpose(unit)
        for copy in arrivals(r):
            copy.wait()

        def advance(n):
            for h in range(heads):
                eta = 0.97 - 0.06 * mom_code[n, h, r].astype(F32)
                keep = 1.0 - (0.01 + 0.02 * forget_code[n, h, r].astype(F32))
                row = h * steps + n
                column = turned_ref[:, row : row + 1]
                matrix = mem_buf[r, h]
                predicted = jnp.sum(column * matrix, axis=0, keepdims=True)
                error = THETA * (predicted - value_ref[row : row + 1, :])
                moved = eta * mom_buf[r, h] - column * error
                mom_buf[r, h] = moved
                mem_buf[r, h] = keep * matrix + moved

        for n in range(steps):
            pl.when(n < count[r])(functools.partial(advance, n))
        for copy in departures(r):
            copy.start()
        return carry

    lax.fori_loop(0, reqs, one, 0)
    for r in range(reqs):
        for copy in departures(r):
            copy.wait()


def combine(
    codes, side, msg_ref, o_hbm, ret_hbm, own_top_ref, own_sum_ref, *rest,
    n, cap, reqs, draft, heads, pieces,
):
    outs = rest[:pieces]
    part_top, part_sum, best, total, weight, own_weight, acc, mixed, o_ref, ret_ref, sems = rest[
        pieces:
    ]
    copies = [
        pltpu.make_async_copy(o_hbm, o_ref, sems.at[0]),
        pltpu.make_async_copy(ret_hbm, ret_ref, sems.at[1]),
    ]
    for copy in copies:
        copy.start()
    span = heads * draft
    block = cap * span + EXTRA
    slots = n * cap
    for d in range(n):
        at = d * block + cap * span
        tail = msg_ref[at : at + EXTRA, :].astype(F32)
        rows = [tail[p * cap : (p + 1) * cap] for p in range(TOP_PARTS + SUM_PARTS)]
        part_top[d * cap : (d + 1) * cap, :] = rows[0] + rows[1] + rows[2]
        part_sum[d * cap : (d + 1) * cap, :] = rows[3] + rows[4]
    best[...] = own_top_ref[...]
    owners = [lax.rem(codes[s // cap, 0, s % cap], reqs) for s in range(slots)]
    for s in range(slots):
        r = owners[s]
        best[pl.ds(r, 1), :] = jnp.maximum(best[pl.ds(r, 1), :], part_top[s : s + 1, :])
    own_weight[...] = jnp.zeros_like(own_weight)
    weight[...] = jnp.zeros_like(weight)
    start = jnp.exp(own_top_ref[...] - best[...])
    total[...] = start * own_sum_ref[...]
    for s in range(slots):
        r = owners[s]
        term = jnp.exp(part_top[s : s + 1, :] - best[pl.ds(r, 1), :])
        weight[s : s + 1, :] = term
        total[pl.ds(r, 1), :] = total[pl.ds(r, 1), :] + term * part_sum[s : s + 1, :]
    inverse = 1.0 / total[...]
    own_weight[0:reqs, :] = start * inverse
    total[...] = inverse
    for s in range(slots):
        weight[s : s + 1, :] = weight[s : s + 1, :] * total[pl.ds(owners[s], 1), :]
    turned = jnp.transpose(weight[...])
    own_turned = jnp.transpose(own_weight[...])
    for copy in copies:
        copy.wait()
    for r in range(reqs):
        rows = slice(r * span, (r + 1) * span)
        acc[rows, :] = o_ref[rows, :] * own_turned[0:span, r : r + 1] + ret_ref[rows, :]
    for s in range(slots):
        at = (s // cap) * block + (s % cap) * span
        rows = pl.ds(pl.multiple_of(owners[s] * span, span), span)
        acc[rows, :] = acc[rows, :] + msg_ref[at : at + span, :].astype(F32) * turned[
            0:span, s : s + 1
        ]
    for r in range(reqs):
        for h in range(heads):
            at = r * span + h * draft
            mixed[r * draft : (r + 1) * draft, h * HD : (h + 1) * HD] = acc[
                at : at + draft, :
            ].astype(BF16)
    rows = reqs * draft // pieces
    for p, out_ref in enumerate(outs):
        first = lax.rem(side[0] + p, pieces) * rows
        out_ref[...] = mixed[pl.ds(pl.multiple_of(first, rows), rows), :]


def run_copies(pairs, sems):
    copies = [
        pltpu.make_async_copy(source, target, sems.at[i])
        for i, (source, target) in enumerate(pairs)
    ]
    for copy in copies:
        copy.start()
    return copies


def first_pairs(side, gate_up_w, down_w, out_w, first_ref, quarter_ref):
    depth, width = down_w.shape[0] // 4, out_w.shape[0] // 4
    down_rows = pl.ds(pl.multiple_of(side[2] * depth, EXTRA), depth)
    out_rows = pl.ds(pl.multiple_of(side[2] * width, EXTRA), width)
    pairs = [
        (down_w.at[down_rows], quarter_ref.at[pl.ds(0, depth)]),
        (out_w.at[out_rows], quarter_ref.at[pl.ds(depth, width)]),
    ]
    step = first_ref.shape[0] // 2
    for i in range(2):
        rows = pl.ds(i * step, step)
        pairs.append((gate_up_w.at[side[1], rows], first_ref.at[rows]))
    return pairs


def cut_last(side, gate_up_w, mid_ref, last_ref, sems, *, pieces):
    step = last_ref.shape[0] // pieces
    start = gate_up_w.shape[1] - last_ref.shape[0]
    half = gate_up_w.at[side[1]]
    middle = mid_ref.shape[0]
    pairs = [(half.at[pl.ds(start - middle, middle)], mid_ref)]
    for i in range(pieces):
        pairs.append((half.at[pl.ds(start + i * step, step)], last_ref.at[pl.ds(i * step, step)]))
    for copy in run_copies(pairs, sems):
        copy.wait()


def stage_weights(
    side, out_w, gate_up_w, down_w, one_a, one_m, one_b, one_q, two_a, two_m, two_q, three_q,
    three_r, four_q, two_b, four_r, out_all, gate_up_all, down_all, sems,
):
    width, depth = out_w.shape[0] // 4, down_w.shape[0] // 4
    pairs = [(gate_up_w, gate_up_all.at[0]), (down_w, down_all.at[0]), (out_w, out_all.at[0])]
    for half, parts in ((side[1], (one_a, one_m, one_b)), (1 - side[1], (two_a, two_m, two_b))):
        at = 0
        for part in parts:
            pairs.append((part, gate_up_all.at[1, half, pl.ds(at, part.shape[0])]))
            at += part.shape[0]
    core, chip = side[1], side[2] // 2
    near = three_q.shape[0]
    places = ((core, chip), (1 - core, chip), (core, 1 - chip), (1 - core, 1 - chip))
    got = ((one_q,), (two_q,), (three_q, three_r), (four_q, four_r))
    for (x, y), parts in zip(places, got):
        base = pl.multiple_of((2 * y + x) * depth, EXTRA)
        rows = pl.ds(pl.multiple_of((2 * y + x) * width, EXTRA), width)
        if len(parts) == 2:
            pairs.append((parts[0], down_all.at[1, pl.ds(base, near)]))
        at = near if len(parts) == 2 else 0
        rest = depth - at
        pairs.append((parts[-1].at[pl.ds(0, rest)], down_all.at[1, pl.ds(base + at, rest)]))
        pairs.append((parts[-1].at[pl.ds(rest, width)], out_all.at[1, rows]))
    for copy in run_copies(pairs, sems):
        copy.wait()


def feed_forward(
    side, tok_ref, mine_ref, theirs_ref, gain_ref, out_w, gate_up_w, down_w, out_ref,
    residual, hidden,
):
    rows = mine_ref.shape[0]
    units = gate_up_w.shape[3]
    tokens = tok_ref[pl.ds(pl.multiple_of(side[0] * rows, rows), rows), :].astype(F32)
    summed = tokens + jnp.dot(mine_ref[...], out_w[0], preferred_element_type=F32)
    summed = summed + jnp.dot(theirs_ref[...], out_w[1], preferred_element_type=F32)
    residual[...] = summed.astype(BF16)
    ffn_in = rms_norm(residual[...], gain_ref[...])
    step = 256
    for half in range(2):
        for first in range(0, units, step):
            cols = slice(first, min(first + step, units))
            gate = jnp.dot(ffn_in, gate_up_w[half, 0, :, cols], preferred_element_type=F32)
            up = jnp.dot(ffn_in, gate_up_w[half, 1, :, cols], preferred_element_type=F32)
            hidden[half, :, cols] = (gate / (1.0 + jnp.exp(-gate)) * up).astype(BF16)
    for at in range(0, out_ref.shape[1], step):
        cols = slice(at, at + step)
        total = residual[:, cols].astype(F32)
        for half in range(2):
            total = total + jnp.dot(hidden[half], down_w[half, :, cols], preferred_element_type=F32)
        out_ref[:, cols] = total.astype(BF16)


def on_device(
    tokens,
    norm_attn,
    w_query,
    w_key,
    w_value,
    w_out,
    persist_keys,
    persist_values,
    kv_cache,
    slot_request,
    slot_page,
    cache_len,
    tree_mask,
    accept_path,
    accept_len,
    memory,
    momentum,
    momentum_code,
    forget_code,
    norm_ffn,
    w_gate_up,
    w_down,
):
    n = lax.axis_size("req")
    group_rows, model = tokens.shape
    reqs = cache_len.shape[0]
    draft = tree_mask.shape[1]
    steps = accept_path.shape[1]
    width = w_query.shape[1]
    heads = width // HD
    span = heads * draft
    slots = kv_cache.shape[0]
    cap = slots // n
    fixed_count = persist_keys.shape[0]
    page_len = kv_cache.shape[2]
    ask_block = cap * HD + EXTRA
    block = cap * span + EXTRA
    scale = 1.0 / math.sqrt(HD)

    label = (slot_page * reqs + lax.rem(slot_request, reqs)).reshape(n, 1, cap)
    codes = lax.all_to_all(label, "req", split_axis=0, concat_axis=0, tiled=True)

    grp = lax.axis_size("grp")
    depth, out_depth = w_down.shape[0] // 4, width // 4
    first, middle = model // 4, model * 7 // 32
    near = (depth + out_depth) // 2 // 48 * 48
    split = (depth, out_depth, first // 2, middle, (model - first - middle) // 2)
    pieces = 2 if grp == 2 and n % 4 == 0 and not any(size % EXTRA for size in split) else 1
    quarter = lax.rem(lax.axis_index("req"), 4)
    core = lax.rem(quarter, 2)
    side = jnp.stack([lax.axis_index("grp"), core, quarter]).astype(jnp.int32)

    cut, units = pieces == 2, w_down.shape[0]
    cuts = ((first, units), (depth + out_depth, model)) if cut else ()
    normed, queries, turned, *shares = pl.pallas_call(
        functools.partial(project_queries, reqs=reqs, draft=draft, heads=heads, cut=cut),
        out_shape=(
            HBM((group_rows, model), BF16),
            HBM((group_rows, width), BF16),
            jax.ShapeDtypeStruct((reqs * HD, LANES), BF16),
        )
        + tuple(VMEM(shape, BF16) for shape in cuts),
        in_specs=([whole(SMEM)] + [whole(HBM)] * 3) * cut + [whole()] * 3,
        out_specs=(whole(),) * (3 + len(cuts)),
        scratch_shapes=[pltpu.SemaphoreType.DMA((4,))] * cut,
        compiler_params=params(14),
        cost_estimate=cost(
            2 * group_rows * model * width, 2 * model * (2 * group_rows + width)
        ),
        name="project_queries",
    )(
        *((side, *keep_in(HBM, w_gate_up, w_down, w_out)) if cut else ()),
        *keep_in(HBM, tokens, norm_attn.reshape(1, -1), w_query),
    )
    if cut:
        half_first, quarters = shares

    if pieces == 2:
        turned, half_first, quarters = lax.optimization_barrier((turned, half_first, quarters))
        swap = [(0, 1), (1, 0)]
        one_a = lax.ppermute(half_first, "grp", swap)
        one_q = lax.ppermute(quarters, "grp", swap)

    packed = pl.pallas_call(
        functools.partial(pack_queries, n=n, cap=cap, reqs=reqs, page_len=page_len),
        out_shape=HBM((n * ask_block, LANES), BF16),
        in_specs=[whole(SMEM), whole(SMEM), whole()],
        out_specs=whole(HBM),
        scratch_shapes=[
            pltpu.VMEM((n * ask_block, LANES), BF16),
            pltpu.SemaphoreType.DMA((n,)),
        ],
        compiler_params=params(8),
        cost_estimate=cost(0, 4 * n * ask_block * LANES),
        name="pack_queries",
    )(codes, *keep_in(HBM, cache_len), turned)
    packed, normed, late = lax.optimization_barrier((packed, normed, w_gate_up))
    asked = lax.all_to_all(packed, "req", split_axis=0, concat_axis=0, tiled=True)

    if pieces == 2:
        half_mid, half_last = pl.pallas_call(
            functools.partial(cut_last, pieces=2),
            out_shape=(VMEM((middle, units), BF16), VMEM((model - first - middle, units), BF16)),
            in_specs=[whole(SMEM), whole(HBM)],
            out_specs=(whole(),) * 2,
            scratch_shapes=[pltpu.SemaphoreType.DMA((3,))],
            compiler_params=params(4),
            cost_estimate=cost(0, 4 * (model - first) * units),
            name="cut_last",
        )(side, *keep_in(HBM, late))

    keys, values = pl.pallas_call(
        project_keys,
        out_shape=(HBM((group_rows, width), BF16),) * 2,
        in_specs=[whole()] * 3,
        out_specs=(whole(),) * 2,
        compiler_params=params(12),
        cost_estimate=cost(
            4 * group_rows * model * width, 2 * model * (group_rows + 2 * width)
        ),
        name="project_keys",
    )(*keep_in(HBM, normed, w_key, w_value))

    row_block = pl.BlockSpec((draft, width), lambda r, *_: (r, 0))
    fixed_block = pl.BlockSpec((fixed_count, width), lambda r, *_: (0, 0))
    matrix_block = pl.BlockSpec((1, heads, HD, HD), lambda r, *_: (r, 0, 0, 0))
    span_block = pl.BlockSpec((span, HD), lambda r, *_: (r, 0))
    own, retrieved, own_top, own_sum = pl.pallas_call(
        functools.partial(local_attention, heads=heads, draft=draft, scale=scale),
        grid=(reqs,),
        out_shape=(
            HBM((reqs * span, HD), F32),
            HBM((reqs * span, HD), F32),
            jax.ShapeDtypeStruct((reqs, LANES), F32),
            jax.ShapeDtypeStruct((reqs, LANES), F32),
        ),
        in_specs=[
            row_block,
            row_block,
            row_block,
            fixed_block,
            fixed_block,
            pl.BlockSpec((1, draft, draft), lambda r: (r, 0, 0)),
            matrix_block,
        ],
        out_specs=(span_block, span_block) + (pl.BlockSpec((reqs, LANES), lambda r: (0, 0)),) * 2,
        compiler_params=params(10),
        cost_estimate=cost(1, 1),
        name="local_attention",
    )(*keep_in(HBM, queries, keys, values, persist_keys, persist_values, tree_mask, memory))

    memory_out, momentum_out = pl.pallas_call(
        functools.partial(update_memory, reqs=reqs, draft=draft, heads=heads, steps=steps),
        out_shape=(HBM(memory.shape, F32),) * 2,
        in_specs=[whole(SMEM)] * 4 + [whole()] * 2 + [whole(HBM)] * 2,
        out_specs=(whole(HBM),) * 2,
        scratch_shapes=[
            pltpu.VMEM(memory.shape, F32),
            pltpu.VMEM(memory.shape, F32),
            pltpu.VMEM((draft, width), F32),
            pltpu.VMEM((draft, width), F32),
            pltpu.VMEM((LANES, HD), F32),
            pltpu.VMEM((heads * steps, HD), F32),
            pltpu.VMEM((HD, LANES), F32),
            pltpu.SemaphoreType.DMA((2, reqs)),
            pltpu.SemaphoreType.DMA((2, reqs)),
        ],
        compiler_params=params(16),
        cost_estimate=cost(
            14 * reqs * heads * HD * HD * steps * 8, 16 * reqs * heads * HD * HD
        ),
        name="update_memory",
    )(
        jnp.transpose(accept_path),
        accept_len,
        jnp.transpose(momentum_code, (1, 2, 0)),
        jnp.transpose(forget_code, (1, 2, 0)),
        *keep_in(HBM, keys, values, memory, momentum),
    )

    if pieces == 2:
        memory_out, momentum_out, half_mid, half_last, one_a, one_q = lax.optimization_barrier(
            (memory_out, momentum_out, half_mid, half_last, one_a, one_q)
        )
        other_core = [(i, i ^ 1) for i in range(n)]
        other_chip = [(i, i ^ 2) for i in range(n)]
        one_m = lax.ppermute(half_mid, "grp", swap)
        one_b = lax.ppermute(half_last, "grp", swap)
        three_q = lax.ppermute(one_q[:near], "req", other_chip)
        three_r = lax.ppermute(one_q[near:], "req", other_chip)
    asked, memory_out, momentum_out, keys, values = lax.optimization_barrier(
        (asked, memory_out, momentum_out, keys, values)
    )
    answers = pl.pallas_call(
        functools.partial(
            page_attention, n=n, cap=cap, draft=draft, heads=heads, page_len=page_len,
            scale=scale, group=2,
        ),
        out_shape=HBM((n * block, LANES), BF16),
        in_specs=[whole(), whole(HBM)],
        out_specs=whole(HBM),
        scratch_shapes=[
            pltpu.VMEM((n, cap) + kv_cache.shape[1:], BF16),
            pltpu.VMEM((n * block, LANES), BF16),
            pltpu.SemaphoreType.DMA((n,)),
            pltpu.SemaphoreType.DMA((n,)),
        ],
        compiler_params=params(24),
        cost_estimate=cost(
            4 * slots * span * page_len * HD,
            4 * slots * page_len * width + 4 * n * block * LANES,
            slots * span * page_len,
        ),
        name="page_attention",
    )(asked, *keep_in(HBM, kv_cache))
    if pieces == 2:
        answers, one_m, three_q = lax.optimization_barrier((answers, one_m, three_q))
        _, one_a, one_q = lax.optimization_barrier((answers, one_a, one_q))
        own, one_m, three_q = lax.optimization_barrier((own, one_m, three_q))
        two_a, two_q, two_m, four_q = (
            lax.ppermute(part, "req", other_core) for part in (one_a, one_q, one_m, three_q)
        )
    returned = lax.all_to_all(answers, "req", split_axis=0, concat_axis=0, tiled=True)
    if pieces == 2:
        returned, one_b, two_a, two_m, two_q, four_q, three_r, own, retrieved = (
            lax.optimization_barrier(
                (returned, one_b, two_a, two_m, two_q, four_q, three_r, own, retrieved)
            )
        )
        two_b = lax.ppermute(one_b, "req", other_core)
        four_r = lax.ppermute(three_r, "req", other_core)
    rows = group_rows // grp
    mixed = pl.pallas_call(
        functools.partial(
            combine, n=n, cap=cap, reqs=reqs, draft=draft, heads=heads, pieces=pieces
        ),
        out_shape=(jax.ShapeDtypeStruct((group_rows // pieces, width), BF16),) * pieces,
        in_specs=[whole(SMEM)] * 2 + [whole()] + [whole(HBM)] * 2 + [whole()] * 2,
        out_specs=(whole(),) * pieces,
        scratch_shapes=[
            pltpu.VMEM((slots, LANES), F32),
            pltpu.VMEM((slots, LANES), F32),
            pltpu.VMEM((reqs, LANES), F32),
            pltpu.VMEM((reqs, LANES), F32),
            pltpu.VMEM((LANES, LANES), F32),
            pltpu.VMEM((LANES, LANES), F32),
            pltpu.VMEM((reqs * span, HD), F32),
            pltpu.VMEM((group_rows, width), BF16),
            pltpu.VMEM((reqs * span, HD), F32),
            pltpu.VMEM((reqs * span, HD), F32),
            pltpu.SemaphoreType.DMA((2,)),
        ],
        compiler_params=params(12),
        cost_estimate=cost(
            8 * slots * span * HD, 2 * n * block * LANES + 8 * reqs * span * HD
        ),
        name="combine",
    )(codes, side, returned, *keep_in(HBM, own, retrieved), own_top, own_sum)

    if pieces == 2:
        mine, asked_for = mixed
        theirs = lax.ppermute(asked_for, "grp", swap)
        mine, two_b, four_r = lax.optimization_barrier((mine, two_b, four_r))
        out_near, gate_up_near, down_near = pl.pallas_call(
            stage_weights,
            out_shape=(
                VMEM((2,) + w_out.shape, BF16),
                VMEM((2,) + w_gate_up.shape, BF16),
                VMEM((2,) + w_down.shape, BF16),
            ),
            in_specs=[whole(SMEM)] + [whole(pl.ANY)] * 15,
            out_specs=(whole(),) * 3,
            scratch_shapes=[pltpu.SemaphoreType.DMA((19,))],
            compiler_params=params(2),
            cost_estimate=cost(0, 2 * model * (2 * width + 6 * units)),
            name="stage_weights",
        )(
            side,
            *keep_in(
                HBM, w_out, w_gate_up, w_down, one_a, one_m, one_b, one_q, two_a, two_m, two_q,
                three_q, three_r, four_q,
            ),
            two_b,
            four_r,
        )
        layer_out = pl.pallas_call(
            feed_forward,
            out_shape=jax.ShapeDtypeStruct((rows, model), BF16),
            in_specs=[whole(SMEM)] + [whole()] * 7,
            out_specs=whole(),
            scratch_shapes=[
                pltpu.VMEM((rows, model), BF16),
                pltpu.VMEM((2, rows, units), BF16),
            ],
            compiler_params=params(14),
            cost_estimate=cost(
                4 * rows * model * (width + 3 * units), 4 * model * (width + 3 * units)
            ),
            name="feed_forward",
        )(
            side, tokens, mine, theirs, norm_ffn.reshape(1, -1),
            *keep_in(VMEM, out_near, gate_up_near, down_near),
        )
        return (layer_out, memory_out, momentum_out)

    partial_out = jnp.dot(mixed[0], w_out, preferred_element_type=F32).astype(BF16)
    head_sum = lax.psum_scatter(partial_out, "grp", scatter_dimension=0, tiled=True).astype(F32)
    own_rows = lax.dynamic_slice_in_dim(tokens, lax.axis_index("grp") * rows, rows, 0)
    residual = (own_rows.astype(F32) + head_sum).astype(BF16)
    ffn_in = rms_norm(residual, norm_ffn)
    piece = lax.all_gather(ffn_in, "grp", axis=0, tiled=True)
    gate = jnp.dot(piece, w_gate_up[0], preferred_element_type=F32)
    up = jnp.dot(piece, w_gate_up[1], preferred_element_type=F32)
    hidden = (jax.nn.silu(gate) * up).astype(BF16)
    ffn_out = lax.psum_scatter(
        jnp.dot(hidden, w_down, preferred_element_type=F32).astype(BF16),
        "grp",
        scatter_dimension=0,
        tiled=True,
    ).astype(F32)
    layer_out = (residual.astype(F32) + ffn_out).astype(BF16)
    return (layer_out, memory_out, momentum_out)


def solution(mesh):
    return jax.shard_map(
        on_device,
        mesh=mesh,
        in_specs=(
            P("req", None),
            P(),
            P(None, "grp"),
            P(None, "grp"),
            P(None, "grp"),
            P("grp", None),
            P(None, "grp"),
            P(None, "grp"),
            P("req", None, None, "grp"),
            P("req"),
            P("req"),
            P("req"),
            P("req", None, None),
            P("req", None),
            P("req"),
            P("req", "grp", None, None),
            P("req", "grp", None, None),
            P("req", None, "grp"),
            P("req", None, "grp"),
            P(),
            P(None, None, "grp"),
            P("grp", None),
        ),
        out_specs=(
            P(("req", "grp"), None),
            P("req", "grp", None, None),
            P("req", "grp", None, None),
        ),
        check_vma=False,
    )
```

```python
import functools
import math

import jax
import jax.numpy as jnp
from jax import lax
from jax.experimental import pallas as pl
from jax.experimental.pallas import tpu as pltpu
from jax.sharding import PartitionSpec as P

HD = 128
LANES = 128
EXTRA = 16
TOP_PARTS = 3
WEIGHT = 20
SUM_PARTS = 2

EPS = 1e-06
THETA = 0.5
NEG = -1e30

VMEM = pltpu.VMEM
SMEM = pltpu.SMEM
HBM = pltpu.HBM
F32 = jnp.float32
BF16 = jnp.bfloat16


def whole(space=VMEM):
    return pl.BlockSpec(memory_space=space)


def cost(flops, moved, special=0):
    return pl.CostEstimate(
        flops=WEIGHT * flops, bytes_accessed=WEIGHT * moved, transcendentals=special
    )


def keep_in(space, *arrays):
    return tuple(pltpu.with_memory_space_constraint(array, space) for array in arrays)


def params(mib=40):
    return pltpu.CompilerParams(vmem_limit_bytes=mib << 20)


def rms_norm(rows, gain):
    values = rows.astype(F32)
    factor = lax.rsqrt(jnp.mean(values * values, axis=-1, keepdims=True) + EPS)
    return (values * factor * gain).astype(BF16)


def nt_dot(left, right):
    return lax.dot_general(left, right, (((1,), (1,)), ((), ())), preferred_element_type=F32)


def column_to_row(column, count):
    row_id = lax.broadcasted_iota(jnp.int32, (count, LANES), 0)
    lane_id = lax.broadcasted_iota(jnp.int32, (count, LANES), 1)
    spread = jnp.where(row_id == lane_id, jnp.broadcast_to(column, (count, LANES)), 0.0)
    return jnp.sum(spread, axis=0, keepdims=True)


def split_parts(row, count):
    parts = []
    for _ in range(count):
        part = row.astype(BF16).astype(F32)
        parts.append(part)
        row = row - part
    return parts


def project_queries(*refs, reqs, draft, heads, cut):
    copies = []
    if cut:
        side, gate_up_w, down_w, out_w, *refs, q_ref, q_sem, sems = refs
        *refs, first_ref, quarter_ref = refs
        refs += [q_ref, q_sem]
        copies = run_copies(
            first_pairs(side, gate_up_w, down_w, out_w, first_ref, quarter_ref), sems
        )
    tok_ref, gain_ref, w_ref, q_hbm, turned_ref, q_ref, q_sem = refs
    normed = rms_norm(tok_ref[...], gain_ref[...])
    q_ref[...] = jnp.dot(normed, w_ref[...], preferred_element_type=F32).astype(BF16)
    copies.append(pltpu.make_async_copy(q_ref, q_hbm, q_sem.at[0]))
    copies[-1].start()
    span = heads * draft
    for r in range(reqs):
        rows = slice(r * draft, (r + 1) * draft)
        pieces = [q_ref[rows, h * HD : (h + 1) * HD].astype(F32) for h in range(heads)]
        if span < LANES:
            pieces.append(jnp.zeros((LANES - span, HD), F32))
        tile = jnp.concatenate(pieces, axis=0)
        turned_ref[r * HD : (r + 1) * HD, :] = jnp.transpose(tile).astype(BF16)
    for copy in copies:
        copy.wait()


def project_keys(tok_ref, gain_ref, wk_ref, wv_ref, k_ref, v_ref):
    normed = rms_norm(tok_ref[...], gain_ref[...])
    k_ref[...] = jnp.dot(normed, wk_ref[...], preferred_element_type=F32).astype(BF16)
    v_ref[...] = jnp.dot(normed, wv_ref[...], preferred_element_type=F32).astype(BF16)


def pack_queries(codes, lengths, turned_ref, out_hbm, out_ref, sems, *, n, cap, reqs, page_len):
    block = cap * HD + EXTRA
    row_id = lax.broadcasted_iota(jnp.int32, (EXTRA, LANES), 0)

    def departure(d):
        rows = pl.ds(pl.multiple_of(d * block, EXTRA), block)
        return pltpu.make_async_copy(out_ref.at[rows], out_hbm.at[rows], sems.at[d])

    def one(d, carry):
        base = pl.multiple_of(d * block, EXTRA)
        tail = jnp.zeros((EXTRA, LANES), F32)
        for c in range(cap):
            code = codes[d, 0, c]
            r = lax.rem(code, reqs)
            page = lax.div(code, reqs)
            live = jnp.clip(lengths[r] - page * page_len, 0, page_len)
            tail = jnp.where(row_id == c, live.astype(F32), tail)
            rows = pl.ds(pl.multiple_of(r * HD, HD), HD)
            out_ref[pl.ds(base + c * HD, HD), :] = turned_ref[rows, :]
        out_ref[pl.ds(base + cap * HD, EXTRA), :] = tail.astype(BF16)
        departure(d).start()
        return carry

    lax.fori_loop(0, n, one, 0)
    for d in range(n):
        departure(d).wait()


def page_attention(
    q_ref, kv_hbm, out_hbm, kv_buf, out_buf, in_sems, out_sems,
    *, n, cap, draft, heads, page_len, scale, group,
):
    span = heads * draft
    ask_block = cap * HD + EXTRA
    block = cap * span + EXTRA
    token = lax.broadcasted_iota(jnp.int32, (page_len, LANES), 0).astype(F32)
    row_id = lax.broadcasted_iota(jnp.int32, (EXTRA, LANES), 0)
    head_of = lax.broadcasted_iota(jnp.int32, (HD, LANES), 1) // draft

    def arrival(d):
        return pltpu.make_async_copy(
            kv_hbm.at[pl.ds(d * cap, cap)], kv_buf.at[d], in_sems.at[d]
        )

    def departure(d):
        rows = pl.ds(pl.multiple_of(d * block, EXTRA), block)
        return pltpu.make_async_copy(out_buf.at[rows], out_hbm.at[rows], out_sems.at[d])

    for d in range(n):
        arrival(d).start()

    def one(i, carry):
        pairs = [(i * group + g, c) for g in range(group) for c in range(cap)]
        limits = []
        for g in range(group):
            d = i * group + g
            arrival(d).wait()
            at = pl.multiple_of(d * ask_block + cap * HD, EXTRA)
            limits.append(q_ref[pl.ds(at, EXTRA), :].astype(F32))
        all_scores = []
        for d, c in pairs:
            at = pl.multiple_of(d * ask_block + c * HD, EXTRA)
            turned = q_ref[pl.ds(at, HD), :]
            blocks = [jnp.where(head_of == h, turned, jnp.zeros_like(turned)) for h in range(heads)]
            all_scores.append(
                jnp.dot(
                    kv_buf[d, c, 0], jnp.concatenate(blocks, axis=0), preferred_element_type=F32
                )
            )
        all_weights = []
        tails = [jnp.zeros((EXTRA, LANES), F32) for _ in range(group)]
        for j, (d, c) in enumerate(pairs):
            g = j // cap
            scores = jnp.where(token < limits[g][c : c + 1, :], all_scores[j] * scale, NEG)
            top = jnp.max(scores, axis=0, keepdims=True)
            weight = jnp.exp(scores - top)
            total = jnp.sum(weight, axis=0, keepdims=True)
            all_weights.append(jnp.transpose(weight).astype(BF16))
            parts = split_parts(top, TOP_PARTS) + split_parts(total, SUM_PARTS)
            for p, part in enumerate(parts):
                tails[g] = jnp.where(row_id == p * cap + c, part, tails[g])
        for j, (d, c) in enumerate(pairs):
            for h in range(heads):
                numer = jnp.dot(
                    all_weights[j][h * draft : (h + 1) * draft, :],
                    kv_buf[d, c, 1, :, h * HD : (h + 1) * HD],
                    preferred_element_type=F32,
                )
                at = pl.multiple_of(d * block + c * span + h * draft, EXTRA)
                out_buf[pl.ds(at, draft), :] = numer.astype(BF16)
        for g in range(group):
            d = i * group + g
            at = pl.multiple_of(d * block + cap * span, EXTRA)
            out_buf[pl.ds(at, EXTRA), :] = tails[g].astype(BF16)
            departure(d).start()
        return carry

    lax.fori_loop(0, n // group, one, 0)
    for d in range(n):
        departure(d).wait()


def local_attention(
    q_ref, k_ref, v_ref, pk_ref, pv_ref, mask_ref, mem_ref,
    o_ref, ret_ref, top_ref, sum_ref, *, heads, draft, scale,
):
    r = pl.program_id(0)
    seen = mask_ref[0] == 1
    tops, totals = [], []
    for h in range(heads):
        cols = slice(h * HD, (h + 1) * HD)
        rows = slice(h * draft, (h + 1) * draft)
        query = q_ref[:, cols]
        tree = jnp.where(seen, nt_dot(query, k_ref[:, cols]) * scale, NEG)
        fixed = nt_dot(query, pk_ref[:, cols]) * scale
        top = jnp.maximum(
            jnp.max(tree, axis=1, keepdims=True), jnp.max(fixed, axis=1, keepdims=True)
        )
        tree_w = jnp.exp(tree - top)
        fixed_w = jnp.exp(fixed - top)
        total = jnp.sum(tree_w, axis=1, keepdims=True) + jnp.sum(fixed_w, axis=1, keepdims=True)
        numer = jnp.dot(tree_w.astype(BF16), v_ref[:, cols], preferred_element_type=F32)
        numer = numer + jnp.dot(fixed_w.astype(BF16), pv_ref[:, cols], preferred_element_type=F32)
        o_ref[rows, :] = numer
        tops.append(top)
        totals.append(total)
        wide = query.astype(F32)
        unit = wide * lax.rsqrt(jnp.sum(wide * wide, axis=1, keepdims=True) + EPS)
        ret_ref[rows, :] = jnp.dot(
            unit, mem_ref[0, h], preferred_element_type=F32, precision=lax.Precision.HIGHEST
        )
    span = heads * draft
    top_ref[pl.ds(r, 1), :] = column_to_row(jnp.concatenate(tops, axis=0), span)
    sum_ref[pl.ds(r, 1), :] = column_to_row(jnp.concatenate(totals, axis=0), span)


def update_memory(
    path, count, mom_code, forget_code, k_ref, v_ref, mem_hbm, mom_hbm, mem_out, mom_out,
    mem_buf, mom_buf, wide_k, wide_v, unit_ref, value_ref, turned_ref, in_sems, out_sems,
    *, reqs, draft, heads, steps,
):
    def arrivals(r):
        return (
            pltpu.make_async_copy(mem_hbm.at[r], mem_buf.at[r], in_sems.at[0, r]),
            pltpu.make_async_copy(mom_hbm.at[r], mom_buf.at[r], in_sems.at[1, r]),
        )

    def departures(r):
        return (
            pltpu.make_async_copy(mem_buf.at[r], mem_out.at[r], out_sems.at[0, r]),
            pltpu.make_async_copy(mom_buf.at[r], mom_out.at[r], out_sems.at[1, r]),
        )

    for r in range(reqs):
        for copy in arrivals(r):
            copy.start()
    unit_ref[...] = jnp.zeros_like(unit_ref)

    def one(r, carry):
        rows = pl.ds(pl.multiple_of(r * draft, draft), draft)
        wide_k[...] = k_ref[rows, :].astype(F32)
        wide_v[...] = v_ref[rows, :].astype(F32)
        for n in range(steps):
            node = path[n, r]
            k_row = wide_k[pl.ds(node, 1), :]
            v_row = wide_v[pl.ds(node, 1), :]
            for h in range(heads):
                unit_ref[h * steps + n : h * steps + n + 1, :] = k_row[:, h * HD : (h + 1) * HD]
                value_ref[h * steps + n : h * steps + n + 1, :] = v_row[:, h * HD : (h + 1) * HD]
        keys = unit_ref[...]
        unit = keys * lax.rsqrt(jnp.sum(keys * keys, axis=1, keepdims=True) + EPS)
        turned_ref[...] = jnp.transpose(unit)
        for copy in arrivals(r):
            copy.wait()

        def advance(n):
            for h in range(heads):
                eta = 0.97 - 0.06 * mom_code[n, h, r].astype(F32)
                keep = 1.0 - (0.01 + 0.02 * forget_code[n, h, r].astype(F32))
                row = h * steps + n
                column = turned_ref[:, row : row + 1]
                matrix = mem_buf[r, h]
                predicted = jnp.sum(column * matrix, axis=0, keepdims=True)
                error = THETA * (predicted - value_ref[row : row + 1, :])
                moved = eta * mom_buf[r, h] - column * error
                mom_buf[r, h] = moved
                mem_buf[r, h] = keep * matrix + moved

        for n in range(steps):
            pl.when(n < count[r])(functools.partial(advance, n))
        for copy in departures(r):
            copy.start()
        return carry

    lax.fori_loop(0, reqs, one, 0)
    for r in range(reqs):
        for copy in departures(r):
            copy.wait()


def combine(
    codes, side, msg_ref, o_hbm, ret_hbm, own_top_ref, own_sum_ref, *rest,
    n, cap, reqs, draft, heads, pieces,
):
    outs = rest[:pieces]
    part_top, part_sum, best, total, weight, own_weight, acc, mixed, o_ref, ret_ref, sems = rest[
        pieces:
    ]
    copies = [
        pltpu.make_async_copy(o_hbm, o_ref, sems.at[0]),
        pltpu.make_async_copy(ret_hbm, ret_ref, sems.at[1]),
    ]
    for copy in copies:
        copy.start()
    span = heads * draft
    block = cap * span + EXTRA
    slots = n * cap
    for d in range(n):
        at = d * block + cap * span
        tail = msg_ref[at : at + EXTRA, :].astype(F32)
        rows = [tail[p * cap : (p + 1) * cap] for p in range(TOP_PARTS + SUM_PARTS)]
        part_top[d * cap : (d + 1) * cap, :] = rows[0] + rows[1] + rows[2]
        part_sum[d * cap : (d + 1) * cap, :] = rows[3] + rows[4]
    best[...] = own_top_ref[...]
    owners = [lax.rem(codes[s // cap, 0, s % cap], reqs) for s in range(slots)]
    for s in range(slots):
        r = owners[s]
        best[pl.ds(r, 1), :] = jnp.maximum(best[pl.ds(r, 1), :], part_top[s : s + 1, :])
    own_weight[...] = jnp.zeros_like(own_weight)
    weight[...] = jnp.zeros_like(weight)
    start = jnp.exp(own_top_ref[...] - best[...])
    total[...] = start * own_sum_ref[...]
    for s in range(slots):
        r = owners[s]
        term = jnp.exp(part_top[s : s + 1, :] - best[pl.ds(r, 1), :])
        weight[s : s + 1, :] = term
        total[pl.ds(r, 1), :] = total[pl.ds(r, 1), :] + term * part_sum[s : s + 1, :]
    inverse = 1.0 / total[...]
    own_weight[0:reqs, :] = start * inverse
    total[...] = inverse
    for s in range(slots):
        weight[s : s + 1, :] = weight[s : s + 1, :] * total[pl.ds(owners[s], 1), :]
    turned = jnp.transpose(weight[...])
    own_turned = jnp.transpose(own_weight[...])
    for copy in copies:
        copy.wait()
    for r in range(reqs):
        rows = slice(r * span, (r + 1) * span)
        acc[rows, :] = o_ref[rows, :] * own_turned[0:span, r : r + 1] + ret_ref[rows, :]
    for s in range(slots):
        at = (s // cap) * block + (s % cap) * span
        rows = pl.ds(pl.multiple_of(owners[s] * span, span), span)
        acc[rows, :] = acc[rows, :] + msg_ref[at : at + span, :].astype(F32) * turned[
            0:span, s : s + 1
        ]
    for r in range(reqs):
        for h in range(heads):
            at = r * span + h * draft
            mixed[r * draft : (r + 1) * draft, h * HD : (h + 1) * HD] = acc[
                at : at + draft, :
            ].astype(BF16)
    rows = reqs * draft // pieces
    for p, out_ref in enumerate(outs):
        first = lax.rem(side[0] + p, pieces) * rows
        out_ref[...] = mixed[pl.ds(pl.multiple_of(first, rows), rows), :]


def run_copies(pairs, sems):
    copies = [
        pltpu.make_async_copy(source, target, sems.at[i])
        for i, (source, target) in enumerate(pairs)
    ]
    for copy in copies:
        copy.start()
    return copies


def first_pairs(side, gate_up_w, down_w, out_w, first_ref, quarter_ref):
    depth, width = down_w.shape[0] // 4, out_w.shape[0] // 4
    down_rows = pl.ds(pl.multiple_of(side[2] * depth, EXTRA), depth)
    out_rows = pl.ds(pl.multiple_of(side[2] * width, EXTRA), width)
    pairs = [
        (down_w.at[down_rows], quarter_ref.at[pl.ds(0, depth)]),
        (out_w.at[out_rows], quarter_ref.at[pl.ds(depth, width)]),
    ]
    step = first_ref.shape[0] // 2
    for i in range(2):
        rows = pl.ds(i * step, step)
        pairs.append((gate_up_w.at[side[1], rows], first_ref.at[rows]))
    return pairs


def cut_last(side, gate_up_w, mid_ref, last_ref, sems, *, pieces):
    step = last_ref.shape[0] // pieces
    start = gate_up_w.shape[1] - last_ref.shape[0]
    half = gate_up_w.at[side[1]]
    middle = mid_ref.shape[0]
    pairs = [(half.at[pl.ds(start - middle, middle)], mid_ref)]
    for i in range(pieces):
        pairs.append((half.at[pl.ds(start + i * step, step)], last_ref.at[pl.ds(i * step, step)]))
    for copy in run_copies(pairs, sems):
        copy.wait()


def stage_weights(
    side, out_w, gate_up_w, down_w, one_a, one_m, one_b, one_q, two_a, two_m, two_q, three_q,
    three_r, four_q, two_b, four_r, out_all, gate_up_all, down_all, sems,
):
    width, depth = out_w.shape[0] // 4, down_w.shape[0] // 4
    pairs = [(gate_up_w, gate_up_all.at[0]), (down_w, down_all.at[0]), (out_w, out_all.at[0])]
    for half, parts in ((side[1], (one_a, one_m, one_b)), (1 - side[1], (two_a, two_m, two_b))):
        at = 0
        for part in parts:
            pairs.append((part, gate_up_all.at[1, half, pl.ds(at, part.shape[0])]))
            at += part.shape[0]
    core, chip = side[1], side[2] // 2
    near = three_q.shape[0]
    places = ((core, chip), (1 - core, chip), (core, 1 - chip), (1 - core, 1 - chip))
    got = ((one_q,), (two_q,), (three_q, three_r), (four_q, four_r))
    for (x, y), parts in zip(places, got):
        base = pl.multiple_of((2 * y + x) * depth, EXTRA)
        rows = pl.ds(pl.multiple_of((2 * y + x) * width, EXTRA), width)
        if len(parts) == 2:
            pairs.append((parts[0], down_all.at[1, pl.ds(base, near)]))
        at = near if len(parts) == 2 else 0
        rest = depth - at
        pairs.append((parts[-1].at[pl.ds(0, rest)], down_all.at[1, pl.ds(base + at, rest)]))
        pairs.append((parts[-1].at[pl.ds(rest, width)], out_all.at[1, rows]))
    for copy in run_copies(pairs, sems):
        copy.wait()


def feed_forward(
    side, tok_ref, mine_ref, theirs_ref, gain_ref, out_w, gate_up_w, down_w, out_ref,
    residual, hidden,
):
    rows = mine_ref.shape[0]
    units = gate_up_w.shape[3]
    tokens = tok_ref[pl.ds(pl.multiple_of(side[0] * rows, rows), rows), :].astype(F32)
    summed = tokens + jnp.dot(mine_ref[...], out_w[0], preferred_element_type=F32)
    summed = summed + jnp.dot(theirs_ref[...], out_w[1], preferred_element_type=F32)
    residual[...] = summed.astype(BF16)
    ffn_in = rms_norm(residual[...], gain_ref[...])
    step = 256
    for half in range(2):
        for first in range(0, units, step):
            cols = slice(first, min(first + step, units))
            gate = jnp.dot(ffn_in, gate_up_w[half, 0, :, cols], preferred_element_type=F32)
            up = jnp.dot(ffn_in, gate_up_w[half, 1, :, cols], preferred_element_type=F32)
            hidden[half, :, cols] = (gate / (1.0 + jnp.exp(-gate)) * up).astype(BF16)
    for at in range(0, out_ref.shape[1], step):
        cols = slice(at, at + step)
        total = residual[:, cols].astype(F32)
        for half in range(2):
            total = total + jnp.dot(hidden[half], down_w[half, :, cols], preferred_element_type=F32)
        out_ref[:, cols] = total.astype(BF16)


def on_device(
    tokens,
    norm_attn,
    w_query,
    w_key,
    w_value,
    w_out,
    persist_keys,
    persist_values,
    kv_cache,
    slot_request,
    slot_page,
    cache_len,
    tree_mask,
    accept_path,
    accept_len,
    memory,
    momentum,
    momentum_code,
    forget_code,
    norm_ffn,
    w_gate_up,
    w_down,
):
    n = lax.axis_size("req")
    group_rows, model = tokens.shape
    reqs = cache_len.shape[0]
    draft = tree_mask.shape[1]
    steps = accept_path.shape[1]
    width = w_query.shape[1]
    heads = width // HD
    span = heads * draft
    slots = kv_cache.shape[0]
    cap = slots // n
    fixed_count = persist_keys.shape[0]
    page_len = kv_cache.shape[2]
    ask_block = cap * HD + EXTRA
    block = cap * span + EXTRA
    scale = 1.0 / math.sqrt(HD)

    label = (slot_page * reqs + lax.rem(slot_request, reqs)).reshape(n, 1, cap)
    codes = lax.all_to_all(label, "req", split_axis=0, concat_axis=0, tiled=True)

    grp = lax.axis_size("grp")
    depth, out_depth = w_down.shape[0] // 4, width // 4
    first, middle = model // 4, model * 7 // 32
    near = depth * 6 // 11 // EXTRA * EXTRA
    split = (depth, out_depth, first // 2, middle, (model - first - middle) // 2)
    pieces = 2 if grp == 2 and n % 4 == 0 and not any(size % EXTRA for size in split) else 1
    quarter = lax.rem(lax.axis_index("req"), 4)
    core = lax.rem(quarter, 2)
    side = jnp.stack([lax.axis_index("grp"), core, quarter]).astype(jnp.int32)

    cut, units = pieces == 2, w_down.shape[0]
    cuts = ((first, units), (depth + out_depth, model)) if cut else ()
    queries, turned, *shares = pl.pallas_call(
        functools.partial(project_queries, reqs=reqs, draft=draft, heads=heads, cut=cut),
        out_shape=(
            HBM((group_rows, width), BF16),
            jax.ShapeDtypeStruct((reqs * HD, LANES), BF16),
        )
        + tuple(VMEM(shape, BF16) for shape in cuts),
        in_specs=([whole(SMEM)] + [whole(HBM)] * 3) * cut + [whole()] * 3,
        out_specs=(whole(HBM),) + (whole(),) * (1 + len(cuts)),
        scratch_shapes=[pltpu.VMEM((group_rows, width), BF16), pltpu.SemaphoreType.DMA((1,))]
        + [pltpu.SemaphoreType.DMA((4,))] * cut,
        compiler_params=params(14),
        cost_estimate=cost(
            2 * group_rows * model * width, 2 * model * (2 * group_rows + width)
        ),
        name="project_queries",
    )(
        *((side, *keep_in(HBM, w_gate_up, w_down, w_out)) if cut else ()),
        *keep_in(HBM, tokens, norm_attn.reshape(1, -1), w_query),
    )
    if cut:
        half_first, quarters = shares

    if pieces == 2:
        turned, half_first, quarters = lax.optimization_barrier((turned, half_first, quarters))
        swap = [(0, 1), (1, 0)]
        one_a = lax.ppermute(half_first, "grp", swap)
        one_q = lax.ppermute(quarters, "grp", swap)

    packed = pl.pallas_call(
        functools.partial(pack_queries, n=n, cap=cap, reqs=reqs, page_len=page_len),
        out_shape=HBM((n * ask_block, LANES), BF16),
        in_specs=[whole(SMEM), whole(SMEM), whole()],
        out_specs=whole(HBM),
        scratch_shapes=[
            pltpu.VMEM((n * ask_block, LANES), BF16),
            pltpu.SemaphoreType.DMA((n,)),
        ],
        compiler_params=params(8),
        cost_estimate=cost(0, 4 * n * ask_block * LANES),
        name="pack_queries",
    )(codes, *keep_in(HBM, cache_len), turned)
    packed, late_tokens, late = lax.optimization_barrier((packed, tokens, w_gate_up))
    asked = lax.all_to_all(packed, "req", split_axis=0, concat_axis=0, tiled=True)

    if pieces == 2:
        half_mid, half_last = pl.pallas_call(
            functools.partial(cut_last, pieces=2),
            out_shape=(VMEM((middle, units), BF16), VMEM((model - first - middle, units), BF16)),
            in_specs=[whole(SMEM), whole(HBM)],
            out_specs=(whole(),) * 2,
            scratch_shapes=[pltpu.SemaphoreType.DMA((3,))],
            compiler_params=params(4),
            cost_estimate=cost(0, 4 * (model - first) * units),
            name="cut_last",
        )(side, *keep_in(HBM, late))

    keys, values = pl.pallas_call(
        project_keys,
        out_shape=(HBM((group_rows, width), BF16),) * 2,
        in_specs=[whole()] * 4,
        out_specs=(whole(),) * 2,
        compiler_params=params(12),
        cost_estimate=cost(
            4 * group_rows * model * width, 2 * model * (group_rows + 2 * width)
        ),
        name="project_keys",
    )(*keep_in(HBM, late_tokens, norm_attn.reshape(1, -1), w_key, w_value))

    row_block = pl.BlockSpec((draft, width), lambda r, *_: (r, 0))
    fixed_block = pl.BlockSpec((fixed_count, width), lambda r, *_: (0, 0))
    matrix_block = pl.BlockSpec((1, heads, HD, HD), lambda r, *_: (r, 0, 0, 0))
    span_block = pl.BlockSpec((span, HD), lambda r, *_: (r, 0))
    own, retrieved, own_top, own_sum = pl.pallas_call(
        functools.partial(local_attention, heads=heads, draft=draft, scale=scale),
        grid=(reqs,),
        out_shape=(
            HBM((reqs * span, HD), F32),
            HBM((reqs * span, HD), F32),
            jax.ShapeDtypeStruct((reqs, LANES), F32),
            jax.ShapeDtypeStruct((reqs, LANES), F32),
        ),
        in_specs=[
            row_block,
            row_block,
            row_block,
            fixed_block,
            fixed_block,
            pl.BlockSpec((1, draft, draft), lambda r: (r, 0, 0)),
            matrix_block,
        ],
        out_specs=(span_block, span_block) + (pl.BlockSpec((reqs, LANES), lambda r: (0, 0)),) * 2,
        compiler_params=params(10),
        cost_estimate=cost(1, 1),
        name="local_attention",
    )(*keep_in(HBM, queries, keys, values, persist_keys, persist_values, tree_mask, memory))

    memory_out, momentum_out = pl.pallas_call(
        functools.partial(update_memory, reqs=reqs, draft=draft, heads=heads, steps=steps),
        out_shape=(HBM(memory.shape, F32),) * 2,
        in_specs=[whole(SMEM)] * 4 + [whole()] * 2 + [whole(HBM)] * 2,
        out_specs=(whole(HBM),) * 2,
        scratch_shapes=[
            pltpu.VMEM(memory.shape, F32),
            pltpu.VMEM(memory.shape, F32),
            pltpu.VMEM((draft, width), F32),
            pltpu.VMEM((draft, width), F32),
            pltpu.VMEM((LANES, HD), F32),
            pltpu.VMEM((heads * steps, HD), F32),
            pltpu.VMEM((HD, LANES), F32),
            pltpu.SemaphoreType.DMA((2, reqs)),
            pltpu.SemaphoreType.DMA((2, reqs)),
        ],
        compiler_params=params(16),
        cost_estimate=cost(
            14 * reqs * heads * HD * HD * steps * 8, 16 * reqs * heads * HD * HD
        ),
        name="update_memory",
    )(
        jnp.transpose(accept_path),
        accept_len,
        jnp.transpose(momentum_code, (1, 2, 0)),
        jnp.transpose(forget_code, (1, 2, 0)),
        *keep_in(HBM, keys, values, memory, momentum),
    )

    if pieces == 2:
        memory_out, momentum_out, half_mid, half_last, one_a, one_q = lax.optimization_barrier(
            (memory_out, momentum_out, half_mid, half_last, one_a, one_q)
        )
        other_core = [(i, i ^ 1) for i in range(n)]
        other_chip = [(i, i ^ 2) for i in range(n)]
        one_m = lax.ppermute(half_mid, "grp", swap)
        one_b = lax.ppermute(half_last, "grp", swap)
        three_q = lax.ppermute(one_q[:near], "req", other_chip)
        three_r = lax.ppermute(one_q[near:], "req", other_chip)
    asked, memory_out, momentum_out, keys, values = lax.optimization_barrier(
        (asked, memory_out, momentum_out, keys, values)
    )
    answers = pl.pallas_call(
        functools.partial(
            page_attention, n=n, cap=cap, draft=draft, heads=heads, page_len=page_len,
            scale=scale, group=math.gcd(n, 4),
        ),
        out_shape=HBM((n * block, LANES), BF16),
        in_specs=[whole(), whole(HBM)],
        out_specs=whole(HBM),
        scratch_shapes=[
            pltpu.VMEM((n, cap) + kv_cache.shape[1:], BF16),
            pltpu.VMEM((n * block, LANES), BF16),
            pltpu.SemaphoreType.DMA((n,)),
            pltpu.SemaphoreType.DMA((n,)),
        ],
        compiler_params=params(24),
        cost_estimate=cost(
            4 * slots * span * page_len * HD,
            4 * slots * page_len * width + 4 * n * block * LANES,
            slots * span * page_len,
        ),
        name="page_attention",
    )(asked, *keep_in(HBM, kv_cache))
    if pieces == 2:
        answers, one_m, three_q = lax.optimization_barrier((answers, one_m, three_q))
        _, one_a, one_q = lax.optimization_barrier((answers, one_a, one_q))
        own, one_m, three_q = lax.optimization_barrier((own, one_m, three_q))
        two_a, two_q, two_m, four_q = (
            lax.ppermute(part, "req", other_core) for part in (one_a, one_q, one_m, three_q)
        )
    returned = lax.all_to_all(answers, "req", split_axis=0, concat_axis=0, tiled=True)
    if pieces == 2:
        returned, one_b, two_a, two_m, two_q, four_q, three_r, own, retrieved = (
            lax.optimization_barrier(
                (returned, one_b, two_a, two_m, two_q, four_q, three_r, own, retrieved)
            )
        )
        two_b = lax.ppermute(one_b, "req", other_core)
        four_r = lax.ppermute(three_r, "req", other_core)
    rows = group_rows // grp
    mixed = pl.pallas_call(
        functools.partial(
            combine, n=n, cap=cap, reqs=reqs, draft=draft, heads=heads, pieces=pieces
        ),
        out_shape=(jax.ShapeDtypeStruct((group_rows // pieces, width), BF16),) * pieces,
        in_specs=[whole(SMEM)] * 2 + [whole()] + [whole(HBM)] * 2 + [whole()] * 2,
        out_specs=(whole(),) * pieces,
        scratch_shapes=[
            pltpu.VMEM((slots, LANES), F32),
            pltpu.VMEM((slots, LANES), F32),
            pltpu.VMEM((reqs, LANES), F32),
            pltpu.VMEM((reqs, LANES), F32),
            pltpu.VMEM((LANES, LANES), F32),
            pltpu.VMEM((LANES, LANES), F32),
            pltpu.VMEM((reqs * span, HD), F32),
            pltpu.VMEM((group_rows, width), BF16),
            pltpu.VMEM((reqs * span, HD), F32),
            pltpu.VMEM((reqs * span, HD), F32),
            pltpu.SemaphoreType.DMA((2,)),
        ],
        compiler_params=params(12),
        cost_estimate=cost(
            8 * slots * span * HD, 2 * n * block * LANES + 8 * reqs * span * HD
        ),
        name="combine",
    )(codes, side, returned, *keep_in(HBM, own, retrieved), own_top, own_sum)

    if pieces == 2:
        mine, asked_for = mixed
        theirs = lax.ppermute(asked_for, "grp", swap)
        mine, two_b, four_r = lax.optimization_barrier((mine, two_b, four_r))
        out_near, gate_up_near, down_near = pl.pallas_call(
            stage_weights,
            out_shape=(
                VMEM((2,) + w_out.shape, BF16),
                VMEM((2,) + w_gate_up.shape, BF16),
                VMEM((2,) + w_down.shape, BF16),
            ),
            in_specs=[whole(SMEM)] + [whole(pl.ANY)] * 15,
            out_specs=(whole(),) * 3,
            scratch_shapes=[pltpu.SemaphoreType.DMA((19,))],
            compiler_params=params(2),
            cost_estimate=cost(0, 2 * model * (2 * width + 6 * units)),
            name="stage_weights",
        )(
            side,
            *keep_in(
                HBM, w_out, w_gate_up, w_down, one_a, one_m, one_b, one_q, two_a, two_m, two_q,
                three_q, three_r, four_q,
            ),
            two_b,
            four_r,
        )
        layer_out = pl.pallas_call(
            feed_forward,
            out_shape=jax.ShapeDtypeStruct((rows, model), BF16),
            in_specs=[whole(SMEM)] + [whole()] * 7,
            out_specs=whole(),
            scratch_shapes=[
                pltpu.VMEM((rows, model), BF16),
                pltpu.VMEM((2, rows, units), BF16),
            ],
            compiler_params=params(14),
            cost_estimate=cost(
                4 * rows * model * (width + 3 * units), 4 * model * (width + 3 * units)
            ),
            name="feed_forward",
        )(
            side, tokens, mine, theirs, norm_ffn.reshape(1, -1),
            *keep_in(VMEM, out_near, gate_up_near, down_near),
        )
        return (layer_out, memory_out, momentum_out)

    partial_out = jnp.dot(mixed[0], w_out, preferred_element_type=F32).astype(BF16)
    head_sum = lax.psum_scatter(partial_out, "grp", scatter_dimension=0, tiled=True).astype(F32)
    own_rows = lax.dynamic_slice_in_dim(tokens, lax.axis_index("grp") * rows, rows, 0)
    residual = (own_rows.astype(F32) + head_sum).astype(BF16)
    ffn_in = rms_norm(residual, norm_ffn)
    piece = lax.all_gather(ffn_in, "grp", axis=0, tiled=True)
    gate = jnp.dot(piece, w_gate_up[0], preferred_element_type=F32)
    up = jnp.dot(piece, w_gate_up[1], preferred_element_type=F32)
    hidden = (jax.nn.silu(gate) * up).astype(BF16)
    ffn_out = lax.psum_scatter(
        jnp.dot(hidden, w_down, preferred_element_type=F32).astype(BF16),
        "grp",
        scatter_dimension=0,
        tiled=True,
    ).astype(F32)
    layer_out = (residual.astype(F32) + ffn_out).astype(BF16)
    return (layer_out, memory_out, momentum_out)


def solution(mesh):
    return jax.shard_map(
        on_device,
        mesh=mesh,
        in_specs=(
            P("req", None),
            P(),
            P(None, "grp"),
            P(None, "grp"),
            P(None, "grp"),
            P("grp", None),
            P(None, "grp"),
            P(None, "grp"),
            P("req", None, None, "grp"),
            P("req"),
            P("req"),
            P("req"),
            P("req", None, None),
            P("req", None),
            P("req"),
            P("req", "grp", None, None),
            P("req", "grp", None, None),
            P("req", None, "grp"),
            P("req", None, "grp"),
            P(),
            P(None, None, "grp"),
            P("grp", None),
        ),
        out_specs=(
            P(("req", "grp"), None),
            P("req", "grp", None, None),
            P("req", "grp", None, None),
        ),
        check_vma=False,
    )
```

```python
import functools
import math

import jax
import jax.numpy as jnp
from jax import lax
from jax.experimental import pallas as pl
from jax.experimental.pallas import tpu as pltpu
from jax.sharding import PartitionSpec as P

HD = 128
LANES = 128
EXTRA = 16
TOP_PARTS = 3
WEIGHT = 20
SUM_PARTS = 2

EPS = 1e-06
THETA = 0.5
NEG = -1e30

VMEM = pltpu.VMEM
SMEM = pltpu.SMEM
HBM = pltpu.HBM
F32 = jnp.float32
BF16 = jnp.bfloat16


def whole(space=VMEM):
    return pl.BlockSpec(memory_space=space)


def cost(flops, moved, special=0):
    return pl.CostEstimate(
        flops=WEIGHT * flops, bytes_accessed=WEIGHT * moved, transcendentals=special
    )


def keep_in(space, *arrays):
    return tuple(pltpu.with_memory_space_constraint(array, space) for array in arrays)


def params(mib=40):
    return pltpu.CompilerParams(vmem_limit_bytes=mib << 20)


def rms_norm(rows, gain):
    values = rows.astype(F32)
    factor = lax.rsqrt(jnp.mean(values * values, axis=-1, keepdims=True) + EPS)
    return (values * factor * gain).astype(BF16)


def nt_dot(left, right):
    return lax.dot_general(left, right, (((1,), (1,)), ((), ())), preferred_element_type=F32)


def column_to_row(column, count):
    row_id = lax.broadcasted_iota(jnp.int32, (count, LANES), 0)
    lane_id = lax.broadcasted_iota(jnp.int32, (count, LANES), 1)
    spread = jnp.where(row_id == lane_id, jnp.broadcast_to(column, (count, LANES)), 0.0)
    return jnp.sum(spread, axis=0, keepdims=True)


def split_parts(row, count):
    parts = []
    for _ in range(count):
        part = row.astype(BF16).astype(F32)
        parts.append(part)
        row = row - part
    return parts


def project_queries(*refs, reqs, draft, heads, cut):
    copies = []
    if cut:
        side, gate_up_w, down_w, out_w, *refs, q_ref, q_sem, sems = refs
        *refs, first_ref, quarter_ref = refs
        refs += [q_ref, q_sem]
        copies = run_copies(
            first_pairs(side, gate_up_w, down_w, out_w, first_ref, quarter_ref), sems
        )
    tok_ref, gain_ref, w_ref, q_hbm, turned_ref, q_ref, q_sem = refs
    normed = rms_norm(tok_ref[...], gain_ref[...])
    q_ref[...] = jnp.dot(normed, w_ref[...], preferred_element_type=F32).astype(BF16)
    copies.append(pltpu.make_async_copy(q_ref, q_hbm, q_sem.at[0]))
    copies[-1].start()
    span = heads * draft
    for r in range(reqs):
        rows = slice(r * draft, (r + 1) * draft)
        pieces = [q_ref[rows, h * HD : (h + 1) * HD].astype(F32) for h in range(heads)]
        if span < LANES:
            pieces.append(jnp.zeros((LANES - span, HD), F32))
        tile = jnp.concatenate(pieces, axis=0)
        turned_ref[r * HD : (r + 1) * HD, :] = jnp.transpose(tile).astype(BF16)
    for copy in copies:
        copy.wait()


def project_keys(tok_ref, gain_ref, wk_ref, wv_ref, k_ref, v_ref):
    normed = rms_norm(tok_ref[...], gain_ref[...])
    k_ref[...] = jnp.dot(normed, wk_ref[...], preferred_element_type=F32).astype(BF16)
    v_ref[...] = jnp.dot(normed, wv_ref[...], preferred_element_type=F32).astype(BF16)


def pack_queries(codes, lengths, turned_ref, out_hbm, out_ref, sems, *, n, cap, reqs, page_len):
    block = cap * HD + EXTRA
    row_id = lax.broadcasted_iota(jnp.int32, (EXTRA, LANES), 0)

    def departure(d):
        rows = pl.ds(pl.multiple_of(d * block, EXTRA), block)
        return pltpu.make_async_copy(out_ref.at[rows], out_hbm.at[rows], sems.at[d])

    def one(d, carry):
        base = pl.multiple_of(d * block, EXTRA)
        tail = jnp.zeros((EXTRA, LANES), F32)
        for c in range(cap):
            code = codes[d, 0, c]
            r = lax.rem(code, reqs)
            page = lax.div(code, reqs)
            live = jnp.clip(lengths[r] - page * page_len, 0, page_len)
            tail = jnp.where(row_id == c, live.astype(F32), tail)
            rows = pl.ds(pl.multiple_of(r * HD, HD), HD)
            out_ref[pl.ds(base + c * HD, HD), :] = turned_ref[rows, :]
        out_ref[pl.ds(base + cap * HD, EXTRA), :] = tail.astype(BF16)
        departure(d).start()
        return carry

    lax.fori_loop(0, n, one, 0)
    for d in range(n):
        departure(d).wait()


def page_attention(
    q_ref, kv_hbm, out_hbm, kv_buf, out_buf, in_sems, out_sems,
    *, n, cap, draft, heads, page_len, scale, group,
):
    span = heads * draft
    ask_block = cap * HD + EXTRA
    block = cap * span + EXTRA
    token = lax.broadcasted_iota(jnp.int32, (page_len, LANES), 0).astype(F32)
    row_id = lax.broadcasted_iota(jnp.int32, (EXTRA, LANES), 0)
    head_of = lax.broadcasted_iota(jnp.int32, (HD, LANES), 1) // draft

    def arrival(d):
        return pltpu.make_async_copy(
            kv_hbm.at[pl.ds(d * cap, cap)], kv_buf.at[d], in_sems.at[d]
        )

    def departure(d):
        rows = pl.ds(pl.multiple_of(d * block, EXTRA), block)
        return pltpu.make_async_copy(out_buf.at[rows], out_hbm.at[rows], out_sems.at[d])

    for d in range(n):
        arrival(d).start()

    def one(i, carry):
        pairs = [(i * group + g, c) for g in range(group) for c in range(cap)]
        limits = []
        for g in range(group):
            d = i * group + g
            arrival(d).wait()
            at = pl.multiple_of(d * ask_block + cap * HD, EXTRA)
            limits.append(q_ref[pl.ds(at, EXTRA), :].astype(F32))
        all_scores = []
        for d, c in pairs:
            at = pl.multiple_of(d * ask_block + c * HD, EXTRA)
            turned = q_ref[pl.ds(at, HD), :]
            blocks = [jnp.where(head_of == h, turned, jnp.zeros_like(turned)) for h in range(heads)]
            all_scores.append(
                jnp.dot(
                    kv_buf[d, c, 0], jnp.concatenate(blocks, axis=0), preferred_element_type=F32
                )
            )
        all_weights = []
        tails = [jnp.zeros((EXTRA, LANES), F32) for _ in range(group)]
        for j, (d, c) in enumerate(pairs):
            g = j // cap
            scores = jnp.where(token < limits[g][c : c + 1, :], all_scores[j] * scale, NEG)
            top = jnp.max(scores, axis=0, keepdims=True)
            weight = jnp.exp(scores - top)
            total = jnp.sum(weight, axis=0, keepdims=True)
            all_weights.append(jnp.transpose(weight).astype(BF16))
            parts = split_parts(top, TOP_PARTS) + split_parts(total, SUM_PARTS)
            for p, part in enumerate(parts):
                tails[g] = jnp.where(row_id == p * cap + c, part, tails[g])
        for j, (d, c) in enumerate(pairs):
            for h in range(heads):
                numer = jnp.dot(
                    all_weights[j][h * draft : (h + 1) * draft, :],
                    kv_buf[d, c, 1, :, h * HD : (h + 1) * HD],
                    preferred_element_type=F32,
                )
                at = pl.multiple_of(d * block + c * span + h * draft, EXTRA)
                out_buf[pl.ds(at, draft), :] = numer.astype(BF16)
        for g in range(group):
            d = i * group + g
            at = pl.multiple_of(d * block + cap * span, EXTRA)
            out_buf[pl.ds(at, EXTRA), :] = tails[g].astype(BF16)
            departure(d).start()
        return carry

    lax.fori_loop(0, n // group, one, 0)
    for d in range(n):
        departure(d).wait()


def local_attention(
    q_ref, k_ref, v_ref, pk_ref, pv_ref, mask_ref, mem_ref,
    o_ref, ret_ref, top_ref, sum_ref, *, heads, draft, scale,
):
    r = pl.program_id(0)
    seen = mask_ref[0] == 1
    tops, totals = [], []
    for h in range(heads):
        cols = slice(h * HD, (h + 1) * HD)
        rows = slice(h * draft, (h + 1) * draft)
        query = q_ref[:, cols]
        tree = jnp.where(seen, nt_dot(query, k_ref[:, cols]) * scale, NEG)
        fixed = nt_dot(query, pk_ref[:, cols]) * scale
        top = jnp.maximum(
            jnp.max(tree, axis=1, keepdims=True), jnp.max(fixed, axis=1, keepdims=True)
        )
        tree_w = jnp.exp(tree - top)
        fixed_w = jnp.exp(fixed - top)
        total = jnp.sum(tree_w, axis=1, keepdims=True) + jnp.sum(fixed_w, axis=1, keepdims=True)
        numer = jnp.dot(tree_w.astype(BF16), v_ref[:, cols], preferred_element_type=F32)
        numer = numer + jnp.dot(fixed_w.astype(BF16), pv_ref[:, cols], preferred_element_type=F32)
        o_ref[rows, :] = numer
        tops.append(top)
        totals.append(total)
        wide = query.astype(F32)
        unit = wide * lax.rsqrt(jnp.sum(wide * wide, axis=1, keepdims=True) + EPS)
        ret_ref[rows, :] = jnp.dot(
            unit, mem_ref[0, h], preferred_element_type=F32, precision=lax.Precision.HIGHEST
        )
    span = heads * draft
    top_ref[pl.ds(r, 1), :] = column_to_row(jnp.concatenate(tops, axis=0), span)
    sum_ref[pl.ds(r, 1), :] = column_to_row(jnp.concatenate(totals, axis=0), span)


def update_memory(
    path, count, mom_code, forget_code, k_ref, v_ref, mem_hbm, mom_hbm, mem_out, mom_out,
    mem_buf, mom_buf, wide_k, wide_v, unit_ref, value_ref, turned_ref, in_sems, out_sems,
    *, reqs, draft, heads, steps,
):
    def arrivals(r):
        return (
            pltpu.make_async_copy(mem_hbm.at[r], mem_buf.at[r], in_sems.at[0, r]),
            pltpu.make_async_copy(mom_hbm.at[r], mom_buf.at[r], in_sems.at[1, r]),
        )

    def departures(r):
        return (
            pltpu.make_async_copy(mem_buf.at[r], mem_out.at[r], out_sems.at[0, r]),
            pltpu.make_async_copy(mom_buf.at[r], mom_out.at[r], out_sems.at[1, r]),
        )

    for r in range(reqs):
        for copy in arrivals(r):
            copy.start()
    unit_ref[...] = jnp.zeros_like(unit_ref)

    def one(r, carry):
        rows = pl.ds(pl.multiple_of(r * draft, draft), draft)
        wide_k[...] = k_ref[rows, :].astype(F32)
        wide_v[...] = v_ref[rows, :].astype(F32)
        for n in range(steps):
            node = path[n, r]
            k_row = wide_k[pl.ds(node, 1), :]
            v_row = wide_v[pl.ds(node, 1), :]
            for h in range(heads):
                unit_ref[h * steps + n : h * steps + n + 1, :] = k_row[:, h * HD : (h + 1) * HD]
                value_ref[h * steps + n : h * steps + n + 1, :] = v_row[:, h * HD : (h + 1) * HD]
        keys = unit_ref[...]
        unit = keys * lax.rsqrt(jnp.sum(keys * keys, axis=1, keepdims=True) + EPS)
        turned_ref[...] = jnp.transpose(unit)
        for copy in arrivals(r):
            copy.wait()

        def advance(n):
            for h in range(heads):
                eta = 0.97 - 0.06 * mom_code[n, h, r].astype(F32)
                keep = 1.0 - (0.01 + 0.02 * forget_code[n, h, r].astype(F32))
                row = h * steps + n
                column = turned_ref[:, row : row + 1]
                matrix = mem_buf[r, h]
                predicted = jnp.sum(column * matrix, axis=0, keepdims=True)
                error = THETA * (predicted - value_ref[row : row + 1, :])
                moved = eta * mom_buf[r, h] - column * error
                mom_buf[r, h] = moved
                mem_buf[r, h] = keep * matrix + moved

        for n in range(steps):
            pl.when(n < count[r])(functools.partial(advance, n))
        for copy in departures(r):
            copy.start()
        return carry

    lax.fori_loop(0, reqs, one, 0)
    for r in range(reqs):
        for copy in departures(r):
            copy.wait()


def combine(
    codes, side, msg_ref, o_hbm, ret_hbm, own_top_ref, own_sum_ref, *rest,
    n, cap, reqs, draft, heads, pieces,
):
    outs = rest[:pieces]
    part_top, part_sum, best, total, weight, own_weight, acc, mixed, o_ref, ret_ref, sems = rest[
        pieces:
    ]
    copies = [
        pltpu.make_async_copy(o_hbm, o_ref, sems.at[0]),
        pltpu.make_async_copy(ret_hbm, ret_ref, sems.at[1]),
    ]
    for copy in copies:
        copy.start()
    span = heads * draft
    block = cap * span + EXTRA
    slots = n * cap
    for d in range(n):
        at = d * block + cap * span
        tail = msg_ref[at : at + EXTRA, :].astype(F32)
        rows = [tail[p * cap : (p + 1) * cap] for p in range(TOP_PARTS + SUM_PARTS)]
        part_top[d * cap : (d + 1) * cap, :] = rows[0] + rows[1] + rows[2]
        part_sum[d * cap : (d + 1) * cap, :] = rows[3] + rows[4]
    best[...] = own_top_ref[...]
    owners = [lax.rem(codes[s // cap, 0, s % cap], reqs) for s in range(slots)]
    for s in range(slots):
        r = owners[s]
        best[pl.ds(r, 1), :] = jnp.maximum(best[pl.ds(r, 1), :], part_top[s : s + 1, :])
    own_weight[...] = jnp.zeros_like(own_weight)
    weight[...] = jnp.zeros_like(weight)
    start = jnp.exp(own_top_ref[...] - best[...])
    total[...] = start * own_sum_ref[...]
    for s in range(slots):
        r = owners[s]
        term = jnp.exp(part_top[s : s + 1, :] - best[pl.ds(r, 1), :])
        weight[s : s + 1, :] = term
        total[pl.ds(r, 1), :] = total[pl.ds(r, 1), :] + term * part_sum[s : s + 1, :]
    inverse = 1.0 / total[...]
    own_weight[0:reqs, :] = start * inverse
    total[...] = inverse
    for s in range(slots):
        weight[s : s + 1, :] = weight[s : s + 1, :] * total[pl.ds(owners[s], 1), :]
    turned = jnp.transpose(weight[...])
    own_turned = jnp.transpose(own_weight[...])
    for copy in copies:
        copy.wait()
    for r in range(reqs):
        rows = slice(r * span, (r + 1) * span)
        acc[rows, :] = o_ref[rows, :] * own_turned[0:span, r : r + 1] + ret_ref[rows, :]
    for s in range(slots):
        at = (s // cap) * block + (s % cap) * span
        rows = pl.ds(pl.multiple_of(owners[s] * span, span), span)
        acc[rows, :] = acc[rows, :] + msg_ref[at : at + span, :].astype(F32) * turned[
            0:span, s : s + 1
        ]
    for r in range(reqs):
        for h in range(heads):
            at = r * span + h * draft
            mixed[r * draft : (r + 1) * draft, h * HD : (h + 1) * HD] = acc[
                at : at + draft, :
            ].astype(BF16)
    rows = reqs * draft // pieces
    for p, out_ref in enumerate(outs):
        first = lax.rem(side[0] + p, pieces) * rows
        out_ref[...] = mixed[pl.ds(pl.multiple_of(first, rows), rows), :]


def run_copies(pairs, sems):
    copies = [
        pltpu.make_async_copy(source, target, sems.at[i])
        for i, (source, target) in enumerate(pairs)
    ]
    for copy in copies:
        copy.start()
    return copies


def first_pairs(side, gate_up_w, down_w, out_w, first_ref, quarter_ref):
    depth, width = down_w.shape[0] // 4, out_w.shape[0] // 4
    down_rows = pl.ds(pl.multiple_of(side[2] * depth, EXTRA), depth)
    out_rows = pl.ds(pl.multiple_of(side[2] * width, EXTRA), width)
    pairs = [
        (down_w.at[down_rows], quarter_ref.at[pl.ds(0, depth)]),
        (out_w.at[out_rows], quarter_ref.at[pl.ds(depth, width)]),
    ]
    step = first_ref.shape[0] // 2
    for i in range(2):
        rows = pl.ds(i * step, step)
        pairs.append((gate_up_w.at[side[1], rows], first_ref.at[rows]))
    return pairs


def cut_last(side, gate_up_w, mid_ref, last_ref, sems, *, pieces):
    step = last_ref.shape[0] // pieces
    start = gate_up_w.shape[1] - last_ref.shape[0]
    half = gate_up_w.at[side[1]]
    middle = mid_ref.shape[0]
    pairs = [(half.at[pl.ds(start - middle, middle)], mid_ref)]
    for i in range(pieces):
        pairs.append((half.at[pl.ds(start + i * step, step)], last_ref.at[pl.ds(i * step, step)]))
    for copy in run_copies(pairs, sems):
        copy.wait()


def stage_weights(
    side, out_w, gate_up_w, down_w, one_a, one_m, one_b, one_q, two_a, two_m, two_q, three_q,
    three_r, four_q, two_b, four_r, out_all, gate_up_all, down_all, sems,
):
    width, depth = out_w.shape[0] // 4, down_w.shape[0] // 4
    pairs = [(gate_up_w, gate_up_all.at[0]), (down_w, down_all.at[0]), (out_w, out_all.at[0])]
    for half, parts in ((side[1], (one_a, one_m, one_b)), (1 - side[1], (two_a, two_m, two_b))):
        at = 0
        for part in parts:
            pairs.append((part, gate_up_all.at[1, half, pl.ds(at, part.shape[0])]))
            at += part.shape[0]
    core, chip = side[1], side[2] // 2
    near = three_q.shape[0]
    places = ((core, chip), (1 - core, chip), (core, 1 - chip), (1 - core, 1 - chip))
    got = ((one_q,), (two_q,), (three_q, three_r), (four_q, four_r))
    for (x, y), parts in zip(places, got):
        base = pl.multiple_of((2 * y + x) * depth, EXTRA)
        rows = pl.ds(pl.multiple_of((2 * y + x) * width, EXTRA), width)
        if len(parts) == 2:
            pairs.append((parts[0], down_all.at[1, pl.ds(base, near)]))
        at = near if len(parts) == 2 else 0
        rest = depth - at
        pairs.append((parts[-1].at[pl.ds(0, rest)], down_all.at[1, pl.ds(base + at, rest)]))
        pairs.append((parts[-1].at[pl.ds(rest, width)], out_all.at[1, rows]))
    for copy in run_copies(pairs, sems):
        copy.wait()


def feed_forward(
    side, tok_ref, mine_ref, theirs_ref, gain_ref, out_w, gate_up_w, down_w, out_ref,
    residual, hidden,
):
    rows = mine_ref.shape[0]
    units = gate_up_w.shape[3]
    tokens = tok_ref[pl.ds(pl.multiple_of(side[0] * rows, rows), rows), :].astype(F32)
    summed = tokens + jnp.dot(mine_ref[...], out_w[0], preferred_element_type=F32)
    summed = summed + jnp.dot(theirs_ref[...], out_w[1], preferred_element_type=F32)
    residual[...] = summed.astype(BF16)
    ffn_in = rms_norm(residual[...], gain_ref[...])
    step = 256
    for half in range(2):
        for first in range(0, units, step):
            cols = slice(first, min(first + step, units))
            gate = jnp.dot(ffn_in, gate_up_w[half, 0, :, cols], preferred_element_type=F32)
            up = jnp.dot(ffn_in, gate_up_w[half, 1, :, cols], preferred_element_type=F32)
            hidden[half, :, cols] = (gate / (1.0 + jnp.exp(-gate)) * up).astype(BF16)
    for at in range(0, out_ref.shape[1], step):
        cols = slice(at, at + step)
        total = residual[:, cols].astype(F32)
        for half in range(2):
            total = total + jnp.dot(hidden[half], down_w[half, :, cols], preferred_element_type=F32)
        out_ref[:, cols] = total.astype(BF16)


def on_device(
    tokens,
    norm_attn,
    w_query,
    w_key,
    w_value,
    w_out,
    persist_keys,
    persist_values,
    kv_cache,
    slot_request,
    slot_page,
    cache_len,
    tree_mask,
    accept_path,
    accept_len,
    memory,
    momentum,
    momentum_code,
    forget_code,
    norm_ffn,
    w_gate_up,
    w_down,
):
    n = lax.axis_size("req")
    group_rows, model = tokens.shape
    reqs = cache_len.shape[0]
    draft = tree_mask.shape[1]
    steps = accept_path.shape[1]
    width = w_query.shape[1]
    heads = width // HD
    span = heads * draft
    slots = kv_cache.shape[0]
    cap = slots // n
    fixed_count = persist_keys.shape[0]
    page_len = kv_cache.shape[2]
    ask_block = cap * HD + EXTRA
    block = cap * span + EXTRA
    scale = 1.0 / math.sqrt(HD)

    label = (slot_page * reqs + lax.rem(slot_request, reqs)).reshape(n, 1, cap)
    codes = lax.all_to_all(label, "req", split_axis=0, concat_axis=0, tiled=True)

    grp = lax.axis_size("grp")
    depth, out_depth = w_down.shape[0] // 4, width // 4
    first, middle = model // 4, model * 6 // 32
    near = depth * 6 // 11 // EXTRA * EXTRA
    split = (depth, out_depth, first // 2, middle, (model - first - middle) // 2)
    pieces = 2 if grp == 2 and n % 4 == 0 and not any(size % EXTRA for size in split) else 1
    quarter = lax.rem(lax.axis_index("req"), 4)
    core = lax.rem(quarter, 2)
    side = jnp.stack([lax.axis_index("grp"), core, quarter]).astype(jnp.int32)

    cut, units = pieces == 2, w_down.shape[0]
    cuts = ((first, units), (depth + out_depth, model)) if cut else ()
    queries, turned, *shares = pl.pallas_call(
        functools.partial(project_queries, reqs=reqs, draft=draft, heads=heads, cut=cut),
        out_shape=(
            HBM((group_rows, width), BF16),
            jax.ShapeDtypeStruct((reqs * HD, LANES), BF16),
        )
        + tuple(VMEM(shape, BF16) for shape in cuts),
        in_specs=([whole(SMEM)] + [whole(HBM)] * 3) * cut + [whole()] * 3,
        out_specs=(whole(HBM),) + (whole(),) * (1 + len(cuts)),
        scratch_shapes=[pltpu.VMEM((group_rows, width), BF16), pltpu.SemaphoreType.DMA((1,))]
        + [pltpu.SemaphoreType.DMA((4,))] * cut,
        compiler_params=params(14),
        cost_estimate=cost(
            2 * group_rows * model * width, 2 * model * (2 * group_rows + width)
        ),
        name="project_queries",
    )(
        *((side, *keep_in(HBM, w_gate_up, w_down, w_out)) if cut else ()),
        *keep_in(HBM, tokens, norm_attn.reshape(1, -1), w_query),
    )
    if cut:
        half_first, quarters = shares

    if pieces == 2:
        turned, half_first, quarters = lax.optimization_barrier((turned, half_first, quarters))
        swap = [(0, 1), (1, 0)]
        one_a = lax.ppermute(half_first, "grp", swap)
        one_q = lax.ppermute(quarters, "grp", swap)

    packed = pl.pallas_call(
        functools.partial(pack_queries, n=n, cap=cap, reqs=reqs, page_len=page_len),
        out_shape=HBM((n * ask_block, LANES), BF16),
        in_specs=[whole(SMEM), whole(SMEM), whole()],
        out_specs=whole(HBM),
        scratch_shapes=[
            pltpu.VMEM((n * ask_block, LANES), BF16),
            pltpu.SemaphoreType.DMA((n,)),
        ],
        compiler_params=params(8),
        cost_estimate=cost(0, 4 * n * ask_block * LANES),
        name="pack_queries",
    )(codes, *keep_in(HBM, cache_len), turned)
    packed, late_tokens, late = lax.optimization_barrier((packed, tokens, w_gate_up))
    asked = lax.all_to_all(packed, "req", split_axis=0, concat_axis=0, tiled=True)

    if pieces == 2:
        half_mid, half_last = pl.pallas_call(
            functools.partial(cut_last, pieces=2),
            out_shape=(VMEM((middle, units), BF16), VMEM((model - first - middle, units), BF16)),
            in_specs=[whole(SMEM), whole(HBM)],
            out_specs=(whole(),) * 2,
            scratch_shapes=[pltpu.SemaphoreType.DMA((3,))],
            compiler_params=params(4),
            cost_estimate=cost(0, 4 * (model - first) * units),
            name="cut_last",
        )(side, *keep_in(HBM, late))

    keys, values = pl.pallas_call(
        project_keys,
        out_shape=(HBM((group_rows, width), BF16),) * 2,
        in_specs=[whole()] * 4,
        out_specs=(whole(),) * 2,
        compiler_params=params(12),
        cost_estimate=cost(
            4 * group_rows * model * width, 2 * model * (group_rows + 2 * width)
        ),
        name="project_keys",
    )(*keep_in(HBM, late_tokens, norm_attn.reshape(1, -1), w_key, w_value))

    row_block = pl.BlockSpec((draft, width), lambda r, *_: (r, 0))
    fixed_block = pl.BlockSpec((fixed_count, width), lambda r, *_: (0, 0))
    matrix_block = pl.BlockSpec((1, heads, HD, HD), lambda r, *_: (r, 0, 0, 0))
    span_block = pl.BlockSpec((span, HD), lambda r, *_: (r, 0))
    own, retrieved, own_top, own_sum = pl.pallas_call(
        functools.partial(local_attention, heads=heads, draft=draft, scale=scale),
        grid=(reqs,),
        out_shape=(
            HBM((reqs * span, HD), F32),
            HBM((reqs * span, HD), F32),
            jax.ShapeDtypeStruct((reqs, LANES), F32),
            jax.ShapeDtypeStruct((reqs, LANES), F32),
        ),
        in_specs=[
            row_block,
            row_block,
            row_block,
            fixed_block,
            fixed_block,
            pl.BlockSpec((1, draft, draft), lambda r: (r, 0, 0)),
            matrix_block,
        ],
        out_specs=(span_block, span_block) + (pl.BlockSpec((reqs, LANES), lambda r: (0, 0)),) * 2,
        compiler_params=params(10),
        cost_estimate=cost(1, 1),
        name="local_attention",
    )(*keep_in(HBM, queries, keys, values, persist_keys, persist_values, tree_mask, memory))

    memory_out, momentum_out = pl.pallas_call(
        functools.partial(update_memory, reqs=reqs, draft=draft, heads=heads, steps=steps),
        out_shape=(HBM(memory.shape, F32),) * 2,
        in_specs=[whole(SMEM)] * 4 + [whole()] * 2 + [whole(HBM)] * 2,
        out_specs=(whole(HBM),) * 2,
        scratch_shapes=[
            pltpu.VMEM(memory.shape, F32),
            pltpu.VMEM(memory.shape, F32),
            pltpu.VMEM((draft, width), F32),
            pltpu.VMEM((draft, width), F32),
            pltpu.VMEM((LANES, HD), F32),
            pltpu.VMEM((heads * steps, HD), F32),
            pltpu.VMEM((HD, LANES), F32),
            pltpu.SemaphoreType.DMA((2, reqs)),
            pltpu.SemaphoreType.DMA((2, reqs)),
        ],
        compiler_params=params(16),
        cost_estimate=cost(
            14 * reqs * heads * HD * HD * steps * 8, 16 * reqs * heads * HD * HD
        ),
        name="update_memory",
    )(
        jnp.transpose(accept_path),
        accept_len,
        jnp.transpose(momentum_code, (1, 2, 0)),
        jnp.transpose(forget_code, (1, 2, 0)),
        *keep_in(HBM, keys, values, memory, momentum),
    )

    if pieces == 2:
        memory_out, momentum_out, half_last, one_a, one_q = lax.optimization_barrier(
            (memory_out, momentum_out, half_last, one_a, one_q)
        )
        other_core = [(i, i ^ 1) for i in range(n)]
        other_chip = [(i, i ^ 2) for i in range(n)]
        one_m = lax.ppermute(half_mid, "grp", swap)
        one_b = lax.ppermute(half_last, "grp", swap)
        three_q = lax.ppermute(one_q[:near], "req", other_chip)
        three_r = lax.ppermute(one_q[near:], "req", other_chip)
    asked, memory_out, momentum_out, keys, values = lax.optimization_barrier(
        (asked, memory_out, momentum_out, keys, values)
    )
    answers = pl.pallas_call(
        functools.partial(
            page_attention, n=n, cap=cap, draft=draft, heads=heads, page_len=page_len,
            scale=scale, group=math.gcd(n, 4),
        ),
        out_shape=HBM((n * block, LANES), BF16),
        in_specs=[whole(), whole(HBM)],
        out_specs=whole(HBM),
        scratch_shapes=[
            pltpu.VMEM((n, cap) + kv_cache.shape[1:], BF16),
            pltpu.VMEM((n * block, LANES), BF16),
            pltpu.SemaphoreType.DMA((n,)),
            pltpu.SemaphoreType.DMA((n,)),
        ],
        compiler_params=params(24),
        cost_estimate=cost(
            4 * slots * span * page_len * HD,
            4 * slots * page_len * width + 4 * n * block * LANES,
            slots * span * page_len,
        ),
        name="page_attention",
    )(asked, *keep_in(HBM, kv_cache))
    if pieces == 2:
        answers, one_m, three_q = lax.optimization_barrier((answers, one_m, three_q))
        _, one_a, one_q = lax.optimization_barrier((answers, one_a, one_q))
        own, one_m, three_q = lax.optimization_barrier((own, one_m, three_q))
        two_a, two_q, two_m, four_q = (
            lax.ppermute(part, "req", other_core) for part in (one_a, one_q, one_m, three_q)
        )
    returned = lax.all_to_all(answers, "req", split_axis=0, concat_axis=0, tiled=True)
    if pieces == 2:
        returned, one_b, two_a, two_m, two_q, four_q, three_r, own, retrieved = (
            lax.optimization_barrier(
                (returned, one_b, two_a, two_m, two_q, four_q, three_r, own, retrieved)
            )
        )
        two_b = lax.ppermute(one_b, "req", other_core)
        four_r = lax.ppermute(three_r, "req", other_core)
    rows = group_rows // grp
    mixed = pl.pallas_call(
        functools.partial(
            combine, n=n, cap=cap, reqs=reqs, draft=draft, heads=heads, pieces=pieces
        ),
        out_shape=(jax.ShapeDtypeStruct((group_rows // pieces, width), BF16),) * pieces,
        in_specs=[whole(SMEM)] * 2 + [whole()] + [whole(HBM)] * 2 + [whole()] * 2,
        out_specs=(whole(),) * pieces,
        scratch_shapes=[
            pltpu.VMEM((slots, LANES), F32),
            pltpu.VMEM((slots, LANES), F32),
            pltpu.VMEM((reqs, LANES), F32),
            pltpu.VMEM((reqs, LANES), F32),
            pltpu.VMEM((LANES, LANES), F32),
            pltpu.VMEM((LANES, LANES), F32),
            pltpu.VMEM((reqs * span, HD), F32),
            pltpu.VMEM((group_rows, width), BF16),
            pltpu.VMEM((reqs * span, HD), F32),
            pltpu.VMEM((reqs * span, HD), F32),
            pltpu.SemaphoreType.DMA((2,)),
        ],
        compiler_params=params(12),
        cost_estimate=cost(
            8 * slots * span * HD, 2 * n * block * LANES + 8 * reqs * span * HD
        ),
        name="combine",
    )(codes, side, returned, *keep_in(HBM, own, retrieved), own_top, own_sum)

    if pieces == 2:
        mine, asked_for = mixed
        theirs = lax.ppermute(asked_for, "grp", swap)
        mine, two_b, four_r = lax.optimization_barrier((mine, two_b, four_r))
        out_near, gate_up_near, down_near = pl.pallas_call(
            stage_weights,
            out_shape=(
                VMEM((2,) + w_out.shape, BF16),
                VMEM((2,) + w_gate_up.shape, BF16),
                VMEM((2,) + w_down.shape, BF16),
            ),
            in_specs=[whole(SMEM)] + [whole(pl.ANY)] * 15,
            out_specs=(whole(),) * 3,
            scratch_shapes=[pltpu.SemaphoreType.DMA((19,))],
            compiler_params=params(2),
            cost_estimate=cost(0, 2 * model * (2 * width + 6 * units)),
            name="stage_weights",
        )(
            side,
            *keep_in(
                HBM, w_out, w_gate_up, w_down, one_a, one_m, one_b, one_q, two_a, two_m, two_q,
                three_q, three_r, four_q,
            ),
            two_b,
            four_r,
        )
        layer_out = pl.pallas_call(
            feed_forward,
            out_shape=jax.ShapeDtypeStruct((rows, model), BF16),
            in_specs=[whole(SMEM)] + [whole()] * 7,
            out_specs=whole(),
            scratch_shapes=[
                pltpu.VMEM((rows, model), BF16),
                pltpu.VMEM((2, rows, units), BF16),
            ],
            compiler_params=params(14),
            cost_estimate=cost(
                4 * rows * model * (width + 3 * units), 4 * model * (width + 3 * units)
            ),
            name="feed_forward",
        )(
            side, tokens, mine, theirs, norm_ffn.reshape(1, -1),
            *keep_in(VMEM, out_near, gate_up_near, down_near),
        )
        return (layer_out, memory_out, momentum_out)

    partial_out = jnp.dot(mixed[0], w_out, preferred_element_type=F32).astype(BF16)
    head_sum = lax.psum_scatter(partial_out, "grp", scatter_dimension=0, tiled=True).astype(F32)
    own_rows = lax.dynamic_slice_in_dim(tokens, lax.axis_index("grp") * rows, rows, 0)
    residual = (own_rows.astype(F32) + head_sum).astype(BF16)
    ffn_in = rms_norm(residual, norm_ffn)
    piece = lax.all_gather(ffn_in, "grp", axis=0, tiled=True)
    gate = jnp.dot(piece, w_gate_up[0], preferred_element_type=F32)
    up = jnp.dot(piece, w_gate_up[1], preferred_element_type=F32)
    hidden = (jax.nn.silu(gate) * up).astype(BF16)
    ffn_out = lax.psum_scatter(
        jnp.dot(hidden, w_down, preferred_element_type=F32).astype(BF16),
        "grp",
        scatter_dimension=0,
        tiled=True,
    ).astype(F32)
    layer_out = (residual.astype(F32) + ffn_out).astype(BF16)
    return (layer_out, memory_out, momentum_out)


def solution(mesh):
    return jax.shard_map(
        on_device,
        mesh=mesh,
        in_specs=(
            P("req", None),
            P(),
            P(None, "grp"),
            P(None, "grp"),
            P(None, "grp"),
            P("grp", None),
            P(None, "grp"),
            P(None, "grp"),
            P("req", None, None, "grp"),
            P("req"),
            P("req"),
            P("req"),
            P("req", None, None),
            P("req", None),
            P("req"),
            P("req", "grp", None, None),
            P("req", "grp", None, None),
            P("req", None, "grp"),
            P("req", None, "grp"),
            P(),
            P(None, None, "grp"),
            P("grp", None),
        ),
        out_specs=(
            P(("req", "grp"), None),
            P("req", "grp", None, None),
            P("req", "grp", None, None),
        ),
        check_vma=False,
    )
```

```python
import functools
import math

import jax
import jax.numpy as jnp
from jax import lax
from jax.experimental import pallas as pl
from jax.experimental.pallas import tpu as pltpu
from jax.sharding import PartitionSpec as P

HD = 128
LANES = 128
EXTRA = 16
TOP_PARTS = 3
WEIGHT = 20
SUM_PARTS = 2

EPS = 1e-06
THETA = 0.5
NEG = -1e30

VMEM = pltpu.VMEM
SMEM = pltpu.SMEM
HBM = pltpu.HBM
F32 = jnp.float32
BF16 = jnp.bfloat16


def whole(space=VMEM):
    return pl.BlockSpec(memory_space=space)


def cost(flops, moved, special=0):
    return pl.CostEstimate(
        flops=WEIGHT * flops, bytes_accessed=WEIGHT * moved, transcendentals=special
    )


def keep_in(space, *arrays):
    return tuple(pltpu.with_memory_space_constraint(array, space) for array in arrays)


def params(mib=40):
    return pltpu.CompilerParams(vmem_limit_bytes=mib << 20)


def rms_norm(rows, gain):
    values = rows.astype(F32)
    factor = lax.rsqrt(jnp.mean(values * values, axis=-1, keepdims=True) + EPS)
    return (values * factor * gain).astype(BF16)


def nt_dot(left, right):
    return lax.dot_general(left, right, (((1,), (1,)), ((), ())), preferred_element_type=F32)


def column_to_row(column, count):
    row_id = lax.broadcasted_iota(jnp.int32, (count, LANES), 0)
    lane_id = lax.broadcasted_iota(jnp.int32, (count, LANES), 1)
    spread = jnp.where(row_id == lane_id, jnp.broadcast_to(column, (count, LANES)), 0.0)
    return jnp.sum(spread, axis=0, keepdims=True)


def split_parts(row, count):
    parts = []
    for _ in range(count):
        part = row.astype(BF16).astype(F32)
        parts.append(part)
        row = row - part
    return parts


def project_queries(*refs, reqs, draft, heads, cut):
    copies = []
    if cut:
        side, gate_up_w, down_w, out_w, *refs, q_ref, q_sem, sems = refs
        *refs, first_ref, quarter_ref = refs
        refs += [q_ref, q_sem]
        copies = run_copies(
            first_pairs(side, gate_up_w, down_w, out_w, first_ref, quarter_ref), sems
        )
    tok_ref, gain_ref, w_ref, q_hbm, turned_ref, q_ref, q_sem = refs
    normed = rms_norm(tok_ref[...], gain_ref[...])
    q_ref[...] = jnp.dot(normed, w_ref[...], preferred_element_type=F32).astype(BF16)
    copies.append(pltpu.make_async_copy(q_ref, q_hbm, q_sem.at[0]))
    copies[-1].start()
    span = heads * draft
    for r in range(reqs):
        rows = slice(r * draft, (r + 1) * draft)
        pieces = [q_ref[rows, h * HD : (h + 1) * HD].astype(F32) for h in range(heads)]
        if span < LANES:
            pieces.append(jnp.zeros((LANES - span, HD), F32))
        tile = jnp.concatenate(pieces, axis=0)
        turned_ref[r * HD : (r + 1) * HD, :] = jnp.transpose(tile).astype(BF16)
    for copy in copies:
        copy.wait()


def project_keys(tok_ref, gain_ref, wk_ref, wv_ref, k_ref, v_ref):
    normed = rms_norm(tok_ref[...], gain_ref[...])
    k_ref[...] = jnp.dot(normed, wk_ref[...], preferred_element_type=F32).astype(BF16)
    v_ref[...] = jnp.dot(normed, wv_ref[...], preferred_element_type=F32).astype(BF16)


def pack_queries(codes, lengths, turned_ref, out_hbm, out_ref, sems, *, n, cap, reqs, page_len):
    block = cap * HD + EXTRA
    row_id = lax.broadcasted_iota(jnp.int32, (EXTRA, LANES), 0)

    def departure(d):
        rows = pl.ds(pl.multiple_of(d * block, EXTRA), block)
        return pltpu.make_async_copy(out_ref.at[rows], out_hbm.at[rows], sems.at[d])

    def one(d, carry):
        base = pl.multiple_of(d * block, EXTRA)
        tail = jnp.zeros((EXTRA, LANES), F32)
        for c in range(cap):
            code = codes[d, 0, c]
            r = lax.rem(code, reqs)
            page = lax.div(code, reqs)
            live = jnp.clip(lengths[r] - page * page_len, 0, page_len)
            tail = jnp.where(row_id == c, live.astype(F32), tail)
            rows = pl.ds(pl.multiple_of(r * HD, HD), HD)
            out_ref[pl.ds(base + c * HD, HD), :] = turned_ref[rows, :]
        out_ref[pl.ds(base + cap * HD, EXTRA), :] = tail.astype(BF16)
        departure(d).start()
        return carry

    lax.fori_loop(0, n, one, 0)
    for d in range(n):
        departure(d).wait()


def page_attention(
    q_ref, kv_hbm, out_hbm, kv_buf, out_buf, in_sems, out_sems,
    *, n, cap, draft, heads, page_len, scale, group,
):
    span = heads * draft
    ask_block = cap * HD + EXTRA
    block = cap * span + EXTRA
    token = lax.broadcasted_iota(jnp.int32, (page_len, LANES), 0).astype(F32)
    row_id = lax.broadcasted_iota(jnp.int32, (EXTRA, LANES), 0)
    head_of = lax.broadcasted_iota(jnp.int32, (HD, LANES), 1) // draft

    def arrival(d):
        return pltpu.make_async_copy(
            kv_hbm.at[pl.ds(d * cap, cap)], kv_buf.at[d], in_sems.at[d]
        )

    def departure(d):
        rows = pl.ds(pl.multiple_of(d * block, EXTRA), block)
        return pltpu.make_async_copy(out_buf.at[rows], out_hbm.at[rows], out_sems.at[d])

    for d in range(n):
        arrival(d).start()

    def one(i, carry):
        pairs = [(i * group + g, c) for g in range(group) for c in range(cap)]
        limits = []
        for g in range(group):
            d = i * group + g
            arrival(d).wait()
            at = pl.multiple_of(d * ask_block + cap * HD, EXTRA)
            limits.append(q_ref[pl.ds(at, EXTRA), :].astype(F32))
        all_scores = []
        for d, c in pairs:
            at = pl.multiple_of(d * ask_block + c * HD, EXTRA)
            turned = q_ref[pl.ds(at, HD), :]
            blocks = [jnp.where(head_of == h, turned, jnp.zeros_like(turned)) for h in range(heads)]
            all_scores.append(
                jnp.dot(
                    kv_buf[d, c, 0], jnp.concatenate(blocks, axis=0), preferred_element_type=F32
                )
            )
        all_weights = []
        tails = [jnp.zeros((EXTRA, LANES), F32) for _ in range(group)]
        for j, (d, c) in enumerate(pairs):
            g = j // cap
            scores = jnp.where(token < limits[g][c : c + 1, :], all_scores[j] * scale, NEG)
            top = jnp.max(scores, axis=0, keepdims=True)
            weight = jnp.exp(scores - top)
            total = jnp.sum(weight, axis=0, keepdims=True)
            all_weights.append(jnp.transpose(weight).astype(BF16))
            parts = split_parts(top, TOP_PARTS) + split_parts(total, SUM_PARTS)
            for p, part in enumerate(parts):
                tails[g] = jnp.where(row_id == p * cap + c, part, tails[g])
        for j, (d, c) in enumerate(pairs):
            for h in range(heads):
                numer = jnp.dot(
                    all_weights[j][h * draft : (h + 1) * draft, :],
                    kv_buf[d, c, 1, :, h * HD : (h + 1) * HD],
                    preferred_element_type=F32,
                )
                at = pl.multiple_of(d * block + c * span + h * draft, EXTRA)
                out_buf[pl.ds(at, draft), :] = numer.astype(BF16)
        for g in range(group):
            d = i * group + g
            at = pl.multiple_of(d * block + cap * span, EXTRA)
            out_buf[pl.ds(at, EXTRA), :] = tails[g].astype(BF16)
            departure(d).start()
        return carry

    lax.fori_loop(0, n // group, one, 0)
    for d in range(n):
        departure(d).wait()


def local_attention(
    q_ref, k_ref, v_ref, pk_ref, pv_ref, mask_ref, mem_ref,
    o_ref, ret_ref, top_ref, sum_ref, *, heads, draft, scale,
):
    r = pl.program_id(0)
    seen = mask_ref[0] == 1
    tops, totals = [], []
    for h in range(heads):
        cols = slice(h * HD, (h + 1) * HD)
        rows = slice(h * draft, (h + 1) * draft)
        query = q_ref[:, cols]
        tree = jnp.where(seen, nt_dot(query, k_ref[:, cols]) * scale, NEG)
        fixed = nt_dot(query, pk_ref[:, cols]) * scale
        top = jnp.maximum(
            jnp.max(tree, axis=1, keepdims=True), jnp.max(fixed, axis=1, keepdims=True)
        )
        tree_w = jnp.exp(tree - top)
        fixed_w = jnp.exp(fixed - top)
        total = jnp.sum(tree_w, axis=1, keepdims=True) + jnp.sum(fixed_w, axis=1, keepdims=True)
        numer = jnp.dot(tree_w.astype(BF16), v_ref[:, cols], preferred_element_type=F32)
        numer = numer + jnp.dot(fixed_w.astype(BF16), pv_ref[:, cols], preferred_element_type=F32)
        o_ref[rows, :] = numer
        tops.append(top)
        totals.append(total)
        wide = query.astype(F32)
        unit = wide * lax.rsqrt(jnp.sum(wide * wide, axis=1, keepdims=True) + EPS)
        ret_ref[rows, :] = jnp.dot(
            unit, mem_ref[0, h], preferred_element_type=F32, precision=lax.Precision.HIGHEST
        )
    span = heads * draft
    top_ref[pl.ds(r, 1), :] = column_to_row(jnp.concatenate(tops, axis=0), span)
    sum_ref[pl.ds(r, 1), :] = column_to_row(jnp.concatenate(totals, axis=0), span)


def update_memory(
    path, count, mom_code, forget_code, k_ref, v_ref, mem_hbm, mom_hbm, mem_out, mom_out,
    mem_buf, mom_buf, wide_k, wide_v, unit_ref, value_ref, turned_ref, in_sems, out_sems,
    *, reqs, draft, heads, steps,
):
    def arrivals(r):
        return (
            pltpu.make_async_copy(mem_hbm.at[r], mem_buf.at[r], in_sems.at[0, r]),
            pltpu.make_async_copy(mom_hbm.at[r], mom_buf.at[r], in_sems.at[1, r]),
        )

    def departures(r):
        return (
            pltpu.make_async_copy(mem_buf.at[r], mem_out.at[r], out_sems.at[0, r]),
            pltpu.make_async_copy(mom_buf.at[r], mom_out.at[r], out_sems.at[1, r]),
        )

    for r in range(reqs):
        for copy in arrivals(r):
            copy.start()
    unit_ref[...] = jnp.zeros_like(unit_ref)

    def one(r, carry):
        rows = pl.ds(pl.multiple_of(r * draft, draft), draft)
        wide_k[...] = k_ref[rows, :].astype(F32)
        wide_v[...] = v_ref[rows, :].astype(F32)
        for n in range(steps):
            node = path[n, r]
            k_row = wide_k[pl.ds(node, 1), :]
            v_row = wide_v[pl.ds(node, 1), :]
            for h in range(heads):
                unit_ref[h * steps + n : h * steps + n + 1, :] = k_row[:, h * HD : (h + 1) * HD]
                value_ref[h * steps + n : h * steps + n + 1, :] = v_row[:, h * HD : (h + 1) * HD]
        keys = unit_ref[...]
        unit = keys * lax.rsqrt(jnp.sum(keys * keys, axis=1, keepdims=True) + EPS)
        turned_ref[...] = jnp.transpose(unit)
        for copy in arrivals(r):
            copy.wait()

        def advance(n):
            for h in range(heads):
                eta = 0.97 - 0.06 * mom_code[n, h, r].astype(F32)
                keep = 1.0 - (0.01 + 0.02 * forget_code[n, h, r].astype(F32))
                row = h * steps + n
                column = turned_ref[:, row : row + 1]
                matrix = mem_buf[r, h]
                predicted = jnp.sum(column * matrix, axis=0, keepdims=True)
                error = THETA * (predicted - value_ref[row : row + 1, :])
                moved = eta * mom_buf[r, h] - column * error
                mom_buf[r, h] = moved
                mem_buf[r, h] = keep * matrix + moved

        for n in range(steps):
            pl.when(n < count[r])(functools.partial(advance, n))
        for copy in departures(r):
            copy.start()
        return carry

    lax.fori_loop(0, reqs, one, 0)
    for r in range(reqs):
        for copy in departures(r):
            copy.wait()


def combine(
    codes, side, msg_ref, o_hbm, ret_hbm, own_top_ref, own_sum_ref, *rest,
    n, cap, reqs, draft, heads, pieces,
):
    outs = rest[:pieces]
    part_top, part_sum, best, total, weight, own_weight, acc, mixed, o_ref, ret_ref, sems = rest[
        pieces:
    ]
    copies = [
        pltpu.make_async_copy(o_hbm, o_ref, sems.at[0]),
        pltpu.make_async_copy(ret_hbm, ret_ref, sems.at[1]),
    ]
    for copy in copies:
        copy.start()
    span = heads * draft
    block = cap * span + EXTRA
    slots = n * cap
    for d in range(n):
        at = d * block + cap * span
        tail = msg_ref[at : at + EXTRA, :].astype(F32)
        rows = [tail[p * cap : (p + 1) * cap] for p in range(TOP_PARTS + SUM_PARTS)]
        part_top[d * cap : (d + 1) * cap, :] = rows[0] + rows[1] + rows[2]
        part_sum[d * cap : (d + 1) * cap, :] = rows[3] + rows[4]
    best[...] = own_top_ref[...]
    owners = [lax.rem(codes[s // cap, 0, s % cap], reqs) for s in range(slots)]
    for s in range(slots):
        r = owners[s]
        best[pl.ds(r, 1), :] = jnp.maximum(best[pl.ds(r, 1), :], part_top[s : s + 1, :])
    own_weight[...] = jnp.zeros_like(own_weight)
    weight[...] = jnp.zeros_like(weight)
    start = jnp.exp(own_top_ref[...] - best[...])
    total[...] = start * own_sum_ref[...]
    for s in range(slots):
        r = owners[s]
        term = jnp.exp(part_top[s : s + 1, :] - best[pl.ds(r, 1), :])
        weight[s : s + 1, :] = term
        total[pl.ds(r, 1), :] = total[pl.ds(r, 1), :] + term * part_sum[s : s + 1, :]
    inverse = 1.0 / total[...]
    own_weight[0:reqs, :] = start * inverse
    total[...] = inverse
    for s in range(slots):
        weight[s : s + 1, :] = weight[s : s + 1, :] * total[pl.ds(owners[s], 1), :]
    turned = jnp.transpose(weight[...])
    own_turned = jnp.transpose(own_weight[...])
    for copy in copies:
        copy.wait()
    for r in range(reqs):
        rows = slice(r * span, (r + 1) * span)
        acc[rows, :] = o_ref[rows, :] * own_turned[0:span, r : r + 1] + ret_ref[rows, :]
    for s in range(slots):
        at = (s // cap) * block + (s % cap) * span
        rows = pl.ds(pl.multiple_of(owners[s] * span, span), span)
        acc[rows, :] = acc[rows, :] + msg_ref[at : at + span, :].astype(F32) * turned[
            0:span, s : s + 1
        ]
    for r in range(reqs):
        for h in range(heads):
            at = r * span + h * draft
            mixed[r * draft : (r + 1) * draft, h * HD : (h + 1) * HD] = acc[
                at : at + draft, :
            ].astype(BF16)
    rows = reqs * draft // pieces
    for p, out_ref in enumerate(outs):
        first = lax.rem(side[0] + p, pieces) * rows
        out_ref[...] = mixed[pl.ds(pl.multiple_of(first, rows), rows), :]


def run_copies(pairs, sems):
    copies = [
        pltpu.make_async_copy(source, target, sems.at[i])
        for i, (source, target) in enumerate(pairs)
    ]
    for copy in copies:
        copy.start()
    return copies


def first_pairs(side, gate_up_w, down_w, out_w, first_ref, quarter_ref):
    depth, width = down_w.shape[0] // 4, out_w.shape[0] // 4
    down_rows = pl.ds(pl.multiple_of(side[2] * depth, EXTRA), depth)
    out_rows = pl.ds(pl.multiple_of(side[2] * width, EXTRA), width)
    pairs = [
        (down_w.at[down_rows], quarter_ref.at[pl.ds(0, depth)]),
        (out_w.at[out_rows], quarter_ref.at[pl.ds(depth, width)]),
    ]
    step = first_ref.shape[0] // 2
    for i in range(2):
        rows = pl.ds(i * step, step)
        pairs.append((gate_up_w.at[side[1], rows], first_ref.at[rows]))
    return pairs


def cut_last(side, gate_up_w, mid_ref, last_ref, sems, *, pieces):
    step = last_ref.shape[0] // pieces
    start = gate_up_w.shape[1] - last_ref.shape[0]
    half = gate_up_w.at[side[1]]
    middle = mid_ref.shape[0]
    pairs = [(half.at[pl.ds(start - middle, middle)], mid_ref)]
    for i in range(pieces):
        pairs.append((half.at[pl.ds(start + i * step, step)], last_ref.at[pl.ds(i * step, step)]))
    for copy in run_copies(pairs, sems):
        copy.wait()


def stage_weights(
    side, out_w, gate_up_w, down_w, one_a, one_m, one_q, two_a, two_m, two_q, three_q,
    three_r, four_q, four_r, out_all, gate_up_own, gate_up_peer, down_all, sems,
):
    width, depth = out_w.shape[0] // 4, down_w.shape[0] // 4
    pairs = [(gate_up_w, gate_up_own), (down_w, down_all.at[0]), (out_w, out_all.at[0])]
    for half, parts in ((side[1], (one_a, one_m)), (1 - side[1], (two_a, two_m))):
        at = 0
        for part in parts:
            pairs.append((part, gate_up_peer.at[half, pl.ds(at, part.shape[0])]))
            at += part.shape[0]
    core, chip = side[1], side[2] // 2
    near = three_q.shape[0]
    places = ((core, chip), (1 - core, chip), (core, 1 - chip), (1 - core, 1 - chip))
    got = ((one_q,), (two_q,), (three_q, three_r), (four_q, four_r))
    for (x, y), parts in zip(places, got):
        base = pl.multiple_of((2 * y + x) * depth, EXTRA)
        rows = pl.ds(pl.multiple_of((2 * y + x) * width, EXTRA), width)
        if len(parts) == 2:
            pairs.append((parts[0], down_all.at[1, pl.ds(base, near)]))
        at = near if len(parts) == 2 else 0
        rest = depth - at
        pairs.append((parts[-1].at[pl.ds(0, rest)], down_all.at[1, pl.ds(base + at, rest)]))
        pairs.append((parts[-1].at[pl.ds(rest, width)], out_all.at[1, rows]))
    for copy in run_copies(pairs, sems):
        copy.wait()


def feed_forward(
    side, tok_ref, mine_ref, theirs_ref, gain_ref, out_w, own_w, peer_w, down_w, one_b, two_b,
    out_ref, residual, ffn_in, hidden,
):
    rows = mine_ref.shape[0]
    units = own_w.shape[2]
    first = peer_w.shape[1]
    tokens = tok_ref[pl.ds(pl.multiple_of(side[0] * rows, rows), rows), :].astype(F32)
    summed = tokens + jnp.dot(mine_ref[...], out_w[0], preferred_element_type=F32)
    summed = summed + jnp.dot(theirs_ref[...], out_w[1], preferred_element_type=F32)
    residual[...] = summed.astype(BF16)
    ffn_in[...] = rms_norm(residual[...], gain_ref[...])
    step = 256

    def gated(gate, up):
        return (gate / (1.0 + jnp.exp(-gate)) * up).astype(BF16)

    for at in range(0, units, step):
        cols = slice(at, min(at + step, units))
        gate = jnp.dot(ffn_in[...], own_w[0, :, cols], preferred_element_type=F32)
        up = jnp.dot(ffn_in[...], own_w[1, :, cols], preferred_element_type=F32)
        hidden[0, :, cols] = gated(gate, up)

    def peer(gate_tail, up_tail):
        for at in range(0, units, step):
            cols = slice(at, min(at + step, units))
            gate, up = (
                jnp.dot(ffn_in[:, :first], peer_w[half, :, cols], preferred_element_type=F32)
                + jnp.dot(ffn_in[:, first:], tail[:, cols], preferred_element_type=F32)
                for half, tail in enumerate((gate_tail, up_tail))
            )
            hidden[1, :, cols] = gated(gate, up)

    pl.when(side[1] == 0)(functools.partial(peer, one_b, two_b))
    pl.when(side[1] == 1)(functools.partial(peer, two_b, one_b))
    for at in range(0, out_ref.shape[1], step):
        cols = slice(at, at + step)
        total = residual[:, cols].astype(F32)
        for half in range(2):
            total = total + jnp.dot(hidden[half], down_w[half, :, cols], preferred_element_type=F32)
        out_ref[:, cols] = total.astype(BF16)


def on_device(
    tokens,
    norm_attn,
    w_query,
    w_key,
    w_value,
    w_out,
    persist_keys,
    persist_values,
    kv_cache,
    slot_request,
    slot_page,
    cache_len,
    tree_mask,
    accept_path,
    accept_len,
    memory,
    momentum,
    momentum_code,
    forget_code,
    norm_ffn,
    w_gate_up,
    w_down,
):
    n = lax.axis_size("req")
    group_rows, model = tokens.shape
    reqs = cache_len.shape[0]
    draft = tree_mask.shape[1]
    steps = accept_path.shape[1]
    width = w_query.shape[1]
    heads = width // HD
    span = heads * draft
    slots = kv_cache.shape[0]
    cap = slots // n
    fixed_count = persist_keys.shape[0]
    page_len = kv_cache.shape[2]
    ask_block = cap * HD + EXTRA
    block = cap * span + EXTRA
    scale = 1.0 / math.sqrt(HD)

    label = (slot_page * reqs + lax.rem(slot_request, reqs)).reshape(n, 1, cap)
    codes = lax.all_to_all(label, "req", split_axis=0, concat_axis=0, tiled=True)

    grp = lax.axis_size("grp")
    depth, out_depth = w_down.shape[0] // 4, width // 4
    first, middle = model // 4, model * 6 // 32
    near = depth * 6 // 11 // EXTRA * EXTRA
    split = (depth, out_depth, first // 2, middle, (model - first - middle) // 2)
    pieces = 2 if grp == 2 and n % 4 == 0 and not any(size % EXTRA for size in split) else 1
    quarter = lax.rem(lax.axis_index("req"), 4)
    core = lax.rem(quarter, 2)
    side = jnp.stack([lax.axis_index("grp"), core, quarter]).astype(jnp.int32)

    cut, units = pieces == 2, w_down.shape[0]
    cuts = ((first, units), (depth + out_depth, model)) if cut else ()
    queries, turned, *shares = pl.pallas_call(
        functools.partial(project_queries, reqs=reqs, draft=draft, heads=heads, cut=cut),
        out_shape=(
            HBM((group_rows, width), BF16),
            jax.ShapeDtypeStruct((reqs * HD, LANES), BF16),
        )
        + tuple(VMEM(shape, BF16) for shape in cuts),
        in_specs=([whole(SMEM)] + [whole(HBM)] * 3) * cut + [whole()] * 3,
        out_specs=(whole(HBM),) + (whole(),) * (1 + len(cuts)),
        scratch_shapes=[pltpu.VMEM((group_rows, width), BF16), pltpu.SemaphoreType.DMA((1,))]
        + [pltpu.SemaphoreType.DMA((4,))] * cut,
        compiler_params=params(14),
        cost_estimate=cost(
            2 * group_rows * model * width, 2 * model * (2 * group_rows + width)
        ),
        name="project_queries",
    )(
        *((side, *keep_in(HBM, w_gate_up, w_down, w_out)) if cut else ()),
        *keep_in(HBM, tokens, norm_attn.reshape(1, -1), w_query),
    )
    if cut:
        half_first, quarters = shares

    if pieces == 2:
        turned, half_first, quarters = lax.optimization_barrier((turned, half_first, quarters))
        swap = [(0, 1), (1, 0)]
        one_a = lax.ppermute(half_first, "grp", swap)
        one_q = lax.ppermute(quarters, "grp", swap)

    packed = pl.pallas_call(
        functools.partial(pack_queries, n=n, cap=cap, reqs=reqs, page_len=page_len),
        out_shape=HBM((n * ask_block, LANES), BF16),
        in_specs=[whole(SMEM), whole(SMEM), whole()],
        out_specs=whole(HBM),
        scratch_shapes=[
            pltpu.VMEM((n * ask_block, LANES), BF16),
            pltpu.SemaphoreType.DMA((n,)),
        ],
        compiler_params=params(8),
        cost_estimate=cost(0, 4 * n * ask_block * LANES),
        name="pack_queries",
    )(codes, *keep_in(HBM, cache_len), turned)
    packed, late_tokens, late = lax.optimization_barrier((packed, tokens, w_gate_up))
    asked = lax.all_to_all(packed, "req", split_axis=0, concat_axis=0, tiled=True)

    if pieces == 2:
        half_mid, half_last = pl.pallas_call(
            functools.partial(cut_last, pieces=2),
            out_shape=(VMEM((middle, units), BF16), VMEM((model - first - middle, units), BF16)),
            in_specs=[whole(SMEM), whole(HBM)],
            out_specs=(whole(),) * 2,
            scratch_shapes=[pltpu.SemaphoreType.DMA((3,))],
            compiler_params=params(4),
            cost_estimate=cost(0, 4 * (model - first) * units),
            name="cut_last",
        )(side, *keep_in(HBM, late))

    keys, values = pl.pallas_call(
        project_keys,
        out_shape=(HBM((group_rows, width), BF16),) * 2,
        in_specs=[whole()] * 4,
        out_specs=(whole(),) * 2,
        compiler_params=params(12),
        cost_estimate=cost(
            4 * group_rows * model * width, 2 * model * (group_rows + 2 * width)
        ),
        name="project_keys",
    )(*keep_in(HBM, late_tokens, norm_attn.reshape(1, -1), w_key, w_value))

    row_block = pl.BlockSpec((draft, width), lambda r, *_: (r, 0))
    fixed_block = pl.BlockSpec((fixed_count, width), lambda r, *_: (0, 0))
    matrix_block = pl.BlockSpec((1, heads, HD, HD), lambda r, *_: (r, 0, 0, 0))
    span_block = pl.BlockSpec((span, HD), lambda r, *_: (r, 0))
    own, retrieved, own_top, own_sum = pl.pallas_call(
        functools.partial(local_attention, heads=heads, draft=draft, scale=scale),
        grid=(reqs,),
        out_shape=(
            HBM((reqs * span, HD), F32),
            HBM((reqs * span, HD), F32),
            jax.ShapeDtypeStruct((reqs, LANES), F32),
            jax.ShapeDtypeStruct((reqs, LANES), F32),
        ),
        in_specs=[
            row_block,
            row_block,
            row_block,
            fixed_block,
            fixed_block,
            pl.BlockSpec((1, draft, draft), lambda r: (r, 0, 0)),
            matrix_block,
        ],
        out_specs=(span_block, span_block) + (pl.BlockSpec((reqs, LANES), lambda r: (0, 0)),) * 2,
        compiler_params=params(10),
        cost_estimate=cost(1, 1),
        name="local_attention",
    )(*keep_in(HBM, queries, keys, values, persist_keys, persist_values, tree_mask, memory))

    memory_out, momentum_out = pl.pallas_call(
        functools.partial(update_memory, reqs=reqs, draft=draft, heads=heads, steps=steps),
        out_shape=(HBM(memory.shape, F32),) * 2,
        in_specs=[whole(SMEM)] * 4 + [whole()] * 2 + [whole(HBM)] * 2,
        out_specs=(whole(HBM),) * 2,
        scratch_shapes=[
            pltpu.VMEM(memory.shape, F32),
            pltpu.VMEM(memory.shape, F32),
            pltpu.VMEM((draft, width), F32),
            pltpu.VMEM((draft, width), F32),
            pltpu.VMEM((LANES, HD), F32),
            pltpu.VMEM((heads * steps, HD), F32),
            pltpu.VMEM((HD, LANES), F32),
            pltpu.SemaphoreType.DMA((2, reqs)),
            pltpu.SemaphoreType.DMA((2, reqs)),
        ],
        compiler_params=params(16),
        cost_estimate=cost(
            14 * reqs * heads * HD * HD * steps * 8, 16 * reqs * heads * HD * HD
        ),
        name="update_memory",
    )(
        jnp.transpose(accept_path),
        accept_len,
        jnp.transpose(momentum_code, (1, 2, 0)),
        jnp.transpose(forget_code, (1, 2, 0)),
        *keep_in(HBM, keys, values, memory, momentum),
    )

    if pieces == 2:
        memory_out, momentum_out, half_last, one_a, one_q = lax.optimization_barrier(
            (memory_out, momentum_out, half_last, one_a, one_q)
        )
        other_core = [(i, i ^ 1) for i in range(n)]
        other_chip = [(i, i ^ 2) for i in range(n)]
        one_m = lax.ppermute(half_mid, "grp", swap)
        one_b = lax.ppermute(half_last, "grp", swap)
        three_q = lax.ppermute(one_q[:near], "req", other_chip)
        three_r = lax.ppermute(one_q[near:], "req", other_chip)
    asked, memory_out, momentum_out, keys, values = lax.optimization_barrier(
        (asked, memory_out, momentum_out, keys, values)
    )
    answers = pl.pallas_call(
        functools.partial(
            page_attention, n=n, cap=cap, draft=draft, heads=heads, page_len=page_len,
            scale=scale, group=math.gcd(n, 4),
        ),
        out_shape=HBM((n * block, LANES), BF16),
        in_specs=[whole(), whole(HBM)],
        out_specs=whole(HBM),
        scratch_shapes=[
            pltpu.VMEM((n, cap) + kv_cache.shape[1:], BF16),
            pltpu.VMEM((n * block, LANES), BF16),
            pltpu.SemaphoreType.DMA((n,)),
            pltpu.SemaphoreType.DMA((n,)),
        ],
        compiler_params=params(24),
        cost_estimate=cost(
            4 * slots * span * page_len * HD,
            4 * slots * page_len * width + 4 * n * block * LANES,
            slots * span * page_len,
        ),
        name="page_attention",
    )(asked, *keep_in(HBM, kv_cache))
    if pieces == 2:
        answers, one_m, three_q = lax.optimization_barrier((answers, one_m, three_q))
        _, one_a, one_q = lax.optimization_barrier((answers, one_a, one_q))
        own, one_m, three_q = lax.optimization_barrier((own, one_m, three_q))
        two_a, two_q, two_m, four_q = (
            lax.ppermute(part, "req", other_core) for part in (one_a, one_q, one_m, three_q)
        )
    returned = lax.all_to_all(answers, "req", split_axis=0, concat_axis=0, tiled=True)
    if pieces == 2:
        returned, two_a, two_m, two_q, four_q, three_r, own, retrieved = lax.optimization_barrier(
            (returned, two_a, two_m, two_q, four_q, three_r, own, retrieved)
        )
        four_r = lax.ppermute(three_r, "req", other_core)
    rows = group_rows // grp
    mixed = pl.pallas_call(
        functools.partial(
            combine, n=n, cap=cap, reqs=reqs, draft=draft, heads=heads, pieces=pieces
        ),
        out_shape=(jax.ShapeDtypeStruct((group_rows // pieces, width), BF16),) * pieces,
        in_specs=[whole(SMEM)] * 2 + [whole()] + [whole(HBM)] * 2 + [whole()] * 2,
        out_specs=(whole(),) * pieces,
        scratch_shapes=[
            pltpu.VMEM((slots, LANES), F32),
            pltpu.VMEM((slots, LANES), F32),
            pltpu.VMEM((reqs, LANES), F32),
            pltpu.VMEM((reqs, LANES), F32),
            pltpu.VMEM((LANES, LANES), F32),
            pltpu.VMEM((LANES, LANES), F32),
            pltpu.VMEM((reqs * span, HD), F32),
            pltpu.VMEM((group_rows, width), BF16),
            pltpu.VMEM((reqs * span, HD), F32),
            pltpu.VMEM((reqs * span, HD), F32),
            pltpu.SemaphoreType.DMA((2,)),
        ],
        compiler_params=params(12),
        cost_estimate=cost(
            8 * slots * span * HD, 2 * n * block * LANES + 8 * reqs * span * HD
        ),
        name="combine",
    )(codes, side, returned, *keep_in(HBM, own, retrieved), own_top, own_sum)

    if pieces == 2:
        mine, asked_for = mixed
        theirs = lax.ppermute(asked_for, "grp", swap)
        mine, four_r, one_b = lax.optimization_barrier((mine, four_r, one_b))
        two_b = lax.ppermute(one_b, "req", other_core)
        out_near, own_near, peer_near, down_near = pl.pallas_call(
            stage_weights,
            out_shape=(
                VMEM((2,) + w_out.shape, BF16),
                VMEM(w_gate_up.shape, BF16),
                VMEM((2, first + middle, units), BF16),
                VMEM((2,) + w_down.shape, BF16),
            ),
            in_specs=[whole(SMEM)] + [whole(pl.ANY)] * 13,
            out_specs=(whole(),) * 4,
            scratch_shapes=[pltpu.SemaphoreType.DMA((17,))],
            compiler_params=params(2),
            cost_estimate=cost(0, 2 * model * (2 * width + 6 * units)),
            name="stage_weights",
        )(
            side,
            *keep_in(
                HBM, w_out, w_gate_up, w_down, one_a, one_m, one_q, two_a, two_m, two_q, three_q,
                three_r, four_q,
            ),
            four_r,
        )
        layer_out = pl.pallas_call(
            feed_forward,
            out_shape=jax.ShapeDtypeStruct((rows, model), BF16),
            in_specs=[whole(SMEM)] + [whole()] * 10,
            out_specs=whole(),
            scratch_shapes=[
                pltpu.VMEM((rows, model), BF16),
                pltpu.VMEM((rows, model), BF16),
                pltpu.VMEM((2, rows, units), BF16),
            ],
            compiler_params=params(14),
            cost_estimate=cost(
                4 * rows * model * (width + 3 * units), 4 * model * (width + 3 * units)
            ),
            name="feed_forward",
        )(
            side, tokens, mine, theirs, norm_ffn.reshape(1, -1),
            *keep_in(VMEM, out_near, own_near, peer_near, down_near, one_b, two_b),
        )
        return (layer_out, memory_out, momentum_out)

    partial_out = jnp.dot(mixed[0], w_out, preferred_element_type=F32).astype(BF16)
    head_sum = lax.psum_scatter(partial_out, "grp", scatter_dimension=0, tiled=True).astype(F32)
    own_rows = lax.dynamic_slice_in_dim(tokens, lax.axis_index("grp") * rows, rows, 0)
    residual = (own_rows.astype(F32) + head_sum).astype(BF16)
    ffn_in = rms_norm(residual, norm_ffn)
    piece = lax.all_gather(ffn_in, "grp", axis=0, tiled=True)
    gate = jnp.dot(piece, w_gate_up[0], preferred_element_type=F32)
    up = jnp.dot(piece, w_gate_up[1], preferred_element_type=F32)
    hidden = (jax.nn.silu(gate) * up).astype(BF16)
    ffn_out = lax.psum_scatter(
        jnp.dot(hidden, w_down, preferred_element_type=F32).astype(BF16),
        "grp",
        scatter_dimension=0,
        tiled=True,
    ).astype(F32)
    layer_out = (residual.astype(F32) + ffn_out).astype(BF16)
    return (layer_out, memory_out, momentum_out)


def solution(mesh):
    return jax.shard_map(
        on_device,
        mesh=mesh,
        in_specs=(
            P("req", None),
            P(),
            P(None, "grp"),
            P(None, "grp"),
            P(None, "grp"),
            P("grp", None),
            P(None, "grp"),
            P(None, "grp"),
            P("req", None, None, "grp"),
            P("req"),
            P("req"),
            P("req"),
            P("req", None, None),
            P("req", None),
            P("req"),
            P("req", "grp", None, None),
            P("req", "grp", None, None),
            P("req", None, "grp"),
            P("req", None, "grp"),
            P(),
            P(None, None, "grp"),
            P("grp", None),
        ),
        out_specs=(
            P(("req", "grp"), None),
            P("req", "grp", None, None),
            P("req", "grp", None, None),
        ),
        check_vma=False,
    )
```
